128 devices in a mesh: dp: 64 (over y, z_hi, x, core), mp: 2 (over z_lo).
Axes of the slice: x: 4, y: 4, z: 4 (z_hi: 2, z_lo: 2; z = z_hi * 2 + z_lo), core: 2. Of those that a mesh axis runs over, the one named last changes fastest.
Arguments:
- belief: bfloat16 [16384, 2652], P('dp'), may hold values from -6 to 6
- target_value: bfloat16 [16384, 1326], P('dp'), may hold values from -6 to 6
- counts: int32 [128], P('dp'), may hold values from 1 to 128, as said below
- w_first: bfloat16 [2652, 1536], P(None, 'mp'), may hold values from -0.125 to 0.125
- w_middle: bfloat16 [1536, 1536], P('mp'), may hold values from -0.15625 to 0.15625
- w_last: bfloat16 [1536, 1326], P(None, 'mp'), may hold values from -0.15625 to 0.15625
Outputs:
- grad_first: float32 [2652, 1536], P(None, ('mp', 'dp'))
- grad_middle: float32 [1536, 1536], P('mp', 'dp')
- grad_last: float32 [1536, 1326], P('dp', 'mp')
The draws below stay inside these ranges and needn't reach their ends.
Inputs may be any that keep to these rules, and one draw needn't show every extreme that they name: `counts`: rows past a subgame's count in its block are padding with arbitrary values.
All inputs are finite; a program needn't handle non-finite values.
Results may differ from the reference program's by a relative error of at most 0.0089.
Values may be sent and summed in bfloat16 or wider, within the bound.
No kernel may reach another device: no remote copies, remote signals or barrier semaphores. Data moves between devices by JAX's collectives and lax.ppermute only.
A program may use at most 192 MiB of HBM per device.

```python
import jax
import jax.numpy as jnp
from jax import lax

IN = 2652
HID = 1536
OUT = 1326
BLOCK = 128
SUB_DEV = 2
ROWS = 16384
PARAMS = 8469504
N_DP = 64


def draw_counts(key, part):
    key_ceiling, key_counts, key_spot = jax.random.split(key, 3)
    ceiling = jax.random.randint(key_ceiling, (N_DP, 1), 48, BLOCK + 1)
    floor_level = ceiling // 2
    drawn = jax.random.randint(key_counts, (N_DP, SUB_DEV), floor_level, ceiling + 1)
    flat_counts = drawn.reshape(N_DP * SUB_DEV)
    spot = jax.random.randint(key_spot, (), 0, N_DP * SUB_DEV)
    return flat_counts.at[spot].set(BLOCK).astype(jnp.int32)


def steps_of(key, shape, shards, least, high):
    level = 1.0
    for position, parts in shards:
        steps = jax.random.uniform(jax.random.fold_in(jax.random.fold_in(key, 6), position), (parts,), jnp.float32, least / len(shards), high / len(shards))
        level = level * jnp.repeat(jnp.exp(steps), shape[position] // parts).reshape((-1,) + (1,) * (len(shape) - 1 - position))
    return level


def scatter_about(own_key, shape, scale, reach, cuts=(), kind=jnp.bfloat16):
    factor_of = steps_of(own_key, shape, cuts, -0.22, 0.18) if cuts else 1.0
    values = jax.random.normal(own_key, shape, jnp.float32) * scale * factor_of
    return jnp.minimum(jnp.maximum(values, -reach), reach).astype(kind)


def setup_inputs(seed: int = 0) -> dict:
    key_of = jax.random.split(jax.random.key(seed), 7)
    return {
        "belief": scatter_about(key_of[0], (ROWS, IN), 1.0, 6.0, ((0, 64),)),
        "target_value": scatter_about(key_of[1], (ROWS, OUT), 1.0, 6.0, ((0, 64),)),
        "counts": draw_counts(jax.random.fold_in(key_of[6], 71), 0),
        "w_first": scatter_about(key_of[3], (IN, HID), IN ** -0.5, 0.125, ((1, 2),)),
        "w_middle": scatter_about(key_of[4], (HID, HID), HID ** -0.5, 0.15625, ((0, 2),)),
        "w_last": scatter_about(key_of[5], (HID, OUT), HID ** -0.5, 0.15625, ((1, 2),)),
    }


def silu_slope(pre_act):
    sigmoid_of = jax.nn.sigmoid(pre_act)
    return sigmoid_of * (1.0 + pre_act * (1.0 - sigmoid_of))

def rows_grads(belief, target_value, live_mask, w_first, w_middle, w_last):
    pre_first = jnp.dot(belief, w_first, preferred_element_type=jnp.float32)
    act_first = jax.nn.silu(pre_first).astype(jnp.bfloat16)
    pre_middle = jnp.dot(act_first, w_middle, preferred_element_type=jnp.float32)
    act_middle = jax.nn.silu(pre_middle).astype(jnp.bfloat16)
    predicted = jnp.dot(act_middle, w_last, preferred_element_type=jnp.float32)
    mismatch = predicted - target_value.astype(jnp.float32)
    slope_out = (jnp.clip(mismatch, -1.0, 1.0) * live_mask[:, None]).astype(jnp.bfloat16)
    raw_last = jnp.dot(act_middle.T, slope_out, preferred_element_type=jnp.float32)
    back_middle = jnp.dot(slope_out, w_last.T, preferred_element_type=jnp.float32)
    slope_middle = (back_middle * silu_slope(pre_middle)).astype(jnp.bfloat16)
    raw_middle = jnp.dot(act_first.T, slope_middle, preferred_element_type=jnp.float32)
    back_first = jnp.dot(slope_middle, w_middle.T, preferred_element_type=jnp.float32)
    slope_first = (back_first * silu_slope(pre_first)).astype(jnp.bfloat16)
    raw_first = jnp.dot(belief.T, slope_first, preferred_element_type=jnp.float32)
    return (raw_first, raw_middle, raw_last)

def reference(belief, target_value, counts, w_first, w_middle, w_last):
    total_rows = belief.shape[0]
    span_rows = SUB_DEV * BLOCK
    block_count = total_rows // span_rows
    live_all = (counts[:, None] > jnp.arange(BLOCK, dtype=jnp.int32)[None, :]).astype(jnp.float32).reshape(total_rows)

    def add_block(running, block_index):
        row_start = (block_index * span_rows).astype(jnp.int32)
        part_belief = lax.dynamic_slice_in_dim(belief, row_start, span_rows, 0)
        part_target = lax.dynamic_slice_in_dim(target_value, row_start, span_rows, 0)
        part_live = lax.dynamic_slice_in_dim(live_all, row_start, span_rows, 0)
        pieces = rows_grads(part_belief, part_target, part_live, w_first, w_middle, w_last)
        return (tuple((left + right for left, right in zip(running, pieces))), None)
    zeros_init = (jnp.zeros(w_first.shape, jnp.float32), jnp.zeros(w_middle.shape, jnp.float32), jnp.zeros(w_last.shape, jnp.float32))
    running, _ = lax.scan(add_block, zeros_init, jnp.arange(block_count, dtype=jnp.int32))
    raw_first, raw_middle, raw_last = running
    square_sum = jnp.sum(raw_first * raw_first) + jnp.sum(raw_middle * raw_middle) + jnp.sum(raw_last * raw_last)
    norm_scale = lax.rsqrt(square_sum / PARAMS + 1e-06)
    return (raw_first * norm_scale, raw_middle * norm_scale, raw_last * norm_scale)
```

```python
import jax
import jax.numpy as jnp
from jax import lax
from jax.sharding import Mesh
from jax.sharding import PartitionSpec as P

BLOCK = 128
PARAMS = 8469504
DP = ("dp_0", "dp_1", "dp_2", "dp_3")
MP_DP = ("mp", "dp_0", "dp_1", "dp_2", "dp_3")
ALL = DP + ("mp",)
Y, ZH, X, CORE = DP
LANES = 128


def swap(shard, axis):
    return lax.ppermute(shard, axis, [(0, 1), (1, 0)])


def across_hi(shard):
    return lax.ppermute(shard, (ZH, "mp"), [(0, 3), (3, 0), (1, 2), (2, 1)])


def pick(blocks, index, dim):
    return lax.dynamic_index_in_dim(blocks, index, dim, keepdims=False)


def wide(shard):
    return shard.astype(jnp.float32)


def narrow(shard):
    return shard.astype(jnp.bfloat16)


def sum_over_ring(blocks, axis, dim):
    size = lax.axis_size(axis)
    me = lax.axis_index(axis)
    total = wide(pick(blocks, me, dim))
    for step in (2, 1, 3) if size == 4 else (1,):
        part = pick(blocks, lax.rem(me + step, size), dim)
        total += wide(lax.ppermute(part, axis, [(i, (i + step) % size) for i in range(size)]))
    return total


def silu_slope(pre_act):
    sigmoid_of = jax.nn.sigmoid(pre_act)
    return sigmoid_of * (1.0 + pre_act * (1.0 - sigmoid_of))


def dot(left, right):
    return jnp.dot(left, right, preferred_element_type=jnp.float32)


def other_half_of(w_last, core):
    rows = w_last.shape[0] // 2
    width = w_last.shape[1]
    half = lax.dynamic_slice_in_dim(w_last, core * rows, rows, 0)
    first, second = 104, 384
    pieces = (
        swap(half[:, :first], "mp"),
        across_hi(half[:, first:second]),
        across_hi(half[:, second:width]),
    )
    mine = jnp.concatenate(pieces, 1)
    theirs = jnp.concatenate([swap(piece, CORE) for piece in pieces], 1)
    is_first = core == 0
    return jnp.concatenate(
        [jnp.where(is_first, mine, theirs), jnp.where(is_first, theirs, mine)], 0
    )


def per_device(belief, target_value, counts, w_first, w_middle, w_last):
    total_rows = belief.shape[0]
    own_width = w_last.shape[1]
    units = w_first.shape[1]
    core = lax.axis_index(CORE)
    mp = lax.axis_index("mp")
    w_other = other_half_of(w_last, core)
    live_rows = (counts[:, None] > jnp.arange(BLOCK, dtype=jnp.int32)[None, :]).reshape(total_rows)
    live_mask = live_rows.astype(jnp.float32)[:, None]

    pre_first = dot(belief, w_first)
    act_first = narrow(jax.nn.silu(pre_first))
    partial_middle = dot(act_first, w_middle)
    pre_middle = partial_middle + wide(swap(narrow(partial_middle), "mp"))
    act_middle = narrow(jax.nn.silu(pre_middle))

    def slope_of(weights, owner):
        target = lax.dynamic_slice_in_dim(target_value, owner * own_width, own_width, 1)
        mismatch = dot(act_middle, weights) - wide(target)
        return narrow(jnp.clip(mismatch, -1.0, 1.0) * live_mask)

    slope_own = slope_of(w_last, mp)
    slope_other = slope_of(w_other, 1 - mp)
    back_middle = dot(slope_own, w_last.T) + dot(slope_other, w_other.T)
    slope_middle = narrow(back_middle * silu_slope(pre_middle))
    back_first = dot(slope_middle, w_middle.T)
    slope_first = narrow(back_first * silu_slope(pre_first))

    block = units // 64
    place = jnp.arange(units, dtype=jnp.int32)
    source = (place % (32 * block) // block * 2 + place // (32 * block)) * block + place % block
    onehot = (place[:, None] == source[None, :]).astype(jnp.bfloat16)
    slope_first = narrow(dot(slope_first, onehot))

    def half_sum(blocks_of):
        sent = swap(narrow(blocks_of(1 - core)), CORE)
        return narrow(blocks_of(core) + wide(sent))

    def first_blocks(which):
        columns = lax.dynamic_slice_in_dim(slope_first, which * (units // 2), units // 2, 1)
        return dot(columns.T, belief)

    raw_last_t = dot(act_middle.T, slope_own).reshape(32, 2, 24, own_width)
    raw_middle_t = dot(slope_middle.T, act_first).reshape(32, 2, 24, units)
    half_last = half_sum(lambda which: pick(raw_last_t, which, 1))
    half_middle = half_sum(lambda which: pick(raw_middle_t, which, 1))
    half_first = half_sum(first_blocks)

    def shard_of(half, order):
        lengths = half.shape[-2:]
        blocks = half.reshape(4, 2, 4, *lengths)
        names = [Y, ZH, X]
        for axis in order:
            dim = names.index(axis)
            names.pop(dim)
            blocks = sum_over_ring(narrow(blocks), axis, dim)
        return blocks

    shard_last = shard_of(half_last, (X, Y, ZH))
    shard_middle = shard_of(half_middle, (X, Y, ZH))
    shard_first = shard_of(half_first.reshape(32, block, -1), (Y, X, ZH))

    local_squares = (
        jnp.sum(shard_first * shard_first)
        + jnp.sum(shard_middle * shard_middle)
        + jnp.sum(shard_last * shard_last)
    )
    gathered = lax.all_to_all(
        jnp.broadcast_to(local_squares, (128, 8, LANES)), ALL, 0, 0, tiled=True
    )
    square_sum = jnp.sum(gathered[:, 0, 0])
    norm_scale = lax.rsqrt(square_sum / PARAMS + 1e-06)
    return ((shard_first * norm_scale).T, (shard_middle * norm_scale).T, shard_last * norm_scale)


def solution(mesh):
    finer = Mesh(mesh.devices.reshape(4, 2, 4, 2, mesh.shape["mp"]), ALL)
    return jax.shard_map(
        per_device,
        mesh=finer,
        in_specs=(P(DP, None), P(DP, None), P(DP), P(None, "mp"), P("mp", None), P(None, "mp")),
        out_specs=(P(None, MP_DP), P("mp", DP), P(DP, "mp")),
        check_vma=False,
    )
```

```python
import functools

import jax
import jax.numpy as jnp
from jax import lax
from jax.experimental import pallas as pl
from jax.experimental.pallas import tpu as pltpu
from jax.sharding import Mesh
from jax.sharding import PartitionSpec as P

BLOCK = 128
PARAMS = 8469504
DP = ("dp_0", "dp_1", "dp_2", "dp_3")
MP_DP = ("mp", "dp_0", "dp_1", "dp_2", "dp_3")
ALL = DP + ("mp",)
Y, ZH, X, CORE = DP
LANES = 128
FETCHED, SECOND = 343, 320
PIECES = ((0, 48), (48, 192), (192, 343))
VMEM = pl.BlockSpec(memory_space=pltpu.VMEM)
SMEM = pl.BlockSpec(memory_space=pltpu.SMEM)
KERNEL = pltpu.CompilerParams(vmem_limit_bytes=56 << 20)


def swap(shard, axis):
    return lax.ppermute(shard, axis, [(0, 1), (1, 0)])


def across_hi(shard):
    return lax.ppermute(shard, (ZH, "mp"), [(0, 3), (3, 0), (1, 2), (2, 1)])


def pick(blocks, index, dim):
    return lax.dynamic_index_in_dim(blocks, index, dim, keepdims=False)


def wide(shard):
    return shard.astype(jnp.float32)


def narrow(shard):
    return shard.astype(jnp.bfloat16)


def sum_over_ring(blocks, axis, dim):
    size = lax.axis_size(axis)
    me = lax.axis_index(axis)
    total = wide(pick(blocks, me, dim))
    for step in (2, 1, 3) if size == 4 else (1,):
        part = pick(blocks, lax.rem(me + step, size), dim)
        total += wide(lax.ppermute(part, axis, [(i, (i + step) % size) for i in range(size)]))
    return total


def silu_slope(pre_act):
    sigmoid_of = jax.nn.sigmoid(pre_act)
    return sigmoid_of * (1.0 + pre_act * (1.0 - sigmoid_of))


def dot(left, right):
    return jnp.dot(left, right, preferred_element_type=jnp.float32)


def contract(left, right, left_dim, right_dim):
    return lax.dot_general(
        left,
        right,
        (((left_dim,), (right_dim,)), ((), ())),
        preferred_element_type=jnp.float32,
    )


def middle_kernel(
    core_ref,
    partial_ref,
    arrived_ref,
    live_ref,
    target_own_ref,
    target_mine_ref,
    target_theirs_ref,
    w_own_ref,
    w_middle_ref,
    first_slope_ref,
    belief_ref,
    *refs,
):
    count = len(PIECES)
    mine_refs, theirs_refs = refs[:count], refs[count : 2 * count]
    act_ref, slope_own_ref, slope_middle_ref, slope_first_ref, sent_ref = refs[2 * count :]
    live = live_ref[...]
    pre_middle = partial_ref[...] + wide(arrived_ref[...])
    sigmoid_of = 1.0 / (1.0 + jnp.exp(-pre_middle))
    act = narrow(pre_middle * sigmoid_of)
    act_ref[...] = act
    act_slope = sigmoid_of * (1.0 + pre_middle * (1.0 - sigmoid_of))

    def slope_of(weights, target):
        mismatch = contract(weights, act, 1, 1) - wide(target)
        return jnp.clip(mismatch, -1.0, 1.0) * live

    slope_own = narrow(slope_of(w_own_ref[...], target_own_ref[...]))
    slope_own_ref[...] = slope_own
    back = contract(slope_own, w_own_ref[...], 0, 0)
    for side, (w_refs, target_ref) in enumerate(
        ((mine_refs, target_mine_ref), (theirs_refs, target_theirs_ref))
    ):
        repeated = jnp.where(core_ref[0] == side, 0, 2 * FETCHED - SECOND - FETCHED)
        for (start, stop), w_ref in zip(PIECES, w_refs):
            slope = slope_of(w_ref[...], target_ref[start:stop, :])
            column = start + lax.broadcasted_iota(jnp.int32, slope.shape, 0)
            slope = narrow(jnp.where(column >= repeated, slope, 0.0))
            back += contract(slope, w_ref[...], 0, 0)
    slope_middle = narrow(back * act_slope)
    slope_middle_ref[...] = slope_middle
    slope_first = narrow(contract(w_middle_ref[...], slope_middle, 1, 1) * first_slope_ref[...])
    slope_first_ref[...] = slope_first
    half = slope_first.shape[0] // 2
    sent_ref[...] = narrow(contract(slope_first[:half], belief_ref[...], 1, 1)).reshape(sent_ref.shape)


def later_kernel(act_middle_ref, slope_own_ref, slope_middle_ref, act_first_ref, last_ref, middle_ref):
    middle_ref[...] = narrow(contract(slope_middle_ref[...], act_first_ref[...], 0, 0))
    last_ref[...] = narrow(contract(act_middle_ref[...].T, slope_own_ref[...], 1, 1))


def first_kernel(slope_first_ref, belief_ref, arrived_ref, out_ref):
    half = slope_first_ref.shape[0] // 2
    own = contract(slope_first_ref[half:, :], belief_ref[...], 1, 1).reshape(out_ref.shape)
    out_ref[...] = narrow(own + wide(arrived_ref[...]))


def call(body, outs, count, scalars=0, name=None):
    return pl.pallas_call(
        body,
        out_shape=[jax.ShapeDtypeStruct(*out) for out in outs],
        in_specs=[SMEM] * scalars + [VMEM] * (count - scalars),
        out_specs=[VMEM] * len(outs),
        compiler_params=KERNEL,
        name=name,
    )


def per_device(belief, target_value, counts, w_first, w_middle, w_last):
    total_rows = belief.shape[0]
    width = w_last.shape[1]
    units = w_first.shape[1]
    hidden = w_middle.shape[1]
    core = lax.axis_index(CORE)
    mp = lax.axis_index("mp")
    bf16, f32 = jnp.bfloat16, jnp.float32

    w_last_t = w_last.T
    fetched = [
        lax.dynamic_slice_in_dim(w_last_t, core * SECOND + start, stop - start, 0)
        for start, stop in PIECES
    ]
    mine = [swap(fetched[0], "mp"), across_hi(fetched[1]), across_hi(fetched[2])]
    theirs = [swap(piece, CORE) for piece in mine]

    pre_first = dot(belief, w_first)
    act_first = narrow(jax.nn.silu(pre_first))
    partial_middle = dot(act_first, w_middle)
    arrived = swap(narrow(partial_middle), "mp")

    live_rows = (counts[:, None] > jnp.arange(BLOCK, dtype=jnp.int32)[None, :]).reshape(1, total_rows)
    live = live_rows.astype(f32)
    target_t = target_value.T
    target_own = lax.dynamic_slice_in_dim(target_t, mp * width, width, 0)
    target_mine = lax.dynamic_slice_in_dim(target_t, (1 - mp) * width + core * SECOND, FETCHED, 0)
    target_theirs = lax.dynamic_slice_in_dim(
        target_t, (1 - mp) * width + (1 - core) * SECOND, FETCHED, 0
    )
    block = units // 64

    def by_owner(rows):
        rows = rows.reshape(4, 2, 4, 2, block, -1).transpose(3, 0, 2, 1, 4, 5)
        rows = jnp.where(core == 0, rows[::-1], rows)
        return rows.reshape(units, -1)

    w_middle_sorted = by_owner(w_middle)
    first_slope = by_owner(silu_slope(pre_first).T)
    belief_t = belief.T

    operands = (
        core.reshape(1),
        partial_middle,
        arrived,
        live,
        target_own,
        target_mine,
        target_theirs,
        w_last_t,
        w_middle_sorted,
        first_slope,
        belief_t,
        *mine,
        *theirs,
    )
    act_middle, slope_own, slope_middle, slope_first, sent = call(
        middle_kernel,
        [
            ((total_rows, hidden), bf16),
            ((width, total_rows), bf16),
            ((total_rows, hidden), bf16),
            ((units, total_rows), bf16),
            ((4, units // 8, belief.shape[1]), bf16),
        ],
        len(operands),
        1,
        "middle",
    )(*operands)
    sent = swap(sent, CORE)
    raw_last, raw_middle = call(
        later_kernel, [((hidden, width), bf16), ((hidden, units), bf16)], 4, 0, "later"
    )(act_middle, slope_own, slope_middle, act_first)
    (half_first,) = call(first_kernel, [(sent.shape, bf16)], 3, 0, "first")(
        slope_first, belief_t, sent
    )

    def half_sum(blocks):
        arrived = swap(pick(blocks, 1 - core, 1), CORE)
        return narrow(wide(pick(blocks, core, 1)) + wide(arrived))

    half_last = half_sum(raw_last.reshape(32, 2, 24, width))
    half_middle = half_sum(raw_middle.reshape(32, 2, 24, units))

    def shard_of(blocks, names, order):
        names = list(names)
        for axis in order:
            dim = names.index(axis)
            names.pop(dim)
            blocks = sum_over_ring(narrow(blocks), axis, dim)
        return blocks

    shard_last = shard_of(half_last.reshape(4, 2, 4, 24, -1), (Y, ZH, X), (X, Y, ZH))
    shard_middle = shard_of(half_middle.reshape(4, 2, 4, 24, -1), (Y, ZH, X), (X, Y, ZH))
    shard_first = sum_over_ring(half_first, Y, 0).reshape(4, 24, -1)
    shard_first = sum_over_ring(narrow(shard_first), X, 0).reshape(2, 12, -1)
    shard_first = sum_over_ring(narrow(shard_first), ZH, 0)

    local_squares = (
        jnp.sum(shard_first * shard_first)
        + jnp.sum(shard_middle * shard_middle)
        + jnp.sum(shard_last * shard_last)
    )
    gathered = lax.all_to_all(
        jnp.broadcast_to(local_squares, (128, 1, LANES)), ALL, 0, 0, tiled=True
    )
    square_sum = jnp.sum(gathered[:, 0, 0])
    norm_scale = lax.rsqrt(square_sum / PARAMS + 1e-06)
    return ((shard_first * norm_scale).T, (shard_middle * norm_scale).T, shard_last * norm_scale)


def solution(mesh):
    finer = Mesh(mesh.devices.reshape(4, 2, 4, 2, mesh.shape["mp"]), ALL)
    return jax.shard_map(
        per_device,
        mesh=finer,
        in_specs=(P(DP, None), P(DP, None), P(DP), P(None, "mp"), P("mp", None), P(None, "mp")),
        out_specs=(P(None, MP_DP), P("mp", DP), P(DP, "mp")),
        check_vma=False,
    )
```

```python
import jax
import jax.numpy as jnp
from jax import lax
from jax.experimental import pallas as pl
from jax.experimental.pallas import tpu as pltpu
from jax.sharding import Mesh
from jax.sharding import PartitionSpec as P

BLOCK = 128
PARAMS = 8469504
DP = ("dp_0", "dp_1", "dp_2", "dp_3")
MP_DP = ("mp", "dp_0", "dp_1", "dp_2", "dp_3")
ALL = DP + ("mp",)
Y, ZH, X, CORE = DP
LANES = 128
CUT = 480
ROWS, COLS = 24, 384
VMEM = pl.BlockSpec(memory_space=pltpu.VMEM)
SMEM = pl.BlockSpec(memory_space=pltpu.SMEM)
HBM = pl.BlockSpec(memory_space=pl.ANY)
BF16, F32 = jnp.bfloat16, jnp.float32


def wide(shard):
    return shard.astype(F32)


def narrow(shard):
    return shard.astype(BF16)


def swap(shard, axis):
    return lax.ppermute(shard, axis, [(0, 1), (1, 0)])


def rotate(shard, axis, step):
    return lax.ppermute(shard, axis, [(i, (i + step) % 4) for i in range(4)])


def silu_slope(pre_act):
    sigmoid_of = jax.nn.sigmoid(pre_act)
    return sigmoid_of * (1.0 + pre_act * (1.0 - sigmoid_of))


def dot(left, right):
    return jnp.dot(left, right, preferred_element_type=F32)


def contract(left, right, left_dim, right_dim):
    return lax.dot_general(
        left, right, (((left_dim,), (right_dim,)), ((), ())), preferred_element_type=F32
    )


def call(body, name, in_specs, outs, scratch=()):
    return pl.pallas_call(
        body,
        out_shape=[jax.ShapeDtypeStruct(*out) for out in outs],
        in_specs=in_specs,
        out_specs=[VMEM] * len(outs),
        scratch_shapes=list(scratch),
        compiler_params=pltpu.CompilerParams(vmem_limit_bytes=56 << 20),
        name=name,
    )


def by_unit(raw_ref, core, out_ref):
    for unit in range(16):
        for z_hi in range(2):
            first = 2 * ROWS * ((unit // 4 * 2 + z_hi) * 4 + unit % 4)
            rows = pl.ds(pl.multiple_of(first + ROWS * core, 8), ROWS)
            for half in range(2):
                out_ref[unit, 2 * z_hi + half] = narrow(
                    raw_ref[rows, half * COLS : (half + 1) * COLS]
                )


def last_kernel(
    place_ref, partial_ref, arrived_ref, live_ref, target_ref, w_ref,
    act_ref, act_slope_ref, slope_ref, sent_ref, own_ref, raw_ref, padded_ref,
):
    core = place_ref[0]
    width = slope_ref.shape[0]
    pre_middle = partial_ref[...] + wide(arrived_ref[...])
    sigmoid_of = 1.0 / (1.0 + jnp.exp(-pre_middle))
    act = narrow(pre_middle * sigmoid_of)
    act_ref[...] = act
    act_slope_ref[...] = sigmoid_of * (1.0 + pre_middle * (1.0 - sigmoid_of))
    mismatch = contract(w_ref[...], act, 1, 1) - wide(target_ref[...])
    slope = narrow(jnp.clip(mismatch, -1.0, 1.0) * live_ref[...])
    slope_ref[...] = slope
    padded_ref[...] = jnp.zeros_like(padded_ref)
    padded_ref[0:width, :] = slope
    raw_ref[...] = contract(act.T, padded_ref[...], 1, 1)
    by_unit(raw_ref, 1 - core, sent_ref)
    by_unit(raw_ref, core, own_ref)


def slopes_kernel(
    place_ref, act_ref, act_slope_ref, slope_ref, live_ref, target_ref, first_slope_ref,
    onehot_ref, w_own_hbm, hi_hbm, hi_again_hbm, lo_hbm, lo_again_hbm, w_middle_hbm, belief_hbm,
    slope_middle_ref, slope_first_ref, sent_ref,
    w_own, w_hi, w_lo, w_middle, belief, sems,
):
    core = place_ref[0]
    copies = [
        pltpu.make_async_copy(source, target, sems.at[i])
        for i, (source, target) in enumerate(
            ((w_own_hbm, w_own), (w_middle_hbm, w_middle), (belief_hbm, belief))
        )
    ]
    fetched = [
        pltpu.make_async_copy(source, target, sems.at[sem])
        for source, target, sem in (
            (hi_hbm, w_hi, 3), (lo_again_hbm, w_lo, 4), (hi_again_hbm, w_hi, 3), (lo_hbm, w_lo, 4),
        )
    ]
    copies[0].start()

    @pl.when(core == 0)
    def _():
        fetched[0].start()
        fetched[1].start()

    @pl.when(core != 0)
    def _():
        fetched[2].start()
        fetched[3].start()

    copies[1].start()
    copies[2].start()
    act = act_ref[...]
    live = live_ref[...]
    copies[0].wait()
    back = contract(slope_ref[...], w_own[...], 0, 0)
    for part, start, weights in ((0, 0, w_hi), (1, CUT, w_lo)):
        fetched[part].wait()
        stop = start + weights.shape[0]
        mismatch = contract(weights[...], act, 1, 1) - wide(target_ref[start:stop, :])
        slope = narrow(jnp.clip(mismatch, -1.0, 1.0) * live)
        back += contract(slope, weights[...], 0, 0)
    slope_middle = narrow(back * act_slope_ref[...])
    slope_middle_ref[...] = slope_middle
    copies[1].wait()
    slope_first = narrow(contract(w_middle[...], slope_middle, 1, 1) * first_slope_ref[...])
    slope_first = narrow(dot(onehot_ref[...], slope_first))
    slope_first_ref[...] = slope_first
    copies[2].wait()
    half = slope_first.shape[0] // 2
    for start, stop in column_cuts(belief.shape[0]):
        raw = narrow(contract(slope_first[:half], belief[start:stop, :], 1, 1))
        put_columns(raw, start // COLS, sent_ref)


def column_cuts(width):
    return [(start, min(start + COLS, width)) for start in range(0, width, COLS)]


def put_columns(raw, granule, out_ref):
    width = raw.shape[1]
    if width < COLS:
        raw = jnp.concatenate([raw, jnp.zeros((raw.shape[0], COLS - width), raw.dtype)], 1)
    for unit in range(16):
        out_ref[unit, granule] = raw[unit * ROWS : (unit + 1) * ROWS]


def middle_kernel(place_ref, slope_middle_ref, act_first_ref, sent_ref, own_ref, raw_ref):
    core = place_ref[0]
    raw_ref[...] = contract(slope_middle_ref[...], act_first_ref[...], 0, 0)
    by_unit(raw_ref, 1 - core, sent_ref)
    by_unit(raw_ref, core, own_ref)


def others(me):
    return [me] + [lax.rem(me + step, 4) for step in (1, 2, 3)]


def last_cut_kernel(place_ref, own_ref, arrived_ref, *out_refs):
    for x, out_ref in zip(others(place_ref[2]), out_refs):
        for y in range(4):
            out_ref[y] = narrow(wide(own_ref[4 * y + x]) + wide(arrived_ref[4 * y + x]))


def first_cut_kernel(
    place_ref, slope_first_ref, belief_ref, arrived_ref, middle_ref, middle_arrived_ref, *refs
):
    x_refs, y_refs, raw_ref = refs[:4], refs[4:8], refs[8]
    half = slope_first_ref.shape[0] // 2
    slope = slope_first_ref[half:, :]
    for start, stop in column_cuts(belief_ref.shape[0]):
        raw = contract(slope, belief_ref[start:stop, :], 1, 1)
        put_columns(raw, start // COLS, raw_ref)
    for y, out_ref in zip(others(place_ref[1]), y_refs):
        for x in range(4):
            unit = 4 * y + x
            out_ref[x] = narrow(raw_ref[unit, 0:5] + wide(arrived_ref[unit, 0:5]))
    for x, out_ref in zip(others(place_ref[2]), x_refs):
        for y in range(4):
            unit = 4 * y + x
            out_ref[y, 0:4] = narrow(wide(middle_ref[unit]) + wide(middle_arrived_ref[unit]))
            out_ref[y, 4:6] = narrow(raw_ref[unit, 5:7] + wide(arrived_ref[unit, 5:7]))


def sum_of(refs, index):
    return sum(wide(ref[index]) for ref in refs[1:]) + wide(refs[0][index])


def second_cut_kernel(place_ref, *refs):
    last_refs, x_refs, y_refs = refs[0:4], refs[4:8], refs[8:12]
    a_refs, b_refs = refs[12:16], refs[16:20]
    for y, out_ref in zip(others(place_ref[1]), a_refs):
        out_ref[0:4] = narrow(sum_of(last_refs, y))
        out_ref[4:10] = narrow(sum_of(x_refs, y))
    for x, out_ref in zip(others(place_ref[2]), b_refs):
        out_ref[...] = narrow(sum_of(y_refs, x))


def third_cut_kernel(place_ref, *refs):
    a_refs, b_refs = refs[0:4], refs[4:8]
    sent_ref, own_ref, sum_a, sum_b = refs[8:12]
    z_hi = place_ref[3]
    sum_a[...] = sum_of(a_refs, slice(None))
    sum_b[...] = sum_of(b_refs, slice(None))
    for side, out_ref in ((1 - z_hi, sent_ref), (z_hi, own_ref)):
        kind = out_ref.dtype
        out_ref[0:2] = sum_a[pl.ds(2 * side, 2)].astype(kind)
        out_ref[2:4] = sum_a[pl.ds(4 + 2 * side, 2)].astype(kind)
        halves = []
        for granule in range(7):
            rows = sum_b[granule] if granule < 5 else sum_a[granule + 3]
            halves.append(jnp.where(side == 0, rows[0:12], rows[12:24]))
        halves.append(jnp.zeros_like(halves[0]))
        for pair in range(4):
            out_ref[4 + pair] = jnp.concatenate(halves[2 * pair : 2 * pair + 2], 0).astype(kind)


def square_kernel(own_ref, arrived_ref, total_ref, squares_ref):
    total = own_ref[...] + wide(arrived_ref[...])
    total_ref[...] = total
    squares_ref[...] = jnp.broadcast_to(jnp.sum(total * total), squares_ref.shape)


def scale_kernel(total_ref, squares_ref, first_ref, middle_ref, last_ref):
    square_sum = jnp.sum(squares_ref[...], axis=0)
    norm_scale = lax.rsqrt(square_sum / PARAMS + 1e-06)
    norm_scale = jnp.concatenate([norm_scale] * 3, 1)
    for ref, start in ((last_ref, 0), (middle_ref, 2)):
        for half in range(2):
            columns = slice(half * COLS, min((half + 1) * COLS, ref.shape[1]))
            width = columns.stop - columns.start
            ref[:, columns] = (total_ref[start + half] * norm_scale)[:, :width]
    for granule, (start, stop) in enumerate(column_cuts(first_ref.shape[1])):
        row = granule % 2 * 12
        scaled = total_ref[4 + granule // 2, row : row + 12] * norm_scale
        first_ref[:, start:stop] = scaled[:, : stop - start]


def per_device(belief, target_value, counts, w_first, w_middle, w_last):
    total_rows, inputs = belief.shape
    width = w_last.shape[1]
    units = w_first.shape[1]
    hidden = w_middle.shape[1]
    core, mp = lax.axis_index(CORE), lax.axis_index("mp")
    place = jnp.stack([core, lax.axis_index(Y), lax.axis_index(X), lax.axis_index(ZH)])
    belief_t, target_t, w_last_t = belief.T, target_value.T, w_last.T

    around = (ZH, CORE, "mp")
    hi = lax.ppermute(w_last_t[:CUT], around, [(0, 5), (5, 0), (1, 4), (4, 1)])
    lo = lax.ppermute(w_last_t[CUT:], around, [(2, 3), (3, 2), (6, 7), (7, 6)])
    hi_again = lax.ppermute(hi, CORE, [(0, 1)])
    lo_again = lax.ppermute(lo, CORE, [(1, 0)])

    pre_first = dot(belief, w_first)
    act_first = narrow(jax.nn.silu(pre_first))
    partial_middle = dot(act_first, w_middle)
    arrived = swap(narrow(partial_middle), "mp")

    live_rows = (counts[:, None] > jnp.arange(BLOCK, dtype=jnp.int32)[None, :]).reshape(1, total_rows)
    live = live_rows.astype(F32)
    target_own = lax.dynamic_slice_in_dim(target_t, mp * width, width, 0)
    target_other = lax.dynamic_slice_in_dim(target_t, (1 - mp) * width, width, 0)
    order = jnp.arange(units, dtype=jnp.int32).reshape(4, 2, 4, 2, -1).transpose(3, 0, 2, 1, 4)
    order = jnp.where(core == 0, order[::-1], order).reshape(units)
    onehot = (order[:, None] == jnp.arange(units, dtype=jnp.int32)[None, :]).astype(BF16)

    granules = lambda *lead: ((*lead, ROWS, COLS), BF16)
    act, act_slope, slope_own, last_sent, last_own = call(
        last_kernel,
        "last",
        [SMEM] + [VMEM] * 5,
        [
            ((total_rows, hidden), BF16),
            ((total_rows, hidden), F32),
            ((width, total_rows), BF16),
            granules(16, 4),
            granules(16, 4),
        ],
        [pltpu.VMEM((hidden, units), F32), pltpu.VMEM((units, total_rows), BF16)],
    )(place, partial_middle, arrived, live, target_own, w_last_t)
    last_arrived = swap(last_sent, CORE)

    slope_middle, slope_first, first_sent = call(
        slopes_kernel,
        "slopes",
        [SMEM] + [VMEM] * 7 + [HBM] * 7,
        [((total_rows, hidden), BF16), ((units, total_rows), BF16), granules(16, 7)],
        [
            pltpu.VMEM((width, hidden), BF16),
            pltpu.VMEM((CUT, hidden), BF16),
            pltpu.VMEM((width - CUT, hidden), BF16),
            pltpu.VMEM((units, hidden), BF16),
            pltpu.VMEM((inputs, total_rows), BF16),
            pltpu.SemaphoreType.DMA((5,)),
        ],
    )(
        place, act, act_slope, slope_own, live, target_other, silu_slope(pre_first).T, onehot,
        w_last_t, hi, hi_again, lo, lo_again, w_middle, belief_t,
    )
    first_arrived = swap(first_sent, CORE)

    last_parts = call(
        last_cut_kernel, "last_cut", [SMEM] + [VMEM] * 2, [granules(4, 4)] * 4
    )(place, last_own, last_arrived)
    last_parts = [last_parts[0]] + [rotate(last_parts[k], X, k) for k in (1, 2, 3)]

    middle_sent, middle_own = call(
        middle_kernel,
        "middle",
        [SMEM] + [VMEM] * 2,
        [granules(16, 4)] * 2,
        [pltpu.VMEM((hidden, units), F32)],
    )(place, slope_middle, act_first)
    middle_arrived = swap(middle_sent, CORE)

    parts = call(
        first_cut_kernel,
        "first_cut",
        [SMEM] + [VMEM] * 5,
        [granules(4, 6)] * 4 + [granules(4, 5)] * 4,
        [pltpu.VMEM((16, 7, ROWS, COLS), F32)],
    )(place, slope_first, belief_t, first_arrived, middle_own, middle_arrived)
    x_parts = [parts[0]] + [rotate(parts[k], X, k) for k in (1, 2, 3)]
    y_parts = [parts[4]] + [rotate(parts[4 + k], Y, k) for k in (1, 2, 3)]

    parts = call(
        second_cut_kernel,
        "second_cut",
        [SMEM] + [VMEM] * 12,
        [granules(10)] * 4 + [granules(5)] * 4,
    )(place, *last_parts, *x_parts, *y_parts)
    a_parts = [parts[0]] + [rotate(parts[k], Y, k) for k in (1, 2, 3)]
    b_parts = [parts[4]] + [rotate(parts[4 + k], X, k) for k in (1, 2, 3)]

    sent, own = call(
        third_cut_kernel,
        "third_cut",
        [SMEM] + [VMEM] * 8,
        [granules(8), ((8, ROWS, COLS), F32)],
        [pltpu.VMEM((10, ROWS, COLS), F32), pltpu.VMEM((5, ROWS, COLS), F32)],
    )(place, *a_parts, *b_parts)

    total, squares = call(
        square_kernel, "square", [VMEM] * 2, [((8, ROWS, COLS), F32), ((128, 1, LANES), F32)]
    )(own, swap(sent, ZH))
    squares = lax.all_to_all(squares, ALL, 0, 0, tiled=True)
    grad_first, grad_middle, grad_last = call(
        scale_kernel,
        "scale",
        [VMEM] * 2,
        [((units // 64, inputs), F32), ((ROWS, units), F32), ((ROWS, width), F32)],
    )(total, squares)
    return grad_first.T, grad_middle.T, grad_last


def solution(mesh):
    finer = Mesh(mesh.devices.reshape(4, 2, 4, 2, mesh.shape["mp"]), ALL)
    return jax.shard_map(
        per_device,
        mesh=finer,
        in_specs=(P(DP, None), P(DP, None), P(DP), P(None, "mp"), P("mp", None), P(None, "mp")),
        out_specs=(P(None, MP_DP), P("mp", DP), P(DP, "mp")),
        check_vma=False,
    )
```

```python
import jax
import jax.numpy as jnp
from jax import lax
from jax.experimental import pallas as pl
from jax.experimental.pallas import tpu as pltpu
from jax.sharding import Mesh
from jax.sharding import PartitionSpec as P

BLOCK = 128
PARAMS = 8469504
DP = ("dp_0", "dp_1", "dp_2", "dp_3")
MP_DP = ("mp", "dp_0", "dp_1", "dp_2", "dp_3")
ALL = DP + ("mp",)
Y, ZH, X, CORE = DP
LANES = 128
CUT = 480
ROWS, COLS = 24, 384
VMEM = pl.BlockSpec(memory_space=pltpu.VMEM)
SMEM = pl.BlockSpec(memory_space=pltpu.SMEM)
BF16, F32 = jnp.bfloat16, jnp.float32


def wide(shard):
    return shard.astype(F32)


def narrow(shard):
    return shard.astype(BF16)


def swap(shard, axis):
    return lax.ppermute(shard, axis, [(0, 1), (1, 0)])


def rotate(shard, axis, step):
    return lax.ppermute(shard, axis, [(i, (i + step) % 4) for i in range(4)])


def silu_slope(pre_act):
    sigmoid_of = jax.nn.sigmoid(pre_act)
    return sigmoid_of * (1.0 + pre_act * (1.0 - sigmoid_of))


def dot(left, right):
    return jnp.dot(left, right, preferred_element_type=F32)


def contract(left, right, left_dim, right_dim):
    return lax.dot_general(
        left, right, (((left_dim,), (right_dim,)), ((), ())), preferred_element_type=F32
    )


def call(body, name, in_specs, outs, scratch=(), final=False):
    kernel = pl.pallas_call(
        body,
        out_shape=[(jax.ShapeDtypeStruct if final else pltpu.VMEM)(*out) for out in outs],
        in_specs=in_specs,
        out_specs=[VMEM] * len(outs),
        scratch_shapes=list(scratch),
        compiler_params=pltpu.CompilerParams(vmem_limit_bytes=24 << 20),
        cost_estimate=pl.CostEstimate(flops=1 << 20, bytes_accessed=1 << 20, transcendentals=0),
        name=name,
    )

    def run(*operands):
        return kernel(
            *(
                pltpu.with_memory_space_constraint(operand, pltpu.VMEM) if spec is VMEM else operand
                for operand, spec in zip(operands, in_specs)
            )
        )

    return run


def by_unit(raw_ref, core, out_ref):
    for unit in range(16):
        for z_hi in range(2):
            first = 2 * ROWS * ((unit // 4 * 2 + z_hi) * 4 + unit % 4)
            rows = pl.ds(pl.multiple_of(first + ROWS * core, 8), ROWS)
            for half in range(2):
                out_ref[unit, 2 * z_hi + half] = narrow(
                    raw_ref[rows, half * COLS : (half + 1) * COLS]
                )


def last_kernel(
    place_ref, partial_ref, arrived_ref, live_ref, target_ref, w_ref,
    act_ref, act_slope_ref, slope_ref, sent_ref, own_ref, raw_ref, padded_ref,
):
    core = place_ref[0]
    width = slope_ref.shape[0]
    pre_middle = partial_ref[...] + wide(arrived_ref[...])
    sigmoid_of = 1.0 / (1.0 + jnp.exp(-pre_middle))
    act = narrow(pre_middle * sigmoid_of)
    act_ref[...] = act
    act_slope_ref[...] = sigmoid_of * (1.0 + pre_middle * (1.0 - sigmoid_of))
    mismatch = contract(w_ref[...], act, 1, 1) - wide(target_ref[...])
    slope = narrow(jnp.clip(mismatch, -1.0, 1.0) * live_ref[...])
    slope_ref[...] = slope
    padded_ref[...] = jnp.zeros_like(padded_ref)
    padded_ref[0:width, :] = slope
    raw_ref[...] = contract(act.T, padded_ref[...], 1, 1)
    by_unit(raw_ref, 1 - core, sent_ref)
    by_unit(raw_ref, core, own_ref)


def slopes_kernel(
    place_ref, act_ref, act_slope_ref, slope_ref, live_ref, target_ref, first_slope_ref,
    onehot_ref, w_own_ref, hi_ref, hi_again_ref, lo_ref, lo_again_ref, w_middle_ref, belief_ref,
    slope_middle_ref, slope_first_ref, sent_ref,
):
    is_first = place_ref[0] == 0
    act = act_ref[...]
    live = live_ref[...]
    back = contract(slope_ref[...], w_own_ref[...], 0, 0)
    w_hi = jnp.where(is_first, hi_ref[...], hi_again_ref[...])
    w_lo = jnp.where(is_first, lo_again_ref[...], lo_ref[...])
    for start, weights in ((0, w_hi), (CUT, w_lo)):
        stop = start + weights.shape[0]
        mismatch = contract(weights, act, 1, 1) - wide(target_ref[start:stop, :])
        slope = narrow(jnp.clip(mismatch, -1.0, 1.0) * live)
        back += contract(slope, weights, 0, 0)
    slope_middle = narrow(back * act_slope_ref[...])
    slope_middle_ref[...] = slope_middle
    slope_first = narrow(contract(w_middle_ref[...], slope_middle, 1, 1) * first_slope_ref[...])
    slope_first = narrow(dot(onehot_ref[...], slope_first))
    slope_first_ref[...] = slope_first
    half = slope_first.shape[0] // 2
    for start, stop in column_cuts(belief_ref.shape[0]):
        raw = narrow(contract(slope_first[:half], belief_ref[start:stop, :], 1, 1))
        put_columns(raw, start // COLS, sent_ref)


def column_cuts(width):
    return [(start, min(start + COLS, width)) for start in range(0, width, COLS)]


def put_columns(raw, granule, out_ref):
    width = raw.shape[1]
    if width < COLS:
        raw = jnp.concatenate([raw, jnp.zeros((raw.shape[0], COLS - width), raw.dtype)], 1)
    for unit in range(16):
        out_ref[unit, granule] = raw[unit * ROWS : (unit + 1) * ROWS]


def middle_kernel(place_ref, slope_middle_ref, act_first_ref, sent_ref, own_ref, raw_ref):
    core = place_ref[0]
    raw_ref[...] = contract(slope_middle_ref[...], act_first_ref[...], 0, 0)
    by_unit(raw_ref, 1 - core, sent_ref)
    by_unit(raw_ref, core, own_ref)


def others(me):
    return [me] + [lax.rem(me + step, 4) for step in (1, 2, 3)]


def last_cut_kernel(place_ref, own_ref, arrived_ref, *out_refs):
    for x, out_ref in zip(others(place_ref[2]), out_refs):
        for y in range(4):
            out_ref[y] = narrow(wide(own_ref[4 * y + x]) + wide(arrived_ref[4 * y + x]))


def first_cut_kernel(
    place_ref, slope_first_ref, belief_ref, arrived_ref, middle_ref, middle_arrived_ref, *refs
):
    x_refs, y_refs, raw_ref = refs[:4], refs[4:8], refs[8]
    half = slope_first_ref.shape[0] // 2
    slope = slope_first_ref[half:, :]
    for start, stop in column_cuts(belief_ref.shape[0]):
        raw = contract(slope, belief_ref[start:stop, :], 1, 1)
        put_columns(raw, start // COLS, raw_ref)
    for y, out_ref in zip(others(place_ref[1]), y_refs):
        for x in range(4):
            unit = 4 * y + x
            out_ref[x] = narrow(raw_ref[unit] + wide(arrived_ref[unit]))
    for x, out_ref in zip(others(place_ref[2]), x_refs):
        for y in range(4):
            unit = 4 * y + x
            out_ref[y] = narrow(wide(middle_ref[unit]) + wide(middle_arrived_ref[unit]))


def sum_of(refs, index):
    return sum(wide(ref[index]) for ref in refs[1:]) + wide(refs[0][index])


def second_cut_kernel(place_ref, *refs):
    last_refs, x_refs, y_refs = refs[0:4], refs[4:8], refs[8:12]
    a_refs, b_refs = refs[12:16], refs[16:20]
    for y, out_ref in zip(others(place_ref[1]), a_refs):
        out_ref[0:4] = narrow(sum_of(last_refs, y))
        out_ref[4:8] = narrow(sum_of(x_refs, y))
    for x, out_ref in zip(others(place_ref[2]), b_refs):
        out_ref[...] = narrow(sum_of(y_refs, x))


def third_cut_kernel(place_ref, *refs):
    a_refs, b_refs = refs[0:4], refs[4:8]
    sent_ref, own_ref, sum_a, sum_b = refs[8:12]
    z_hi = place_ref[3]
    sum_a[...] = sum_of(a_refs, slice(None))
    sum_b[...] = sum_of(b_refs, slice(None))
    for side, out_ref in ((1 - z_hi, sent_ref), (z_hi, own_ref)):
        kind = out_ref.dtype
        out_ref[0:2] = sum_a[pl.ds(2 * side, 2)].astype(kind)
        out_ref[2:4] = sum_a[pl.ds(4 + 2 * side, 2)].astype(kind)
        halves = []
        for granule in range(7):
            rows = sum_b[granule]
            halves.append(jnp.where(side == 0, rows[0:12], rows[12:24]))
        halves.append(jnp.zeros_like(halves[0]))
        for pair in range(4):
            out_ref[4 + pair] = jnp.concatenate(halves[2 * pair : 2 * pair + 2], 0).astype(kind)


def square_kernel(own_ref, arrived_ref, total_ref, squares_ref):
    total = own_ref[...] + wide(arrived_ref[...])
    total_ref[...] = total
    squares_ref[...] = jnp.broadcast_to(jnp.sum(total * total), squares_ref.shape)


def scale_kernel(total_ref, squares_ref, first_ref, middle_ref, last_ref):
    square_sum = jnp.sum(squares_ref[...], axis=0)
    norm_scale = lax.rsqrt(square_sum / PARAMS + 1e-06)
    norm_scale = jnp.concatenate([norm_scale] * 3, 1)
    for ref, start in ((last_ref, 0), (middle_ref, 2)):
        for half in range(2):
            columns = slice(half * COLS, min((half + 1) * COLS, ref.shape[1]))
            width = columns.stop - columns.start
            ref[:, columns] = (total_ref[start + half] * norm_scale)[:, :width]
    for granule, (start, stop) in enumerate(column_cuts(first_ref.shape[1])):
        row = granule % 2 * 12
        scaled = total_ref[4 + granule // 2, row : row + 12] * norm_scale
        first_ref[:, start:stop] = scaled[:, : stop - start]


def per_device(belief, target_value, counts, w_first, w_middle, w_last):
    total_rows, inputs = belief.shape
    width = w_last.shape[1]
    units = w_first.shape[1]
    hidden = w_middle.shape[1]
    core, mp = lax.axis_index(CORE), lax.axis_index("mp")
    place = jnp.stack([core, lax.axis_index(Y), lax.axis_index(X), lax.axis_index(ZH)])
    belief_t, target_t, w_last_t = belief.T, target_value.T, w_last.T

    around = (ZH, CORE, "mp")
    hi = lax.ppermute(w_last_t[:CUT], around, [(0, 5), (5, 0), (1, 4), (4, 1)])
    lo = lax.ppermute(w_last_t[CUT:], around, [(2, 3), (3, 2), (6, 7), (7, 6)])

    pre_first = dot(belief, w_first)
    act_first = narrow(jax.nn.silu(pre_first))
    partial_middle = dot(act_first, w_middle)
    arrived = swap(narrow(partial_middle), "mp")
    hi, lo, arrived = lax.optimization_barrier((hi, lo, arrived))
    hi_again = lax.ppermute(hi, CORE, [(0, 1)])
    lo_again = lax.ppermute(lo, CORE, [(1, 0)])

    live_rows = (counts[:, None] > jnp.arange(BLOCK, dtype=jnp.int32)[None, :]).reshape(1, total_rows)
    live = live_rows.astype(F32)
    target_own = lax.dynamic_slice_in_dim(target_t, mp * width, width, 0)
    target_other = lax.dynamic_slice_in_dim(target_t, (1 - mp) * width, width, 0)
    order = jnp.arange(units, dtype=jnp.int32).reshape(4, 2, 4, 2, -1).transpose(3, 0, 2, 1, 4)
    order = jnp.where(core == 0, order[::-1], order).reshape(units)
    onehot = (order[:, None] == jnp.arange(units, dtype=jnp.int32)[None, :]).astype(BF16)

    granules = lambda *lead: ((*lead, ROWS, COLS), BF16)
    act, act_slope, slope_own, last_sent, last_own = call(
        last_kernel,
        "last",
        [SMEM] + [VMEM] * 5,
        [
            ((total_rows, hidden), BF16),
            ((total_rows, hidden), F32),
            ((width, total_rows), BF16),
            granules(16, 4),
            granules(16, 4),
        ],
        [pltpu.VMEM((hidden, units), F32), pltpu.VMEM((units, total_rows), BF16)],
    )(place, partial_middle, arrived, live, target_own, w_last_t)
    last_arrived = swap(last_sent, CORE)

    slope_middle, slope_first, first_sent = call(
        slopes_kernel,
        "slopes",
        [SMEM] + [VMEM] * 14,
        [((total_rows, hidden), BF16), ((units, total_rows), BF16), granules(16, 7)],
    )(
        place, act, act_slope, slope_own, live, target_other, silu_slope(pre_first).T, onehot,
        w_last_t, hi, hi_again, lo, lo_again, w_middle, belief_t,
    )
    first_arrived = swap(first_sent, CORE)

    last_parts = call(
        last_cut_kernel, "last_cut", [SMEM] + [VMEM] * 2, [granules(4, 4)] * 4
    )(place, last_own, last_arrived)
    last_parts = [last_parts[0]] + [rotate(last_parts[k], X, k) for k in (1, 2, 3)]

    middle_sent, middle_own = call(
        middle_kernel,
        "middle",
        [SMEM] + [VMEM] * 2,
        [granules(16, 4)] * 2,
        [pltpu.VMEM((hidden, units), F32)],
    )(place, slope_middle, act_first)
    middle_arrived = swap(middle_sent, CORE)

    parts = call(
        first_cut_kernel,
        "first_cut",
        [SMEM] + [VMEM] * 5,
        [granules(4, 4)] * 4 + [granules(4, 7)] * 4,
        [pltpu.VMEM((16, 7, ROWS, COLS), F32)],
    )(place, slope_first, belief_t, first_arrived, middle_own, middle_arrived)
    x_parts = [parts[0]] + [rotate(parts[k], X, k) for k in (1, 2, 3)]
    y_parts = [parts[4]] + [rotate(parts[4 + k], Y, k) for k in (1, 2, 3)]

    parts = call(
        second_cut_kernel,
        "second_cut",
        [SMEM] + [VMEM] * 12,
        [granules(8)] * 4 + [granules(7)] * 4,
    )(place, *last_parts, *x_parts, *y_parts)
    a_parts = [parts[0]] + [rotate(parts[k], Y, k) for k in (1, 2, 3)]
    b_parts = [parts[4]] + [rotate(parts[4 + k], X, k) for k in (1, 2, 3)]

    sent, own = call(
        third_cut_kernel,
        "third_cut",
        [SMEM] + [VMEM] * 8,
        [granules(8), ((8, ROWS, COLS), F32)],
        [pltpu.VMEM((8, ROWS, COLS), F32), pltpu.VMEM((7, ROWS, COLS), F32)],
    )(place, *a_parts, *b_parts)

    total, squares = call(
        square_kernel, "square", [VMEM] * 2, [((8, ROWS, COLS), F32), ((128, 1, LANES), F32)]
    )(own, swap(sent, ZH))
    squares = lax.all_to_all(squares, ALL, 0, 0, tiled=True)
    grad_first, grad_middle, grad_last = call(
        scale_kernel,
        "scale",
        [VMEM] * 2,
        [((units // 64, inputs), F32), ((ROWS, units), F32), ((ROWS, width), F32)],
        final=True,
    )(total, squares)
    return grad_first.T, grad_middle.T, grad_last


def solution(mesh):
    finer = Mesh(mesh.devices.reshape(4, 2, 4, 2, mesh.shape["mp"]), ALL)
    return jax.shard_map(
        per_device,
        mesh=finer,
        in_specs=(P(DP, None), P(DP, None), P(DP), P(None, "mp"), P("mp", None), P(None, "mp")),
        out_specs=(P(None, MP_DP), P("mp", DP), P(DP, "mp")),
        check_vma=False,
    )
```

```python
import jax
import jax.numpy as jnp
from jax import lax
from jax.experimental import pallas as pl
from jax.experimental.pallas import tpu as pltpu
from jax.sharding import Mesh
from jax.sharding import PartitionSpec as P

BLOCK = 128
PARAMS = 8469504
DP = ("dp_0", "dp_1", "dp_2", "dp_3")
MP_DP = ("mp", "dp_0", "dp_1", "dp_2", "dp_3")
ALL = DP + ("mp",)
Y, ZH, X, CORE = DP
LANES = 128
ROWS, COLS = 24, 384
VMEM = pl.BlockSpec(memory_space=pltpu.VMEM)
SMEM = pl.BlockSpec(memory_space=pltpu.SMEM)
BF16, F32 = jnp.bfloat16, jnp.float32


def wide(shard):
    return shard.astype(F32)


def narrow(shard):
    return shard.astype(BF16)


def swap(shard, axis):
    return lax.ppermute(shard, axis, [(0, 1), (1, 0)])


def to_pair(shard, axis, order):
    pairs = [(i, i ^ 1) for i in range(4)] if order == 0 else [(i, 3 - i) for i in range(4)]
    return lax.ppermute(shard, axis, pairs)


def silu_slope(pre_act):
    sigmoid_of = jax.nn.sigmoid(pre_act)
    return sigmoid_of * (1.0 + pre_act * (1.0 - sigmoid_of))


def dot(left, right):
    return jnp.dot(left, right, preferred_element_type=F32)


def contract(left, right, left_dim, right_dim):
    return lax.dot_general(
        left, right, (((left_dim,), (right_dim,)), ((), ())), preferred_element_type=F32
    )


def call(body, name, in_specs, outs, scratch=(), final=False):
    kernel = pl.pallas_call(
        body,
        out_shape=[(jax.ShapeDtypeStruct if final else pltpu.VMEM)(*out) for out in outs],
        in_specs=in_specs,
        out_specs=[VMEM] * len(outs),
        scratch_shapes=list(scratch),
        compiler_params=pltpu.CompilerParams(vmem_limit_bytes=24 << 20),
        cost_estimate=pl.CostEstimate(flops=1 << 34, bytes_accessed=1 << 26, transcendentals=0),
        name=name,
    )

    def run(*operands):
        return kernel(
            *(
                pltpu.with_memory_space_constraint(operand, pltpu.VMEM) if spec is VMEM else operand
                for operand, spec in zip(operands, in_specs)
            )
        )

    return run


def by_unit(raw_ref, core, out_ref, start):
    for unit in range(16):
        for z_hi in range(2):
            first = 2 * ROWS * ((unit // 4 * 2 + z_hi) * 4 + unit % 4)
            rows = pl.ds(pl.multiple_of(first + ROWS * core, 8), ROWS)
            for half in range(2):
                out_ref[unit, start + 2 * z_hi + half] = narrow(
                    raw_ref[rows, half * COLS : (half + 1) * COLS]
                )


def hidden_kernel(
    partial_ref, arrived_ref, live_ref, target_ref, w_ref,
    act_ref, act_slope_ref, slope_ref, back_ref,
):
    pre_middle = partial_ref[...] + wide(arrived_ref[...])
    sigmoid_of = 1.0 / (1.0 + jnp.exp(-pre_middle))
    act = narrow(pre_middle * sigmoid_of)
    act_ref[...] = act
    act_slope_ref[...] = sigmoid_of * (1.0 + pre_middle * (1.0 - sigmoid_of))
    slope = slope_of(w_ref[...], act, target_ref[...], live_ref[...])
    slope_ref[...] = slope
    back_ref[...] = contract(slope, w_ref[...], 0, 0)


def slope_of(weights, act, target, live):
    mismatch = contract(weights, act, 1, 1) - wide(target)
    return narrow(jnp.clip(mismatch, -1.0, 1.0) * live)


def slopes_kernel(
    place_ref, act_ref, act_slope_ref, back_ref, live_ref, target_ref, first_slope_ref,
    onehot_ref, fetched_ref, relayed_ref, w_middle_ref, belief_ref,
    slope_middle_ref, slope_first_ref, sent_ref,
):
    w_other = jnp.where(place_ref[0] == 0, fetched_ref[...], relayed_ref[...])
    slope = slope_of(w_other, act_ref[...], target_ref[...], live_ref[...])
    back = back_ref[...] + contract(slope, w_other, 0, 0)
    slope_middle = narrow(back * act_slope_ref[...])
    slope_middle_ref[...] = slope_middle
    slope_first = narrow(contract(w_middle_ref[...], slope_middle, 1, 1) * first_slope_ref[...])
    slope_first = narrow(dot(onehot_ref[...], slope_first))
    slope_first_ref[...] = slope_first
    half = slope_first.shape[0] // 2
    for start, stop in column_cuts(belief_ref.shape[0]):
        raw = narrow(contract(slope_first[:half], belief_ref[start:stop, :], 1, 1))
        put_columns(raw, start // COLS, sent_ref)


def column_cuts(width):
    return [(start, min(start + COLS, width)) for start in range(0, width, COLS)]


def put_columns(raw, granule, out_ref):
    width = raw.shape[1]
    if width < COLS:
        raw = jnp.concatenate([raw, jnp.zeros((raw.shape[0], COLS - width), raw.dtype)], 1)
    for unit in range(16):
        out_ref[unit, granule] = raw[unit * ROWS : (unit + 1) * ROWS]


def later_kernel(
    place_ref, act_ref, slope_ref, slope_middle_ref, act_first_ref, sent_ref, own_ref, raw_ref, padded_ref
):
    core = place_ref[0]
    padded_ref[...] = jnp.zeros_like(padded_ref)
    padded_ref[0 : slope_ref.shape[0], :] = slope_ref[...]
    raw_ref[...] = contract(act_ref[...].T, padded_ref[...], 1, 1)
    by_unit(raw_ref, 1 - core, sent_ref, 0)
    by_unit(raw_ref, core, own_ref, 0)
    raw_ref[...] = contract(slope_middle_ref[...], act_first_ref[...], 0, 0)
    by_unit(raw_ref, 1 - core, sent_ref, 4)
    by_unit(raw_ref, core, own_ref, 4)


def kept_and_sent(me, order):
    near, far, opposite = lax.bitwise_xor(me, 1), 3 - me, lax.bitwise_xor(me, 2)
    return ((me, far), (near, opposite)) if order == 0 else ((me, near), (far, opposite))


def cut_first_kernel(place_ref, slope_first_ref, belief_ref, arrived_ref, *refs):
    raw_ref = refs[-1]
    half = slope_first_ref.shape[0] // 2
    slope = slope_first_ref[half:, :]
    for start, stop in column_cuts(belief_ref.shape[0]):
        raw = contract(slope, belief_ref[start:stop, :], 1, 1)
        put_columns(raw, start // COLS, raw_ref)
    for order, part in enumerate((slice(0, 4), slice(4, 7))):
        for side, blocks in enumerate(kept_and_sent(place_ref[1], order)):
            out_ref = refs[2 * order + side]
            for position, y in enumerate(blocks):
                for x in range(4):
                    total = raw_ref[4 * y + x, part] + wide(arrived_ref[4 * y + x, part])
                    out_ref[position, x] = total.astype(out_ref.dtype)


def cut_rest_kernel(place_ref, own_ref, arrived_ref, *refs):
    for order, part in enumerate((slice(0, 4), slice(4, 8))):
        for side, blocks in enumerate(kept_and_sent(place_ref[2], order)):
            out_ref = refs[2 * order + side]
            for position, x in enumerate(blocks):
                for y in range(4):
                    total = wide(own_ref[4 * y + x, part]) + wide(arrived_ref[4 * y + x, part])
                    out_ref[position, y] = total.astype(out_ref.dtype)


def halve_kernel(*refs):
    for part in range(4):
        kept_ref, arrived_ref = refs[2 * part : 2 * part + 2]
        kept_out, sent_out = refs[8 + 2 * part : 10 + 2 * part]
        kept_out[...] = kept_ref[0] + wide(arrived_ref[0])
        sent_out[...] = narrow(kept_ref[1] + wide(arrived_ref[1]))


def turn_kernel(place_ref, *refs):
    scratch = refs[16:]
    for part in range(4):
        kept_ref, arrived_ref = refs[2 * part : 2 * part + 2]
        scratch[part][...] = kept_ref[...] + wide(arrived_ref[...])
        for side, blocks in enumerate(kept_and_sent(place_ref[2 if part < 2 else 1], part % 2)):
            out_ref = refs[8 + 2 * part + side]
            for position, block in enumerate(blocks):
                out_ref[position] = scratch[part][block].astype(out_ref.dtype)


def z_cut_kernel(place_ref, *refs):
    sent_ref, own_ref, last_sum, middle_sum = refs[8:12]
    z_hi = place_ref[3]
    low, high, last, middle = (
        refs[2 * part][...] + wide(refs[2 * part + 1][...]) for part in range(4)
    )
    last_sum[...] = last
    middle_sum[...] = middle
    rows = [low[granule] for granule in range(4)] + [high[granule] for granule in range(3)]
    for side, out_ref in ((1 - z_hi, sent_ref), (z_hi, own_ref)):
        kind = out_ref.dtype
        out_ref[0:2] = last_sum[pl.ds(2 * side, 2)].astype(kind)
        out_ref[2:4] = middle_sum[pl.ds(2 * side, 2)].astype(kind)
        halves = [jnp.where(side == 0, row[0:12], row[12:24]) for row in rows]
        halves.append(jnp.zeros_like(halves[0]))
        for pair in range(4):
            out_ref[4 + pair] = jnp.concatenate(halves[2 * pair : 2 * pair + 2], 0).astype(kind)


def square_kernel(own_ref, arrived_ref, total_ref, squares_ref):
    total = own_ref[...] + wide(arrived_ref[...])
    total_ref[...] = total
    squares_ref[...] = jnp.broadcast_to(jnp.sum(total * total), squares_ref.shape)


def scale_kernel(total_ref, squares_ref, first_ref, middle_ref, last_ref):
    square_sum = jnp.sum(squares_ref[...], axis=0)
    norm_scale = lax.rsqrt(square_sum / PARAMS + 1e-06)
    norm_scale = jnp.concatenate([norm_scale] * 3, 1)
    for ref, start in ((last_ref, 0), (middle_ref, 2)):
        for half in range(2):
            columns = slice(half * COLS, min((half + 1) * COLS, ref.shape[1]))
            width = columns.stop - columns.start
            ref[:, columns] = (total_ref[start + half] * norm_scale)[:, :width]
    for granule, (start, stop) in enumerate(column_cuts(first_ref.shape[1])):
        row = granule % 2 * 12
        scaled = total_ref[4 + granule // 2, row : row + 12] * norm_scale
        first_ref[:, start:stop] = scaled[:, : stop - start]


def granules(*lead, kind=BF16):
    return ((*lead, ROWS, COLS), kind)


def per_device(belief, target_value, counts, w_first, w_middle, w_last):
    total_rows, inputs = belief.shape
    width = w_last.shape[1]
    units = w_first.shape[1]
    hidden = w_middle.shape[1]
    belief_t, w_last_t = belief.T, w_last.T

    around = (ZH, CORE, "mp")
    fetched = lax.ppermute(w_last_t, around, [(0, 5), (5, 0), (1, 4), (4, 1)])

    pre_first = dot(belief, w_first)
    act_first = narrow(jax.nn.silu(pre_first))
    partial_middle = dot(act_first, w_middle)
    hidden_sent = narrow(partial_middle)
    arrived = swap(hidden_sent, "mp")

    indices = jnp.stack([lax.axis_index(axis) for axis in (CORE, Y, X, ZH, "mp")])
    indices, pre_first, target_value, hidden_sent = lax.optimization_barrier(
        (indices, pre_first, target_value, hidden_sent)
    )
    core, mp = indices[0], indices[4]
    live_rows = (counts[:, None] > jnp.arange(BLOCK, dtype=jnp.int32)[None, :]).reshape(1, total_rows)
    live = live_rows.astype(F32)
    target_t = target_value.T
    target_own = lax.dynamic_slice_in_dim(target_t, mp * width, width, 0)
    target_other = lax.dynamic_slice_in_dim(target_t, (1 - mp) * width, width, 0)
    order = jnp.arange(units, dtype=jnp.int32).reshape(4, 2, 4, 2, -1).transpose(3, 0, 2, 1, 4)
    order = jnp.where(core == 0, order[::-1], order).reshape(units)
    onehot = (order[:, None] == jnp.arange(units, dtype=jnp.int32)[None, :]).astype(BF16)
    first_slope = silu_slope(pre_first).T
    fetched, place, live, target_own, target_other, onehot, first_slope = lax.optimization_barrier(
        (fetched, indices[:4], live, target_own, target_other, onehot, first_slope)
    )
    relayed = lax.ppermute(fetched, CORE, [(0, 1)])

    act, act_slope, slope_own, back_own = call(
        hidden_kernel,
        "hidden",
        [VMEM] * 5,
        [
            ((total_rows, hidden), BF16),
            ((total_rows, hidden), F32),
            ((width, total_rows), BF16),
            ((total_rows, hidden), F32),
        ],
    )(partial_middle, arrived, live, target_own, w_last_t)

    slope_middle, slope_first, first_sent = call(
        slopes_kernel,
        "slopes",
        [SMEM] + [VMEM] * 11,
        [((total_rows, hidden), BF16), ((units, total_rows), BF16), granules(16, 7)],
    )(
        place, act, act_slope, back_own, live, target_other, first_slope, onehot,
        fetched, relayed, w_middle, belief_t,
    )
    first_arrived = swap(first_sent, CORE)

    rest_sent, rest_own = call(
        later_kernel,
        "later",
        [SMEM] + [VMEM] * 4,
        [granules(16, 8)] * 2,
        [pltpu.VMEM((hidden, units), F32), pltpu.VMEM((units, total_rows), BF16)],
    )(place, act, slope_own, slope_middle, act_first)
    rest_arrived = swap(rest_sent, CORE)

    def pairs(*sizes):
        return [out for size in sizes for out in (granules(*size, kind=F32), granules(*size))]

    def exchange(parts, axes, orders):
        return [
            part if side == 0 else to_pair(part, axes[i], orders[i])
            for i in range(len(parts) // 2)
            for side, part in enumerate(parts[2 * i : 2 * i + 2])
        ]

    parts = exchange(
        call(
            cut_first_kernel,
            "cut_first",
            [SMEM] + [VMEM] * 3,
            pairs((2, 4, 4), (2, 4, 3)),
            [pltpu.VMEM((16, 7, ROWS, COLS), F32)],
        )(place, slope_first, belief_t, first_arrived),
        (Y, Y),
        (0, 1),
    )
    parts += exchange(
        call(cut_rest_kernel, "cut_rest", [SMEM] + [VMEM] * 2, pairs((2, 4, 4), (2, 4, 4)))(
            place, rest_own, rest_arrived
        ),
        (X, X),
        (0, 1),
    )
    sizes = (4, 3, 4, 4)
    parts = exchange(
        call(halve_kernel, "halve", [VMEM] * 8, pairs(*((4, size) for size in sizes)))(*parts),
        (Y, Y, X, X),
        (1, 0, 1, 0),
    )
    parts = exchange(
        call(
            turn_kernel,
            "turn",
            [SMEM] + [VMEM] * 8,
            pairs(*((2, size) for size in sizes)),
            [pltpu.VMEM((4, size, ROWS, COLS), F32) for size in sizes],
        )(place, *parts),
        (X, X, Y, Y),
        (0, 1, 0, 1),
    )
    parts = exchange(
        call(halve_kernel, "halve", [VMEM] * 8, pairs(*((size,) for size in sizes)))(*parts),
        (X, X, Y, Y),
        (1, 0, 1, 0),
    )
    sent, own = call(
        z_cut_kernel,
        "z_cut",
        [SMEM] + [VMEM] * 8,
        [granules(8), granules(8, kind=F32)],
        [pltpu.VMEM((4, ROWS, COLS), F32)] * 2,
    )(place, *parts)

    total, squares = call(
        square_kernel, "square", [VMEM] * 2, [((8, ROWS, COLS), F32), ((128, 1, LANES), F32)]
    )(own, swap(sent, ZH))
    squares = lax.all_to_all(squares, ALL, 0, 0, tiled=True)
    grad_first, grad_middle, grad_last = call(
        scale_kernel,
        "scale",
        [VMEM] * 2,
        [((units // 64, inputs), F32), ((ROWS, units), F32), ((ROWS, width), F32)],
        final=True,
    )(total, squares)
    return grad_first.T, grad_middle.T, grad_last


def solution(mesh):
    finer = Mesh(mesh.devices.reshape(4, 2, 4, 2, mesh.shape["mp"]), ALL)
    return jax.shard_map(
        per_device,
        mesh=finer,
        in_specs=(P(DP, None), P(DP, None), P(DP), P(None, "mp"), P("mp", None), P(None, "mp")),
        out_specs=(P(None, MP_DP), P("mp", DP), P(DP, "mp")),
        check_vma=False,
    )
```

```python
import jax
import jax.numpy as jnp
import numpy as np
from jax import lax
from jax.experimental import pallas as pl
from jax.experimental.pallas import tpu as pltpu
from jax.sharding import Mesh
from jax.sharding import PartitionSpec as P

BLOCK = 128
PARAMS = 8469504
DP = ("dp_0", "dp_1", "dp_2", "dp_3")
MP_DP = ("mp", "dp_0", "dp_1", "dp_2", "dp_3")
ALL = DP + ("mp",)
Y, ZH, X, CORE = DP
LANES = 128
ROWS, COLS = 24, 384
VMEM = pl.BlockSpec(memory_space=pltpu.VMEM)
SMEM = pl.BlockSpec(memory_space=pltpu.SMEM)
HBM = pl.BlockSpec(memory_space=pl.ANY)
BF16, F32 = jnp.bfloat16, jnp.float32


def wide(shard):
    return shard.astype(F32)


def narrow(shard):
    return shard.astype(BF16)


def swap(shard, axis):
    return lax.ppermute(shard, axis, [(0, 1), (1, 0)])


def to_pair(shard, axis, order):
    pairs = [(i, i ^ 1) for i in range(4)] if order == 0 else [(i, 3 - i) for i in range(4)]
    return lax.ppermute(shard, axis, pairs)


def silu_slope(pre_act):
    sigmoid_of = 1.0 / (1.0 + jnp.exp(-pre_act))
    return sigmoid_of * (1.0 + pre_act * (1.0 - sigmoid_of))


def dot(left, right):
    return jnp.dot(left, right, preferred_element_type=F32)


def contract(left, right, left_dim, right_dim):
    return lax.dot_general(
        left, right, (((left_dim,), (right_dim,)), ((), ())), preferred_element_type=F32
    )


def call(body, name, in_specs, outs, scratch=(), final=False):
    kernel = pl.pallas_call(
        body,
        out_shape=[(jax.ShapeDtypeStruct if final else pltpu.VMEM)(*out) for out in outs],
        in_specs=in_specs,
        out_specs=[VMEM] * len(outs),
        scratch_shapes=list(scratch),
        compiler_params=pltpu.CompilerParams(vmem_limit_bytes=24 << 20),
        cost_estimate=pl.CostEstimate(flops=1 << 34, bytes_accessed=1 << 26, transcendentals=0),
        name=name,
    )

    def run(*operands):
        return kernel(
            *(
                pltpu.with_memory_space_constraint(operand, pltpu.VMEM) if spec is VMEM else operand
                for operand, spec in zip(operands, in_specs)
            )
        )

    return run


def by_unit(raw_ref, core, out_ref, start):
    for unit in range(16):
        for z_hi in range(2):
            first = 2 * ROWS * ((unit // 4 * 2 + z_hi) * 4 + unit % 4)
            rows = pl.ds(pl.multiple_of(first + ROWS * core, 8), ROWS)
            for half in range(2):
                out_ref[unit, start + 2 * z_hi + half] = narrow(
                    raw_ref[rows, half * COLS : (half + 1) * COLS]
                )


def forward_kernel(
    belief_ref, w_first_ref, w_middle_ref, pre_first_ref, act_first_ref, sent_ref
):
    pre_first = contract(belief_ref[...], w_first_ref[...], 0, 0)
    pre_first_ref[...] = pre_first
    act_first = narrow(pre_first / (1.0 + jnp.exp(-pre_first)))
    act_first_ref[...] = act_first
    sent_ref[...] = narrow(dot(act_first, w_middle_ref[...]))


def stage_kernel(
    place_ref, counts_ref, pre_first_ref, orders_ref, target_hbm, w_last_hbm,
    w_own_ref, target_own_ref, target_other_ref, first_slope_ref, onehot_ref, live_ref,
    target_ref, sems,
):
    copies = (
        pltpu.make_async_copy(target_hbm, target_ref, sems.at[0]),
        pltpu.make_async_copy(w_last_hbm, w_own_ref, sems.at[1]),
    )
    for copy in copies:
        copy.start()
    first_slope_ref[...] = silu_slope(pre_first_ref[...])
    order = jnp.where(place_ref[0] == 0, orders_ref[0], orders_ref[1])
    units = lax.broadcasted_iota(jnp.int32, onehot_ref.shape, 1)
    onehot_ref[...] = jnp.where(order == units, 1.0, 0.0).astype(BF16)
    row = lax.broadcasted_iota(jnp.int32, live_ref.shape, 1)
    count = jnp.where(row < BLOCK, counts_ref[0], counts_ref[1] + BLOCK)
    live_ref[...] = jnp.where(row < count, 1.0, 0.0)
    copies[0].wait()
    width = target_own_ref.shape[0]
    low, high = target_ref[0:width, :], target_ref[width : 2 * width, :]
    is_low = place_ref[4] == 0
    target_own_ref[...] = jnp.where(is_low, low, high)
    target_other_ref[...] = jnp.where(is_low, high, low)
    copies[1].wait()


def hidden_kernel(
    partial_ref, arrived_ref, live_ref, target_ref, w_ref,
    act_ref, act_slope_ref, slope_ref, back_ref,
):
    pre_middle = wide(partial_ref[...]) + wide(arrived_ref[...])
    sigmoid_of = 1.0 / (1.0 + jnp.exp(-pre_middle))
    act = narrow(pre_middle * sigmoid_of)
    act_ref[...] = act
    act_slope_ref[...] = sigmoid_of * (1.0 + pre_middle * (1.0 - sigmoid_of))
    slope = slope_of(w_ref[...], act, target_ref[...], live_ref[...])
    slope_ref[...] = slope
    back_ref[...] = contract(slope, w_ref[...], 0, 0)


def slope_of(weights, act, target, live):
    mismatch = contract(weights, act, 1, 1) - wide(target)
    return narrow(jnp.clip(mismatch, -1.0, 1.0) * live)


def slopes_kernel(
    place_ref, act_ref, act_slope_ref, back_ref, live_ref, target_ref, first_slope_ref,
    onehot_ref, fetched_ref, relayed_ref, w_middle_ref, belief_ref,
    slope_middle_ref, slope_first_ref, sent_ref,
):
    w_other = jnp.where(place_ref[0] == 0, fetched_ref[...], relayed_ref[...])
    slope = slope_of(w_other, act_ref[...], target_ref[...], live_ref[...])
    back = back_ref[...] + contract(slope, w_other, 0, 0)
    slope_middle = narrow(back * act_slope_ref[...])
    slope_middle_ref[...] = slope_middle
    slope_first = narrow(contract(slope_middle, w_middle_ref[...], 1, 1) * first_slope_ref[...])
    slope_first = narrow(contract(onehot_ref[...], slope_first, 1, 1))
    slope_first_ref[...] = slope_first
    half = slope_first.shape[0] // 2
    for start, stop in column_cuts(belief_ref.shape[0]):
        raw = narrow(contract(slope_first[:half], belief_ref[start:stop, :], 1, 1))
        put_columns(raw, start // COLS, sent_ref)


def column_cuts(width):
    return [(start, min(start + COLS, width)) for start in range(0, width, COLS)]


def put_columns(raw, granule, out_ref):
    width = raw.shape[1]
    if width < COLS:
        raw = jnp.concatenate([raw, jnp.zeros((raw.shape[0], COLS - width), raw.dtype)], 1)
    for unit in range(16):
        out_ref[unit, granule] = raw[unit * ROWS : (unit + 1) * ROWS]


def later_kernel(
    place_ref, act_ref, slope_ref, slope_middle_ref, act_first_ref, sent_ref, own_ref, raw_ref, padded_ref
):
    core = place_ref[0]
    padded_ref[...] = jnp.zeros_like(padded_ref)
    padded_ref[0 : slope_ref.shape[0], :] = slope_ref[...]
    raw_ref[...] = contract(act_ref[...].T, padded_ref[...], 1, 1)
    by_unit(raw_ref, 1 - core, sent_ref, 0)
    by_unit(raw_ref, core, own_ref, 0)
    raw_ref[...] = contract(slope_middle_ref[...], act_first_ref[...], 0, 0)
    by_unit(raw_ref, 1 - core, sent_ref, 4)
    by_unit(raw_ref, core, own_ref, 4)


def kept_and_sent(me, order):
    near, far, opposite = lax.bitwise_xor(me, 1), 3 - me, lax.bitwise_xor(me, 2)
    return ((me, far), (near, opposite)) if order == 0 else ((me, near), (far, opposite))


def cut_first_kernel(place_ref, slope_first_ref, belief_ref, arrived_ref, *refs):
    raw_ref = refs[-1]
    half = slope_first_ref.shape[0] // 2
    slope = slope_first_ref[half:, :]
    for start, stop in column_cuts(belief_ref.shape[0]):
        raw = contract(slope, belief_ref[start:stop, :], 1, 1)
        put_columns(raw, start // COLS, raw_ref)
    for order, part in enumerate((slice(0, 4), slice(4, 7))):
        for side, blocks in enumerate(kept_and_sent(place_ref[1], order)):
            out_ref = refs[2 * order + side]
            for position, y in enumerate(blocks):
                for x in range(4):
                    total = raw_ref[4 * y + x, part] + wide(arrived_ref[4 * y + x, part])
                    out_ref[position, x] = total.astype(out_ref.dtype)


def cut_rest_kernel(place_ref, own_ref, arrived_ref, *refs):
    for order, part in enumerate((slice(0, 4), slice(4, 8))):
        for side, blocks in enumerate(kept_and_sent(place_ref[2], order)):
            out_ref = refs[2 * order + side]
            for position, x in enumerate(blocks):
                for y in range(4):
                    total = wide(own_ref[4 * y + x, part]) + wide(arrived_ref[4 * y + x, part])
                    out_ref[position, y] = total.astype(out_ref.dtype)


def halve_kernel(*refs):
    for part in range(4):
        kept_ref, arrived_ref = refs[2 * part : 2 * part + 2]
        kept_out, sent_out = refs[8 + 2 * part : 10 + 2 * part]
        kept_out[...] = kept_ref[0] + wide(arrived_ref[0])
        sent_out[...] = narrow(kept_ref[1] + wide(arrived_ref[1]))


def turn_kernel(place_ref, *refs):
    scratch = refs[16:]
    for part in range(4):
        kept_ref, arrived_ref = refs[2 * part : 2 * part + 2]
        scratch[part][...] = kept_ref[...] + wide(arrived_ref[...])
        for side, blocks in enumerate(kept_and_sent(place_ref[2 if part < 2 else 1], part % 2)):
            out_ref = refs[8 + 2 * part + side]
            for position, block in enumerate(blocks):
                out_ref[position] = scratch[part][block].astype(out_ref.dtype)


def z_cut_kernel(place_ref, *refs):
    sent_ref, own_ref, last_sum, middle_sum = refs[8:12]
    z_hi = place_ref[3]
    low, high, last, middle = (
        refs[2 * part][...] + wide(refs[2 * part + 1][...]) for part in range(4)
    )
    last_sum[...] = last
    middle_sum[...] = middle
    rows = [low[granule] for granule in range(4)] + [high[granule] for granule in range(3)]
    for side, out_ref in ((1 - z_hi, sent_ref), (z_hi, own_ref)):
        kind = out_ref.dtype
        out_ref[0:2] = last_sum[pl.ds(2 * side, 2)].astype(kind)
        out_ref[2:4] = middle_sum[pl.ds(2 * side, 2)].astype(kind)
        halves = [jnp.where(side == 0, row[0:12], row[12:24]) for row in rows]
        halves.append(jnp.zeros_like(halves[0]))
        for pair in range(4):
            out_ref[4 + pair] = jnp.concatenate(halves[2 * pair : 2 * pair + 2], 0).astype(kind)


def square_kernel(own_ref, arrived_ref, total_ref, squares_ref):
    total = own_ref[...] + wide(arrived_ref[...])
    total_ref[...] = total
    squares_ref[...] = jnp.broadcast_to(jnp.sum(total * total), squares_ref.shape)


def scale_kernel(total_ref, squares_ref, first_ref, middle_ref, last_ref):
    square_sum = jnp.sum(squares_ref[...], axis=0)
    norm_scale = lax.rsqrt(square_sum / PARAMS + 1e-06)
    norm_scale = jnp.concatenate([norm_scale] * 3, 1)
    for ref, start in ((last_ref, 0), (middle_ref, 2)):
        for half in range(2):
            columns = slice(half * COLS, min((half + 1) * COLS, ref.shape[1]))
            width = columns.stop - columns.start
            ref[:, columns] = (total_ref[start + half] * norm_scale)[:, :width]
    for granule, (start, stop) in enumerate(column_cuts(first_ref.shape[1])):
        row = granule % 2 * 12
        scaled = total_ref[4 + granule // 2, row : row + 12] * norm_scale
        first_ref[:, start:stop] = scaled[:, : stop - start]


def granules(*lead, kind=BF16):
    return ((*lead, ROWS, COLS), kind)


def per_device(belief, target_value, counts, w_first, w_middle, w_last):
    total_rows, inputs = belief.shape
    width = w_last.shape[1]
    units = w_first.shape[1]
    hidden = w_middle.shape[1]
    belief_t, w_last_t = belief.T, w_last.T

    around = (ZH, CORE, "mp")
    fetched = lax.ppermute(w_last_t, around, [(0, 5), (5, 0), (1, 4), (4, 1)])

    indices = (CORE, Y, X, ZH, "mp")
    place = jnp.stack([lax.axis_index(axis) for axis in indices])
    pre_first, act_first, hidden_sent = call(
        forward_kernel,
        "forward",
        [VMEM] * 3,
        [
            ((total_rows, units), F32),
            ((total_rows, units), BF16),
            ((total_rows, hidden), BF16),
        ],
        final=True,
    )(belief_t, w_first, w_middle)
    arrived = swap(hidden_sent, "mp")

    order = np.arange(units, dtype=np.int32).reshape(4, 2, 4, 2, -1).transpose(3, 0, 2, 1, 4)
    orders = np.stack([order[::-1], order]).reshape(2, units, 1)
    w_own, target_own, target_other, first_slope, onehot, live = call(
        stage_kernel,
        "stage",
        [SMEM, SMEM, VMEM, VMEM, HBM, HBM],
        [
            ((width, hidden), BF16),
            ((width, total_rows), BF16),
            ((width, total_rows), BF16),
            ((total_rows, units), F32),
            ((units, units), BF16),
            ((1, total_rows), F32),
        ],
        [pltpu.VMEM((2 * width, total_rows), BF16), pltpu.SemaphoreType.DMA((2,))],
    )(place, counts, pre_first, jnp.asarray(orders), target_value.T, w_last_t)
    fetched, live = lax.optimization_barrier((fetched, live))
    relayed = lax.ppermute(fetched, CORE, [(0, 1)])

    act, act_slope, slope_own, back_own = call(
        hidden_kernel,
        "hidden",
        [VMEM] * 5,
        [
            ((total_rows, hidden), BF16),
            ((total_rows, hidden), F32),
            ((width, total_rows), BF16),
            ((total_rows, hidden), F32),
        ],
    )(hidden_sent, arrived, live, target_own, w_own)

    slope_middle, slope_first, first_sent = call(
        slopes_kernel,
        "slopes",
        [SMEM] + [VMEM] * 11,
        [((total_rows, hidden), BF16), ((units, total_rows), BF16), granules(16, 7)],
    )(
        place, act, act_slope, back_own, live, target_other, first_slope, onehot,
        fetched, relayed, w_middle, belief_t,
    )
    first_arrived = swap(first_sent, CORE)

    rest_sent, rest_own = call(
        later_kernel,
        "later",
        [SMEM] + [VMEM] * 4,
        [granules(16, 8)] * 2,
        [pltpu.VMEM((hidden, units), F32), pltpu.VMEM((units, total_rows), BF16)],
    )(place, act, slope_own, slope_middle, act_first)
    rest_arrived = swap(rest_sent, CORE)

    def pairs(*sizes):
        return [out for size in sizes for out in (granules(*size, kind=F32), granules(*size))]

    def exchange(parts, axes, orders):
        return [
            part if side == 0 else to_pair(part, axes[i], orders[i])
            for i in range(len(parts) // 2)
            for side, part in enumerate(parts[2 * i : 2 * i + 2])
        ]

    parts = exchange(
        call(
            cut_first_kernel,
            "cut_first",
            [SMEM] + [VMEM] * 3,
            pairs((2, 4, 4), (2, 4, 3)),
            [pltpu.VMEM((16, 7, ROWS, COLS), F32)],
        )(place, slope_first, belief_t, first_arrived),
        (Y, Y),
        (0, 1),
    )
    parts += exchange(
        call(cut_rest_kernel, "cut_rest", [SMEM] + [VMEM] * 2, pairs((2, 4, 4), (2, 4, 4)))(
            place, rest_own, rest_arrived
        ),
        (X, X),
        (0, 1),
    )
    sizes = (4, 3, 4, 4)
    parts = exchange(
        call(halve_kernel, "halve", [VMEM] * 8, pairs(*((4, size) for size in sizes)))(*parts),
        (Y, Y, X, X),
        (1, 0, 1, 0),
    )
    parts = exchange(
        call(
            turn_kernel,
            "turn",
            [SMEM] + [VMEM] * 8,
            pairs(*((2, size) for size in sizes)),
            [pltpu.VMEM((4, size, ROWS, COLS), F32) for size in sizes],
        )(place, *parts),
        (X, X, Y, Y),
        (0, 1, 0, 1),
    )
    parts = exchange(
        call(halve_kernel, "halve", [VMEM] * 8, pairs(*((size,) for size in sizes)))(*parts),
        (X, X, Y, Y),
        (1, 0, 1, 0),
    )
    sent, own = call(
        z_cut_kernel,
        "z_cut",
        [SMEM] + [VMEM] * 8,
        [granules(8), granules(8, kind=F32)],
        [pltpu.VMEM((4, ROWS, COLS), F32)] * 2,
    )(place, *parts)

    total, squares = call(
        square_kernel, "square", [VMEM] * 2, [((8, ROWS, COLS), F32), ((128, 1, LANES), F32)]
    )(own, swap(sent, ZH))
    squares = lax.all_to_all(squares, ALL, 0, 0, tiled=True)
    grad_first, grad_middle, grad_last = call(
        scale_kernel,
        "scale",
        [VMEM] * 2,
        [((units // 64, inputs), F32), ((ROWS, units), F32), ((ROWS, width), F32)],
        final=True,
    )(total, squares)
    return grad_first.T, grad_middle.T, grad_last


def solution(mesh):
    finer = Mesh(mesh.devices.reshape(4, 2, 4, 2, mesh.shape["mp"]), ALL)
    return jax.shard_map(
        per_device,
        mesh=finer,
        in_specs=(P(DP, None), P(DP, None), P(DP), P(None, "mp"), P("mp", None), P(None, "mp")),
        out_specs=(P(None, MP_DP), P("mp", DP), P(DP, "mp")),
        check_vma=False,
    )
```

```python
import jax
import jax.numpy as jnp
import numpy as np
from jax import lax
from jax.experimental import pallas as pl
from jax.experimental.pallas import tpu as pltpu
from jax.sharding import Mesh
from jax.sharding import PartitionSpec as P

BLOCK = 128
PARAMS = 8469504
DP = ("dp_0", "dp_1", "dp_2", "dp_3")
MP_DP = ("mp", "dp_0", "dp_1", "dp_2", "dp_3")
ALL = DP + ("mp",)
Y, ZH, X, CORE = DP
LANES = 128
ROWS, COLS = 24, 384
DEPTH = 512
VMEM = pl.BlockSpec(memory_space=pltpu.VMEM)
SMEM = pl.BlockSpec(memory_space=pltpu.SMEM)
HBM = pl.BlockSpec(memory_space=pl.ANY)
BF16, F32 = jnp.bfloat16, jnp.float32


def wide(shard):
    return shard.astype(F32)


def narrow(shard):
    return shard.astype(BF16)


def swap(shard, axis):
    return lax.ppermute(shard, axis, [(0, 1), (1, 0)])


def to_pair(shard, axis, order):
    pairs = [(i, i ^ 1) for i in range(4)] if order == 0 else [(i, 3 - i) for i in range(4)]
    return lax.ppermute(shard, axis, pairs)


def silu_slope(pre_act):
    sigmoid_of = 1.0 / (1.0 + jnp.exp(-pre_act))
    return sigmoid_of * (1.0 + pre_act * (1.0 - sigmoid_of))


def dot(left, right):
    return jnp.dot(left, right, preferred_element_type=F32)


def contract(left, right, left_dim, right_dim):
    return lax.dot_general(
        left, right, (((left_dim,), (right_dim,)), ((), ())), preferred_element_type=F32
    )


def call(body, name, in_specs, outs, scratch=(), kind=pltpu.VMEM):
    kernel = pl.pallas_call(
        body,
        out_shape=[kind(*out) for out in outs],
        in_specs=in_specs,
        out_specs=[VMEM] * len(outs),
        scratch_shapes=list(scratch),
        compiler_params=pltpu.CompilerParams(vmem_limit_bytes=24 << 20),
        cost_estimate=pl.CostEstimate(flops=1 << 34, bytes_accessed=1 << 26, transcendentals=0),
        name=name,
    )

    def run(*operands):
        return kernel(
            *(
                pltpu.with_memory_space_constraint(operand, pltpu.VMEM) if spec is VMEM else operand
                for operand, spec in zip(operands, in_specs)
            )
        )

    return run


def rows_of_core(rows_ref, core, out_ref):
    for block in range(32):
        y, x, z_hi = block // 8, block // 2 % 4, block % 2
        first = 2 * ROWS * ((2 * y + z_hi) * 4 + x)
        rows = pl.ds(pl.multiple_of(first + ROWS * core, 8), ROWS)
        out_ref[ROWS * block : ROWS * (block + 1), :] = narrow(rows_ref[rows, :])


def forward_kernel(
    belief_hbm, w_first_hbm, w_middle_hbm, pre_first_ref, act_first_ref, sent_ref,
    belief, w_first, w_middle, sems,
):
    inputs = belief.shape[0]
    cuts = [(start, min(start + DEPTH, inputs)) for start in range(0, inputs, DEPTH)]
    copies = []
    for i, (start, stop) in enumerate(cuts):
        rows = pl.ds(start, stop - start)
        copies.append(
            (
                pltpu.make_async_copy(belief_hbm.at[rows], belief.at[rows], sems.at[2 * i]),
                pltpu.make_async_copy(w_first_hbm.at[rows], w_first.at[rows], sems.at[2 * i + 1]),
            )
        )
    copies.append((pltpu.make_async_copy(w_middle_hbm, w_middle, sems.at[2 * len(cuts)]),))
    for pair in copies:
        for copy in pair:
            copy.start()
    pre_first = jnp.zeros(pre_first_ref.shape, F32)
    for (start, stop), pair in zip(cuts, copies):
        for copy in pair:
            copy.wait()
        pre_first += contract(belief[start:stop, :], w_first[start:stop, :], 0, 0)
    pre_first_ref[...] = pre_first
    act_first = narrow(pre_first / (1.0 + jnp.exp(-pre_first)))
    act_first_ref[...] = act_first
    copies[-1][0].wait()
    sent_ref[...] = narrow(dot(act_first, w_middle[...]))


def stage_kernel(
    place_ref, counts_ref, pre_first_ref, orders_ref, target_hbm, w_last_hbm,
    w_own_ref, target_own_ref, target_other_ref, first_slope_ref, onehot_ref, live_ref,
    target_ref, sems,
):
    copies = (
        pltpu.make_async_copy(target_hbm, target_ref, sems.at[0]),
        pltpu.make_async_copy(w_last_hbm, w_own_ref, sems.at[1]),
    )
    for copy in copies:
        copy.start()
    first_slope_ref[...] = silu_slope(pre_first_ref[...])
    order = jnp.where(place_ref[0] == 0, orders_ref[0], orders_ref[1])
    units = lax.broadcasted_iota(jnp.int32, onehot_ref.shape, 1)
    onehot_ref[...] = jnp.where(order == units, 1.0, 0.0).astype(BF16)
    row = lax.broadcasted_iota(jnp.int32, live_ref.shape, 1)
    count = jnp.where(row < BLOCK, counts_ref[0], counts_ref[1] + BLOCK)
    live_ref[...] = jnp.where(row < count, 1.0, 0.0)
    copies[0].wait()
    width = target_own_ref.shape[0]
    low, high = target_ref[0:width, :], target_ref[width : 2 * width, :]
    is_low = place_ref[4] == 0
    target_own_ref[...] = jnp.where(is_low, low, high)
    target_other_ref[...] = jnp.where(is_low, high, low)
    copies[1].wait()


def hidden_kernel(
    place_ref, partial_ref, arrived_ref, live_ref, target_ref, w_ref,
    act_ref, act_slope_ref, back_ref, sent_ref, own_ref, rows_ref,
):
    core = place_ref[0]
    pre_middle = wide(partial_ref[...]) + wide(arrived_ref[...])
    sigmoid_of = 1.0 / (1.0 + jnp.exp(-pre_middle))
    act = narrow(pre_middle * sigmoid_of)
    act_ref[...] = act
    act_slope_ref[...] = sigmoid_of * (1.0 + pre_middle * (1.0 - sigmoid_of))
    slope = slope_of(w_ref[...], act, target_ref[...], live_ref[...])
    half = own_ref.shape[0]
    sent_ref[half:, :] = slope
    back_ref[...] = contract(slope, w_ref[...], 0, 0)
    rows_ref[...] = wide(act).T
    rows_of_core(rows_ref, 1 - core, sent_ref)
    rows_of_core(rows_ref, core, own_ref)


def slope_of(weights, act, target, live):
    mismatch = contract(weights, act, 1, 1) - wide(target)
    return narrow(jnp.clip(mismatch, -1.0, 1.0) * live)


def slopes_kernel(
    place_ref, act_ref, act_slope_ref, back_ref, live_ref, target_ref, first_slope_ref,
    onehot_ref, fetched_ref, relayed_ref, w_middle_ref, sent_ref, own_ref, rows_ref,
):
    core = place_ref[0]
    w_other = jnp.where(core == 0, fetched_ref[...], relayed_ref[...])
    slope = slope_of(w_other, act_ref[...], target_ref[...], live_ref[...])
    back = back_ref[...] + contract(slope, w_other, 0, 0)
    slope_middle = narrow(back * act_slope_ref[...])
    slope_first = narrow(contract(slope_middle, w_middle_ref[...], 1, 1) * first_slope_ref[...])
    slope_first = narrow(contract(onehot_ref[...], slope_first, 1, 1))
    half = slope_first.shape[0] // 2
    sent_ref[2 * half :, :] = slope_first[:half]
    own_ref[2 * half :, :] = slope_first[half:]
    rows_ref[...] = wide(slope_middle).T
    rows_of_core(rows_ref, 1 - core, sent_ref)
    rows_of_core(rows_ref, core, own_ref)


def column_cuts(width):
    return [(start, min(start + COLS, width)) for start in range(0, width, COLS)]


def put_columns(raw, granule, out_ref):
    width = raw.shape[1]
    if width < COLS:
        raw = jnp.concatenate([raw, jnp.zeros((raw.shape[0], COLS - width), raw.dtype)], 1)
    for unit in range(16):
        out_ref[unit, granule] = raw[unit * ROWS : (unit + 1) * ROWS]


def kept_and_sent(me, order):
    near, far, opposite = lax.bitwise_xor(me, 1), 3 - me, lax.bitwise_xor(me, 2)
    return ((me, far), (near, opposite)) if order == 0 else ((me, near), (far, opposite))


def cut_rows(raw_ref, me, order, kept_ref, sent_ref):
    for out_ref, blocks in zip((kept_ref, sent_ref), kept_and_sent(me, order)):
        for position, x in enumerate(blocks):
            for y in range(4):
                for granule in range(4):
                    first = ROWS * (2 * (4 * y + x) + granule // 2)
                    columns = slice(granule % 2 * COLS, (granule % 2 + 1) * COLS)
                    rows = raw_ref[pl.ds(pl.multiple_of(first, 8), ROWS), columns]
                    out_ref[position, y, granule] = rows.astype(out_ref.dtype)


def last_kernel(place_ref, own_ref, sent_ref, arrived_ref, kept_out, sent_out, raw_ref, padded_ref):
    half = own_ref.shape[0]
    width = sent_ref.shape[0] - half
    padded_ref[...] = jnp.zeros_like(padded_ref)
    padded_ref[0, 0:width, :] = sent_ref[half:, :]
    padded_ref[1, 0:width, :] = arrived_ref[half:, :]
    raw_ref[...] = contract(own_ref[...], padded_ref[0], 1, 1) + contract(
        arrived_ref[0:half, :], padded_ref[1], 1, 1
    )
    cut_rows(raw_ref, place_ref[2], 0, kept_out, sent_out)


def middle_kernel(
    place_ref, own_ref, arrived_ref, act_ref, sibling_act_ref, kept_out, sent_out, raw_ref
):
    half = raw_ref.shape[0]
    raw_ref[...] = dot(own_ref[0:half, :], act_ref[...]) + dot(
        arrived_ref[0:half, :], sibling_act_ref[...]
    )
    cut_rows(raw_ref, place_ref[2], 1, kept_out, sent_out)


def first_kernel(place_ref, own_ref, arrived_ref, belief_ref, sibling_belief_ref, *refs):
    raw_ref = refs[-1]
    start_row = own_ref.shape[0] // 3 * 2
    own, arrived = own_ref[start_row:, :], arrived_ref[start_row:, :]
    for start, stop in column_cuts(belief_ref.shape[0]):
        raw = contract(own, belief_ref[start:stop, :], 1, 1) + contract(
            arrived, sibling_belief_ref[start:stop, :], 1, 1
        )
        put_columns(raw, start // COLS, raw_ref)
    for order, part in enumerate((slice(0, 4), slice(4, 7))):
        for side, blocks in enumerate(kept_and_sent(place_ref[1], order)):
            out_ref = refs[2 * order + side]
            for position, y in enumerate(blocks):
                for x in range(4):
                    out_ref[position, x] = raw_ref[4 * y + x, part].astype(out_ref.dtype)


def halve_kernel(*refs):
    for part in range(4):
        kept_ref, arrived_ref = refs[2 * part : 2 * part + 2]
        kept_out, sent_out = refs[8 + 2 * part : 10 + 2 * part]
        kept_out[...] = kept_ref[0] + wide(arrived_ref[0])
        sent_out[...] = narrow(kept_ref[1] + wide(arrived_ref[1]))


def turn_kernel(place_ref, *refs):
    scratch = refs[16:]
    for part in range(4):
        kept_ref, arrived_ref = refs[2 * part : 2 * part + 2]
        scratch[part][...] = kept_ref[...] + wide(arrived_ref[...])
        for side, blocks in enumerate(kept_and_sent(place_ref[2 if part < 2 else 1], part % 2)):
            out_ref = refs[8 + 2 * part + side]
            for position, block in enumerate(blocks):
                out_ref[position] = scratch[part][block].astype(out_ref.dtype)


def z_cut_kernel(place_ref, *refs):
    sent_ref, own_ref, last_sum, middle_sum = refs[8:12]
    z_hi = place_ref[3]
    low, high, last, middle = (
        refs[2 * part][...] + wide(refs[2 * part + 1][...]) for part in range(4)
    )
    last_sum[...] = last
    middle_sum[...] = middle
    rows = [low[granule] for granule in range(4)] + [high[granule] for granule in range(3)]
    for side, out_ref in ((1 - z_hi, sent_ref), (z_hi, own_ref)):
        kind = out_ref.dtype
        out_ref[0:2] = last_sum[pl.ds(2 * side, 2)].astype(kind)
        out_ref[2:4] = middle_sum[pl.ds(2 * side, 2)].astype(kind)
        halves = [jnp.where(side == 0, row[0:12], row[12:24]) for row in rows]
        halves.append(jnp.zeros_like(halves[0]))
        for pair in range(4):
            out_ref[4 + pair] = jnp.concatenate(halves[2 * pair : 2 * pair + 2], 0).astype(kind)


def square_kernel(own_ref, arrived_ref, total_ref, squares_ref):
    total = own_ref[...] + wide(arrived_ref[...])
    total_ref[...] = total
    squares_ref[...] = jnp.broadcast_to(jnp.sum(total * total), squares_ref.shape)


def scale_kernel(total_ref, squares_ref, first_ref, middle_ref, last_ref):
    square_sum = jnp.sum(squares_ref[...], axis=0)
    norm_scale = lax.rsqrt(square_sum / PARAMS + 1e-06)
    norm_scale = jnp.concatenate([norm_scale] * 3, 1)
    for ref, start in ((last_ref, 0), (middle_ref, 2)):
        for half in range(2):
            columns = slice(half * COLS, min((half + 1) * COLS, ref.shape[1]))
            width = columns.stop - columns.start
            ref[:, columns] = (total_ref[start + half] * norm_scale)[:, :width]
    for granule, (start, stop) in enumerate(column_cuts(first_ref.shape[1])):
        row = granule % 2 * 12
        scaled = total_ref[4 + granule // 2, row : row + 12] * norm_scale
        first_ref[:, start:stop] = scaled[:, : stop - start]


def granules(*lead, kind=BF16):
    return ((*lead, ROWS, COLS), kind)


def per_device(belief, target_value, counts, w_first, w_middle, w_last):
    total_rows, inputs = belief.shape
    width = w_last.shape[1]
    units = w_first.shape[1]
    hidden = w_middle.shape[1]
    belief_t, w_last_t = belief.T, w_last.T

    around = (ZH, CORE, "mp")
    fetched = lax.ppermute(w_last_t, around, [(0, 5), (5, 0), (1, 4), (4, 1)])

    indices = (CORE, Y, X, ZH, "mp")
    place = jnp.stack([lax.axis_index(axis) for axis in indices])
    pre_first, act_first, hidden_sent = call(
        forward_kernel,
        "forward",
        [HBM] * 3,
        [
            ((total_rows, units), F32),
            ((total_rows, units), BF16),
            ((total_rows, hidden), BF16),
        ],
        [
            pltpu.VMEM((inputs, total_rows), BF16),
            pltpu.VMEM((inputs, units), BF16),
            pltpu.VMEM((units, hidden), BF16),
            pltpu.SemaphoreType.DMA((2 * pl.cdiv(inputs, DEPTH) + 1,)),
        ],
        kind=pltpu.HBM,
    )(belief_t, w_first, w_middle)
    arrived = swap(hidden_sent, "mp")
    belief_swapped, act_first = lax.optimization_barrier((belief_t, act_first))
    sibling_belief = swap(belief_swapped, CORE)
    sibling_act = swap(act_first, CORE)

    order = np.arange(units, dtype=np.int32).reshape(4, 2, 4, 2, -1).transpose(3, 0, 2, 1, 4)
    orders = np.stack([order[::-1], order]).reshape(2, units, 1)
    w_own, target_own, target_other, first_slope, onehot, live = call(
        stage_kernel,
        "stage",
        [SMEM, SMEM, VMEM, VMEM, HBM, HBM],
        [
            ((width, hidden), BF16),
            ((width, total_rows), BF16),
            ((width, total_rows), BF16),
            ((total_rows, units), F32),
            ((units, units), BF16),
            ((1, total_rows), F32),
        ],
        [pltpu.VMEM((2 * width, total_rows), BF16), pltpu.SemaphoreType.DMA((2,))],
    )(place, counts, pre_first, jnp.asarray(orders), target_value.T, w_last_t)
    fetched, live = lax.optimization_barrier((fetched, live))
    relayed = lax.ppermute(fetched, CORE, [(0, 1)])

    act, act_slope, back_own, last_sent, last_own = call(
        hidden_kernel,
        "hidden",
        [SMEM] + [VMEM] * 5,
        [
            ((total_rows, hidden), BF16),
            ((total_rows, hidden), F32),
            ((total_rows, hidden), F32),
            ((hidden // 2 + width, total_rows), BF16),
            ((hidden // 2, total_rows), BF16),
        ],
        [pltpu.VMEM((hidden, total_rows), F32)],
    )(place, hidden_sent, arrived, live, target_own, w_own)
    last_arrived = swap(last_sent, CORE)

    slopes_sent, slopes_own = call(
        slopes_kernel,
        "slopes",
        [SMEM] + [VMEM] * 10,
        [((hidden // 2 + units // 2, total_rows), BF16)] * 2,
        [pltpu.VMEM((hidden, total_rows), F32)],
    )(
        place, act, act_slope, back_own, live, target_other, first_slope, onehot,
        fetched, relayed, w_middle,
    )
    slopes_arrived = swap(slopes_sent, CORE)

    def pairs(*sizes):
        return [out for size in sizes for out in (granules(*size, kind=F32), granules(*size))]

    def exchange(parts, axes, orders):
        return [
            part if side == 0 else to_pair(part, axes[i], orders[i])
            for i in range(len(parts) // 2)
            for side, part in enumerate(parts[2 * i : 2 * i + 2])
        ]

    raw = pltpu.VMEM((hidden // 2, units), F32)
    last_parts = call(
        last_kernel,
        "last",
        [SMEM] + [VMEM] * 3,
        pairs((2, 4, 4)),
        [raw, pltpu.VMEM((2, units, total_rows), BF16)],
    )(place, last_own, last_sent, last_arrived)
    first_parts = call(
        first_kernel,
        "first",
        [SMEM] + [VMEM] * 4,
        pairs((2, 4, 4), (2, 4, 3)),
        [pltpu.VMEM((16, 7, ROWS, COLS), F32)],
    )(place, slopes_own, slopes_arrived, belief_t, sibling_belief)
    middle_parts = call(
        middle_kernel, "middle", [SMEM] + [VMEM] * 4, pairs((2, 4, 4)), [raw]
    )(place, slopes_own, slopes_arrived, act_first, sibling_act)
    parts = exchange([*first_parts, *last_parts, *middle_parts], (Y, Y, X, X), (0, 1, 0, 1))
    sizes = (4, 3, 4, 4)
    parts = exchange(
        call(halve_kernel, "halve", [VMEM] * 8, pairs(*((4, size) for size in sizes)))(*parts),
        (Y, Y, X, X),
        (1, 0, 1, 0),
    )
    parts = exchange(
        call(
            turn_kernel,
            "turn",
            [SMEM] + [VMEM] * 8,
            pairs(*((2, size) for size in sizes)),
            [pltpu.VMEM((4, size, ROWS, COLS), F32) for size in sizes],
        )(place, *parts),
        (X, X, Y, Y),
        (0, 1, 0, 1),
    )
    parts = exchange(
        call(halve_kernel, "halve", [VMEM] * 8, pairs(*((size,) for size in sizes)))(*parts),
        (X, X, Y, Y),
        (1, 0, 1, 0),
    )
    sent, own = call(
        z_cut_kernel,
        "z_cut",
        [SMEM] + [VMEM] * 8,
        [granules(8), granules(8, kind=F32)],
        [pltpu.VMEM((4, ROWS, COLS), F32)] * 2,
    )(place, *parts)

    total, squares = call(
        square_kernel, "square", [VMEM] * 2, [((8, ROWS, COLS), F32), ((128, 1, LANES), F32)]
    )(own, swap(sent, ZH))
    squares = lax.all_to_all(squares, ALL, 0, 0, tiled=True)
    grad_first, grad_middle, grad_last = call(
        scale_kernel,
        "scale",
        [VMEM] * 2,
        [((units // 64, inputs), F32), ((ROWS, units), F32), ((ROWS, width), F32)],
        kind=jax.ShapeDtypeStruct,
    )(total, squares)
    return grad_first.T, grad_middle.T, grad_last


def solution(mesh):
    finer = Mesh(mesh.devices.reshape(4, 2, 4, 2, mesh.shape["mp"]), ALL)
    return jax.shard_map(
        per_device,
        mesh=finer,
        in_specs=(P(DP, None), P(DP, None), P(DP), P(None, "mp"), P("mp", None), P(None, "mp")),
        out_specs=(P(None, MP_DP), P("mp", DP), P(DP, "mp")),
        check_vma=False,
    )
```

```python
import jax
import jax.numpy as jnp
import numpy as np
from jax import lax
from jax.experimental import pallas as pl
from jax.experimental.pallas import tpu as pltpu
from jax.sharding import Mesh
from jax.sharding import PartitionSpec as P

BLOCK = 128
PARAMS = 8469504
DP = ("dp_0", "dp_1", "dp_2", "dp_3")
MP_DP = ("mp", "dp_0", "dp_1", "dp_2", "dp_3")
ALL = DP + ("mp",)
Y, ZH, X, CORE = DP
LANES = 128
ROWS, COLS = 24, 384
DEPTH = 512
VMEM = pl.BlockSpec(memory_space=pltpu.VMEM)
SMEM = pl.BlockSpec(memory_space=pltpu.SMEM)
HBM = pl.BlockSpec(memory_space=pl.ANY)
BF16, F32 = jnp.bfloat16, jnp.float32


def wide(shard):
    return shard.astype(F32)


def narrow(shard):
    return shard.astype(BF16)


def swap(shard, axis):
    return lax.ppermute(shard, axis, [(0, 1), (1, 0)])


def to_pair(shard, axis, order):
    pairs = [(i, i ^ 1) for i in range(4)] if order == 0 else [(i, 3 - i) for i in range(4)]
    return lax.ppermute(shard, axis, pairs)


def silu_slope(pre_act):
    sigmoid_of = 1.0 / (1.0 + jnp.exp(-pre_act))
    return sigmoid_of * (1.0 + pre_act * (1.0 - sigmoid_of))


def dot(left, right):
    return jnp.dot(left, right, preferred_element_type=F32)


def contract(left, right, left_dim, right_dim):
    return lax.dot_general(
        left, right, (((left_dim,), (right_dim,)), ((), ())), preferred_element_type=F32
    )


def call(body, name, in_specs, outs, scratch=(), kind=pltpu.VMEM):
    kernel = pl.pallas_call(
        body,
        out_shape=[kind(*out) for out in outs],
        in_specs=in_specs,
        out_specs=[VMEM] * len(outs),
        scratch_shapes=list(scratch),
        compiler_params=pltpu.CompilerParams(vmem_limit_bytes=24 << 20),
        cost_estimate=pl.CostEstimate(flops=1 << 34, bytes_accessed=1 << 26, transcendentals=0),
        name=name,
    )

    def run(*operands):
        return kernel(
            *(
                operand if spec is SMEM else pltpu.with_memory_space_constraint(
                    operand, pltpu.VMEM if spec is VMEM else pltpu.HBM
                )
                for operand, spec in zip(operands, in_specs)
            )
        )

    return run


def rows_of_core(rows_ref, core, out_ref):
    for block in range(32):
        y, x, z_hi = block // 8, block // 2 % 4, block % 2
        first = 2 * ROWS * ((2 * y + z_hi) * 4 + x)
        rows = pl.ds(pl.multiple_of(first + ROWS * core, 8), ROWS)
        out_ref[ROWS * block : ROWS * (block + 1), :] = narrow(rows_ref[rows, :])


def forward_kernel(
    belief_hbm, w_first_hbm, w_middle_hbm, pre_first_ref, act_first_ref, sent_ref,
    belief, w_first, w_middle, sems,
):
    inputs = belief.shape[0]
    cuts = [(start, min(start + DEPTH, inputs)) for start in range(0, inputs, DEPTH)]
    copies = []
    for i, (start, stop) in enumerate(cuts):
        rows = pl.ds(start, stop - start)
        copies.append(
            (
                pltpu.make_async_copy(belief_hbm.at[rows], belief.at[rows], sems.at[2 * i]),
                pltpu.make_async_copy(w_first_hbm.at[rows], w_first.at[rows], sems.at[2 * i + 1]),
            )
        )
    copies.append((pltpu.make_async_copy(w_middle_hbm, w_middle, sems.at[2 * len(cuts)]),))
    for pair in copies:
        for copy in pair:
            copy.start()
    pre_first = jnp.zeros(pre_first_ref.shape, F32)
    for (start, stop), pair in zip(cuts, copies):
        for copy in pair:
            copy.wait()
        pre_first += contract(belief[start:stop, :], w_first[start:stop, :], 0, 0)
    pre_first_ref[...] = pre_first
    act_first = narrow(pre_first / (1.0 + jnp.exp(-pre_first)))
    act_first_ref[...] = act_first
    copies[-1][0].wait()
    sent_ref[...] = narrow(dot(act_first, w_middle[...]))


def stage_kernel(
    place_ref, counts_ref, pre_first_ref, orders_ref, target_hbm, w_last_hbm,
    w_own_ref, target_own_ref, target_other_ref, first_slope_ref, onehot_ref, live_ref,
    target_ref, sems,
):
    copies = (
        pltpu.make_async_copy(target_hbm, target_ref, sems.at[0]),
        pltpu.make_async_copy(w_last_hbm, w_own_ref, sems.at[1]),
    )
    for copy in copies:
        copy.start()
    first_slope_ref[...] = silu_slope(pre_first_ref[...])
    order = jnp.where(place_ref[0] == 0, orders_ref[0], orders_ref[1])
    units = lax.broadcasted_iota(jnp.int32, onehot_ref.shape, 1)
    onehot_ref[...] = jnp.where(order == units, 1.0, 0.0).astype(BF16)
    row = lax.broadcasted_iota(jnp.int32, live_ref.shape, 1)
    count = jnp.where(row < BLOCK, counts_ref[0], counts_ref[1] + BLOCK)
    live_ref[...] = jnp.where(row < count, 1.0, 0.0)
    copies[0].wait()
    width = target_own_ref.shape[0]
    low, high = target_ref[0:width, :], target_ref[width : 2 * width, :]
    is_low = place_ref[4] == 0
    target_own_ref[...] = jnp.where(is_low, low, high)
    target_other_ref[...] = jnp.where(is_low, high, low)
    copies[1].wait()


def hidden_kernel(
    place_ref, partial_ref, arrived_ref, live_ref, target_ref, w_ref,
    act_ref, act_slope_ref, back_ref, sent_ref, own_ref, rows_ref,
):
    core = place_ref[0]
    pre_middle = wide(partial_ref[...]) + wide(arrived_ref[...])
    sigmoid_of = 1.0 / (1.0 + jnp.exp(-pre_middle))
    act = narrow(pre_middle * sigmoid_of)
    act_ref[...] = act
    act_slope_ref[...] = sigmoid_of * (1.0 + pre_middle * (1.0 - sigmoid_of))
    slope = slope_of(w_ref[...], act, target_ref[...], live_ref[...])
    half = own_ref.shape[0]
    sent_ref[half:, :] = slope
    back_ref[...] = contract(slope, w_ref[...], 0, 0)
    rows_ref[...] = wide(act).T
    rows_of_core(rows_ref, 1 - core, sent_ref)
    rows_of_core(rows_ref, core, own_ref)


def slope_of(weights, act, target, live):
    mismatch = contract(weights, act, 1, 1) - wide(target)
    return narrow(jnp.clip(mismatch, -1.0, 1.0) * live)


def slopes_kernel(
    place_ref, act_ref, act_slope_ref, back_ref, live_ref, target_ref, first_slope_ref,
    onehot_ref, fetched_ref, relayed_ref, w_middle_ref, sent_ref, own_ref, rows_ref,
):
    core = place_ref[0]
    w_other = jnp.where(core == 0, fetched_ref[...], relayed_ref[...])
    slope = slope_of(w_other, act_ref[...], target_ref[...], live_ref[...])
    back = back_ref[...] + contract(slope, w_other, 0, 0)
    slope_middle = narrow(back * act_slope_ref[...])
    slope_first = narrow(contract(slope_middle, w_middle_ref[...], 1, 1) * first_slope_ref[...])
    slope_first = narrow(contract(onehot_ref[...], slope_first, 1, 1))
    half = slope_first.shape[0] // 2
    sent_ref[2 * half :, :] = slope_first[:half]
    own_ref[2 * half :, :] = slope_first[half:]
    rows_ref[...] = wide(slope_middle).T
    rows_of_core(rows_ref, 1 - core, sent_ref)
    rows_of_core(rows_ref, core, own_ref)


def column_cuts(width):
    return [(start, min(start + COLS, width)) for start in range(0, width, COLS)]


def put_columns(raw, granule, out_ref):
    width = raw.shape[1]
    if width < COLS:
        raw = jnp.concatenate([raw, jnp.zeros((raw.shape[0], COLS - width), raw.dtype)], 1)
    for unit in range(16):
        out_ref[unit, granule] = raw[unit * ROWS : (unit + 1) * ROWS]


def kept_and_sent(me, order):
    near, far, opposite = lax.bitwise_xor(me, 1), 3 - me, lax.bitwise_xor(me, 2)
    return ((me, far), (near, opposite)) if order == 0 else ((me, near), (far, opposite))


def cut_rows(raw_ref, me, order, kept_ref, sent_ref):
    for out_ref, blocks in zip((kept_ref, sent_ref), kept_and_sent(me, order)):
        for position, x in enumerate(blocks):
            for y in range(4):
                for granule in range(4):
                    first = ROWS * (2 * (4 * y + x) + granule // 2)
                    columns = slice(granule % 2 * COLS, (granule % 2 + 1) * COLS)
                    rows = raw_ref[pl.ds(pl.multiple_of(first, 8), ROWS), columns]
                    out_ref[position, y, granule] = rows.astype(out_ref.dtype)


def last_kernel(place_ref, own_ref, sent_ref, arrived_ref, kept_out, sent_out, raw_ref, padded_ref):
    half = own_ref.shape[0]
    width = sent_ref.shape[0] - half
    padded_ref[...] = jnp.zeros_like(padded_ref)
    padded_ref[0, 0:width, :] = sent_ref[half:, :]
    padded_ref[1, 0:width, :] = arrived_ref[half:, :]
    raw_ref[...] = contract(own_ref[...], padded_ref[0], 1, 1) + contract(
        arrived_ref[0:half, :], padded_ref[1], 1, 1
    )
    cut_rows(raw_ref, place_ref[2], 0, kept_out, sent_out)


def middle_kernel(
    place_ref, own_ref, arrived_ref, act_ref, sibling_act_ref, kept_out, sent_out, raw_ref
):
    half = raw_ref.shape[0]
    raw_ref[...] = dot(own_ref[0:half, :], act_ref[...]) + dot(
        arrived_ref[0:half, :], sibling_act_ref[...]
    )
    cut_rows(raw_ref, place_ref[2], 1, kept_out, sent_out)


def first_kernel(place_ref, own_ref, arrived_ref, belief_ref, sibling_belief_ref, *refs):
    raw_ref = refs[-1]
    start_row = own_ref.shape[0] // 3 * 2
    own, arrived = own_ref[start_row:, :], arrived_ref[start_row:, :]
    for start, stop in column_cuts(belief_ref.shape[0]):
        raw = contract(own, belief_ref[start:stop, :], 1, 1) + contract(
            arrived, sibling_belief_ref[start:stop, :], 1, 1
        )
        put_columns(raw, start // COLS, raw_ref)
    for order, part in enumerate((slice(0, 4), slice(4, 7))):
        for side, blocks in enumerate(kept_and_sent(place_ref[1], order)):
            out_ref = refs[2 * order + side]
            for position, y in enumerate(blocks):
                for x in range(4):
                    out_ref[position, x] = raw_ref[4 * y + x, part].astype(out_ref.dtype)


def halve_kernel(*refs):
    for part in range(4):
        kept_ref, arrived_ref = refs[2 * part : 2 * part + 2]
        kept_out, sent_out = refs[8 + 2 * part : 10 + 2 * part]
        kept_out[...] = kept_ref[0] + wide(arrived_ref[0])
        sent_out[...] = narrow(kept_ref[1] + wide(arrived_ref[1]))


def turn_kernel(place_ref, *refs):
    scratch = refs[16:]
    for part in range(4):
        kept_ref, arrived_ref = refs[2 * part : 2 * part + 2]
        scratch[part][...] = kept_ref[...] + wide(arrived_ref[...])
        for side, blocks in enumerate(kept_and_sent(place_ref[2 if part < 2 else 1], part % 2)):
            out_ref = refs[8 + 2 * part + side]
            for position, block in enumerate(blocks):
                out_ref[position] = scratch[part][block].astype(out_ref.dtype)


def z_cut_kernel(place_ref, *refs):
    sent_ref, own_ref, last_sum, middle_sum = refs[8:12]
    z_hi = place_ref[3]
    low, high, last, middle = (
        refs[2 * part][...] + wide(refs[2 * part + 1][...]) for part in range(4)
    )
    last_sum[...] = last
    middle_sum[...] = middle
    rows = [low[granule] for granule in range(4)] + [high[granule] for granule in range(3)]
    for side, out_ref in ((1 - z_hi, sent_ref), (z_hi, own_ref)):
        kind = out_ref.dtype
        out_ref[0:2] = last_sum[pl.ds(2 * side, 2)].astype(kind)
        out_ref[2:4] = middle_sum[pl.ds(2 * side, 2)].astype(kind)
        halves = [jnp.where(side == 0, row[0:12], row[12:24]) for row in rows]
        halves.append(jnp.zeros_like(halves[0]))
        for pair in range(4):
            out_ref[4 + pair] = jnp.concatenate(halves[2 * pair : 2 * pair + 2], 0).astype(kind)


def square_kernel(own_ref, arrived_ref, total_ref, squares_ref):
    total = own_ref[...] + wide(arrived_ref[...])
    total_ref[...] = total
    squares_ref[...] = jnp.broadcast_to(jnp.sum(total * total), squares_ref.shape)


def scale_kernel(total_ref, squares_ref, first_ref, middle_ref, last_ref):
    square_sum = jnp.sum(squares_ref[...], axis=0)
    norm_scale = lax.rsqrt(square_sum / PARAMS + 1e-06)
    norm_scale = jnp.concatenate([norm_scale] * 3, 1)
    for ref, start in ((last_ref, 0), (middle_ref, 2)):
        for half in range(2):
            columns = slice(half * COLS, min((half + 1) * COLS, ref.shape[1]))
            width = columns.stop - columns.start
            ref[:, columns] = (total_ref[start + half] * norm_scale)[:, :width]
    for granule, (start, stop) in enumerate(column_cuts(first_ref.shape[1])):
        row = granule % 2 * 12
        scaled = total_ref[4 + granule // 2, row : row + 12] * norm_scale
        first_ref[:, start:stop] = scaled[:, : stop - start]


def granules(*lead, kind=BF16):
    return ((*lead, ROWS, COLS), kind)


def per_device(belief, target_value, counts, w_first, w_middle, w_last):
    total_rows, inputs = belief.shape
    width = w_last.shape[1]
    units = w_first.shape[1]
    hidden = w_middle.shape[1]
    belief_t, w_last_t = belief.T, w_last.T

    around = (ZH, CORE, "mp")
    fetched = lax.ppermute(w_last_t, around, [(0, 5), (5, 0), (1, 4), (4, 1)])

    indices = (CORE, Y, X, ZH, "mp")
    place = jnp.stack([lax.axis_index(axis) for axis in indices])
    pre_first, act_first, hidden_sent = call(
        forward_kernel,
        "forward",
        [HBM] * 3,
        [
            ((total_rows, units), F32),
            ((total_rows, units), BF16),
            ((total_rows, hidden), BF16),
        ],
        [
            pltpu.VMEM((inputs, total_rows), BF16),
            pltpu.VMEM((inputs, units), BF16),
            pltpu.VMEM((units, hidden), BF16),
            pltpu.SemaphoreType.DMA((2 * pl.cdiv(inputs, DEPTH) + 1,)),
        ],
        kind=pltpu.HBM,
    )(belief_t, w_first, w_middle)
    arrived = swap(hidden_sent, "mp")
    belief_swapped, act_first = lax.optimization_barrier((belief_t, act_first))
    sibling_belief = swap(belief_swapped, CORE)
    sibling_act = swap(act_first, CORE)

    order = np.arange(units, dtype=np.int32).reshape(4, 2, 4, 2, -1).transpose(3, 0, 2, 1, 4)
    orders = np.stack([order[::-1], order]).reshape(2, units, 1)
    w_own, target_own, target_other, first_slope, onehot, live = call(
        stage_kernel,
        "stage",
        [SMEM, SMEM, VMEM, VMEM, HBM, HBM],
        [
            ((width, hidden), BF16),
            ((width, total_rows), BF16),
            ((width, total_rows), BF16),
            ((total_rows, units), F32),
            ((units, units), BF16),
            ((1, total_rows), F32),
        ],
        [pltpu.VMEM((2 * width, total_rows), BF16), pltpu.SemaphoreType.DMA((2,))],
    )(place, counts, pre_first, jnp.asarray(orders), target_value.T, w_last_t)
    fetched, live, sibling_belief, sibling_act = lax.optimization_barrier(
        (fetched, live, sibling_belief, sibling_act)
    )
    relayed = lax.ppermute(fetched, CORE, [(0, 1)])

    act, act_slope, back_own, last_sent, last_own = call(
        hidden_kernel,
        "hidden",
        [SMEM] + [VMEM] * 5,
        [
            ((total_rows, hidden), BF16),
            ((total_rows, hidden), F32),
            ((total_rows, hidden), F32),
            ((hidden // 2 + width, total_rows), BF16),
            ((hidden // 2, total_rows), BF16),
        ],
        [pltpu.VMEM((hidden, total_rows), F32)],
    )(place, hidden_sent, arrived, live, target_own, w_own)
    last_arrived = swap(last_sent, CORE)

    slopes_sent, slopes_own = call(
        slopes_kernel,
        "slopes",
        [SMEM] + [VMEM] * 10,
        [((hidden // 2 + units // 2, total_rows), BF16)] * 2,
        [pltpu.VMEM((hidden, total_rows), F32)],
    )(
        place, act, act_slope, back_own, live, target_other, first_slope, onehot,
        fetched, relayed, w_middle,
    )
    slopes_arrived = swap(slopes_sent, CORE)

    def pairs(*sizes):
        return [out for size in sizes for out in (granules(*size, kind=F32), granules(*size))]

    def exchange(parts, axes, orders):
        return [
            part if side == 0 else to_pair(part, axes[i], orders[i])
            for i in range(len(parts) // 2)
            for side, part in enumerate(parts[2 * i : 2 * i + 2])
        ]

    raw = pltpu.VMEM((hidden // 2, units), F32)
    last_parts = call(
        last_kernel,
        "last",
        [SMEM] + [VMEM] * 3,
        pairs((2, 4, 4)),
        [raw, pltpu.VMEM((2, units, total_rows), BF16)],
    )(place, last_own, last_sent, last_arrived)
    first_parts = call(
        first_kernel,
        "first",
        [SMEM] + [VMEM] * 4,
        pairs((2, 4, 4), (2, 4, 3)),
        [pltpu.VMEM((16, 7, ROWS, COLS), F32)],
    )(place, slopes_own, slopes_arrived, belief_t, sibling_belief)
    middle_parts = call(
        middle_kernel, "middle", [SMEM] + [VMEM] * 4, pairs((2, 4, 4)), [raw]
    )(place, slopes_own, slopes_arrived, act_first, sibling_act)
    parts = exchange([*first_parts, *last_parts, *middle_parts], (Y, Y, X, X), (0, 1, 0, 1))
    sizes = (4, 3, 4, 4)
    parts = exchange(
        call(halve_kernel, "halve", [VMEM] * 8, pairs(*((4, size) for size in sizes)))(*parts),
        (Y, Y, X, X),
        (1, 0, 1, 0),
    )
    parts = exchange(
        call(
            turn_kernel,
            "turn",
            [SMEM] + [VMEM] * 8,
            pairs(*((2, size) for size in sizes)),
            [pltpu.VMEM((4, size, ROWS, COLS), F32) for size in sizes],
        )(place, *parts),
        (X, X, Y, Y),
        (0, 1, 0, 1),
    )
    parts = exchange(
        call(halve_kernel, "halve", [VMEM] * 8, pairs(*((size,) for size in sizes)))(*parts),
        (X, X, Y, Y),
        (1, 0, 1, 0),
    )
    sent, own = call(
        z_cut_kernel,
        "z_cut",
        [SMEM] + [VMEM] * 8,
        [granules(8), granules(8, kind=F32)],
        [pltpu.VMEM((4, ROWS, COLS), F32)] * 2,
    )(place, *parts)

    total, squares = call(
        square_kernel, "square", [VMEM] * 2, [((8, ROWS, COLS), F32), ((128, 1, LANES), F32)]
    )(own, swap(sent, ZH))
    squares = lax.all_to_all(squares, ALL, 0, 0, tiled=True)
    grad_first, grad_middle, grad_last = call(
        scale_kernel,
        "scale",
        [VMEM] * 2,
        [((units // 64, inputs), F32), ((ROWS, units), F32), ((ROWS, width), F32)],
        kind=jax.ShapeDtypeStruct,
    )(total, squares)
    return grad_first.T, grad_middle.T, grad_last


def solution(mesh):
    finer = Mesh(mesh.devices.reshape(4, 2, 4, 2, mesh.shape["mp"]), ALL)
    return jax.shard_map(
        per_device,
        mesh=finer,
        in_specs=(P(DP, None), P(DP, None), P(DP), P(None, "mp"), P("mp", None), P(None, "mp")),
        out_specs=(P(None, MP_DP), P("mp", DP), P(DP, "mp")),
        check_vma=False,
    )
```

```python
import jax
import jax.numpy as jnp
import numpy as np
from jax import lax
from jax.experimental import pallas as pl
from jax.experimental.pallas import tpu as pltpu
from jax.sharding import Mesh
from jax.sharding import PartitionSpec as P

BLOCK = 128
PARAMS = 8469504
DP = ("dp_0", "dp_1", "dp_2", "dp_3")
MP_DP = ("mp", "dp_0", "dp_1", "dp_2", "dp_3")
ALL = DP + ("mp",)
Y, ZH, X, CORE = DP
LANES = 128
ROWS, COLS = 24, 384
SIZE, SECOND = 344, 320
DEPTH = 512
VMEM = pl.BlockSpec(memory_space=pltpu.VMEM)
SMEM = pl.BlockSpec(memory_space=pltpu.SMEM)
HBM = pl.BlockSpec(memory_space=pl.ANY)
BF16, F32 = jnp.bfloat16, jnp.float32


def wide(shard):
    return shard.astype(F32)


def narrow(shard):
    return shard.astype(BF16)


def swap(shard, axis):
    return lax.ppermute(shard, axis, [(0, 1), (1, 0)])


def to_pair(shard, axis, order):
    pairs = [(i, i ^ 1) for i in range(4)] if order == 0 else [(i, 3 - i) for i in range(4)]
    return lax.ppermute(shard, axis, pairs)


def silu_slope(pre_act):
    sigmoid_of = 1.0 / (1.0 + jnp.exp(-pre_act))
    return sigmoid_of * (1.0 + pre_act * (1.0 - sigmoid_of))


def dot(left, right):
    return jnp.dot(left, right, preferred_element_type=F32)


def contract(left, right, left_dim, right_dim):
    return lax.dot_general(
        left, right, (((left_dim,), (right_dim,)), ((), ())), preferred_element_type=F32
    )


def call(body, name, in_specs, outs, scratch=(), kind=pltpu.VMEM):
    kernel = pl.pallas_call(
        body,
        out_shape=[kind(*out) for out in outs],
        in_specs=in_specs,
        out_specs=[VMEM] * len(outs),
        scratch_shapes=list(scratch),
        compiler_params=pltpu.CompilerParams(vmem_limit_bytes=24 << 20),
        cost_estimate=pl.CostEstimate(flops=1 << 34, bytes_accessed=1 << 26, transcendentals=0),
        name=name,
    )

    def run(*operands):
        return kernel(
            *(
                operand if spec is SMEM else pltpu.with_memory_space_constraint(
                    operand, pltpu.VMEM if spec is VMEM else pltpu.HBM
                )
                for operand, spec in zip(operands, in_specs)
            )
        )

    return run


def rows_of_core(rows_ref, core, out_ref):
    for block in range(32):
        y, x, z_hi = block // 8, block // 2 % 4, block % 2
        first = 2 * ROWS * ((2 * y + z_hi) * 4 + x)
        rows = pl.ds(pl.multiple_of(first + ROWS * core, 8), ROWS)
        out_ref[ROWS * block : ROWS * (block + 1), :] = narrow(rows_ref[rows, :])


def forward_kernel(
    belief_hbm, w_first_hbm, w_middle_hbm, pre_first_ref, act_first_ref, sent_ref,
    belief, w_first, w_middle, sems,
):
    inputs = belief.shape[0]
    cuts = [(start, min(start + DEPTH, inputs)) for start in range(0, inputs, DEPTH)]
    copies = []
    for i, (start, stop) in enumerate(cuts):
        rows = pl.ds(start, stop - start)
        copies.append(
            (
                pltpu.make_async_copy(belief_hbm.at[rows], belief.at[rows], sems.at[2 * i]),
                pltpu.make_async_copy(w_first_hbm.at[rows], w_first.at[rows], sems.at[2 * i + 1]),
            )
        )
    copies.append((pltpu.make_async_copy(w_middle_hbm, w_middle, sems.at[2 * len(cuts)]),))
    for pair in copies:
        for copy in pair:
            copy.start()
    pre_first = jnp.zeros(pre_first_ref.shape, F32)
    for (start, stop), pair in zip(cuts, copies):
        for copy in pair:
            copy.wait()
        pre_first += contract(belief[start:stop, :], w_first[start:stop, :], 0, 0)
    pre_first_ref[...] = pre_first
    act_first = narrow(pre_first / (1.0 + jnp.exp(-pre_first)))
    act_first_ref[...] = act_first
    copies[-1][0].wait()
    sent_ref[...] = narrow(dot(act_first, w_middle[...]))


def half_kernel(place_ref, w_last_hbm, half_ref, w_last, sem):
    copy = pltpu.make_async_copy(w_last_hbm, w_last, sem)
    copy.start()
    copy.wait()
    size, total = half_ref.shape[0], w_last.shape[0]

    @pl.when(place_ref[0] == 0)
    def _():
        half_ref[...] = w_last[0:size, :]

    @pl.when(place_ref[0] != 0)
    def _():
        half_ref[size - 8 :, :] = jnp.zeros((8, half_ref.shape[1]), half_ref.dtype)
        half_ref[0 : total - SECOND, :] = w_last[SECOND:total, :]


def stage_kernel(
    place_ref, counts_ref, pre_first_ref, orders_ref, target_hbm, w_last_hbm,
    w_own_ref, target_own_ref, target_other_ref, first_slope_ref, onehot_ref, live_ref,
    target_ref, sems,
):
    copies = (
        pltpu.make_async_copy(target_hbm, target_ref, sems.at[0]),
        pltpu.make_async_copy(w_last_hbm, w_own_ref, sems.at[1]),
    )
    for copy in copies:
        copy.start()
    first_slope_ref[...] = silu_slope(pre_first_ref[...])
    order = jnp.where(place_ref[0] == 0, orders_ref[0], orders_ref[1])
    units = lax.broadcasted_iota(jnp.int32, onehot_ref.shape, 1)
    onehot_ref[...] = jnp.where(order == units, 1.0, 0.0).astype(BF16)
    row = lax.broadcasted_iota(jnp.int32, live_ref.shape, 1)
    count = jnp.where(row < BLOCK, counts_ref[0], counts_ref[1] + BLOCK)
    live_ref[...] = jnp.where(row < count, 1.0, 0.0)
    copies[0].wait()
    width = target_own_ref.shape[0]
    low, high = target_ref[0:width, :], target_ref[width : 2 * width, :]
    is_low = place_ref[4] == 0
    target_own_ref[...] = jnp.where(is_low, low, high)
    target_other_ref[...] = jnp.where(is_low, high, low)
    copies[1].wait()


def hidden_kernel(
    place_ref, partial_ref, arrived_ref, live_ref, target_ref, w_ref,
    act_ref, act_slope_ref, back_ref, sent_ref, own_ref, rows_ref,
):
    core = place_ref[0]
    pre_middle = wide(partial_ref[...]) + wide(arrived_ref[...])
    sigmoid_of = 1.0 / (1.0 + jnp.exp(-pre_middle))
    act = narrow(pre_middle * sigmoid_of)
    act_ref[...] = act
    act_slope_ref[...] = sigmoid_of * (1.0 + pre_middle * (1.0 - sigmoid_of))
    slope = slope_of(w_ref[...], act, target_ref[...], live_ref[...])
    half = own_ref.shape[0]
    sent_ref[half:, :] = slope
    back_ref[...] = contract(slope, w_ref[...], 0, 0)
    rows_ref[...] = wide(act).T
    rows_of_core(rows_ref, 1 - core, sent_ref)
    rows_of_core(rows_ref, core, own_ref)


def slope_of(weights, act, target, live):
    mismatch = contract(weights, act, 1, 1) - wide(target)
    return narrow(jnp.clip(mismatch, -1.0, 1.0) * live)


def slopes_kernel(
    place_ref, act_ref, act_slope_ref, back_ref, live_ref, target_ref, first_slope_ref,
    onehot_ref, fetched_ref, relayed_ref, w_middle_ref, sent_ref, own_ref, rows_ref,
):
    core = place_ref[0]
    size, total = fetched_ref.shape[0], target_ref.shape[0]
    act, live = act_ref[...], live_ref[...]
    back = back_ref[...]
    for is_own, start, stop in ((core == 0, 0, size), (core != 0, SECOND, total)):
        rows = slice(0, stop - start)
        weights = jnp.where(is_own, fetched_ref[rows, :], relayed_ref[rows, :])
        slope = slope_of(weights, act, target_ref[start:stop, :], live)
        if start:
            column = lax.broadcasted_iota(jnp.int32, slope.shape, 0) + start
            slope = jnp.where(column >= size, slope, jnp.zeros_like(slope))
        back += contract(slope, weights, 0, 0)
    slope_middle = narrow(back * act_slope_ref[...])
    slope_first = narrow(contract(slope_middle, w_middle_ref[...], 1, 1) * first_slope_ref[...])
    slope_first = narrow(contract(onehot_ref[...], slope_first, 1, 1))
    half = slope_first.shape[0] // 2
    sent_ref[2 * half :, :] = slope_first[:half]
    own_ref[2 * half :, :] = slope_first[half:]
    rows_ref[...] = wide(slope_middle).T
    rows_of_core(rows_ref, 1 - core, sent_ref)
    rows_of_core(rows_ref, core, own_ref)


def column_cuts(width):
    return [(start, min(start + COLS, width)) for start in range(0, width, COLS)]


def put_columns(raw, granule, out_ref):
    width = raw.shape[1]
    if width < COLS:
        raw = jnp.concatenate([raw, jnp.zeros((raw.shape[0], COLS - width), raw.dtype)], 1)
    for unit in range(16):
        out_ref[unit, granule] = raw[unit * ROWS : (unit + 1) * ROWS]


def kept_and_sent(me, order):
    near, far, opposite = lax.bitwise_xor(me, 1), 3 - me, lax.bitwise_xor(me, 2)
    return ((me, far), (near, opposite)) if order == 0 else ((me, near), (far, opposite))


def cut_rows(raw_ref, me, order, kept_ref, sent_ref):
    for out_ref, blocks in zip((kept_ref, sent_ref), kept_and_sent(me, order)):
        for position, x in enumerate(blocks):
            for y in range(4):
                for granule in range(4):
                    first = ROWS * (2 * (4 * y + x) + granule // 2)
                    columns = slice(granule % 2 * COLS, (granule % 2 + 1) * COLS)
                    rows = raw_ref[pl.ds(pl.multiple_of(first, 8), ROWS), columns]
                    out_ref[position, y, granule] = rows.astype(out_ref.dtype)


def last_kernel(place_ref, own_ref, sent_ref, arrived_ref, kept_out, sent_out, raw_ref, padded_ref):
    half = own_ref.shape[0]
    width = sent_ref.shape[0] - half
    padded_ref[...] = jnp.zeros_like(padded_ref)
    padded_ref[0, 0:width, :] = sent_ref[half:, :]
    padded_ref[1, 0:width, :] = arrived_ref[half:, :]
    raw_ref[...] = contract(own_ref[...], padded_ref[0], 1, 1) + contract(
        arrived_ref[0:half, :], padded_ref[1], 1, 1
    )
    cut_rows(raw_ref, place_ref[2], 0, kept_out, sent_out)


def middle_kernel(
    place_ref, own_ref, arrived_ref, act_ref, sibling_act_ref, kept_out, sent_out, raw_ref
):
    half = raw_ref.shape[0]
    raw_ref[...] = dot(own_ref[0:half, :], act_ref[...]) + dot(
        arrived_ref[0:half, :], sibling_act_ref[...]
    )
    cut_rows(raw_ref, place_ref[2], 1, kept_out, sent_out)


def first_kernel(place_ref, own_ref, arrived_ref, belief_ref, sibling_belief_ref, *refs):
    raw_ref = refs[-1]
    start_row = own_ref.shape[0] // 3 * 2
    own, arrived = own_ref[start_row:, :], arrived_ref[start_row:, :]
    for start, stop in column_cuts(belief_ref.shape[0]):
        raw = contract(own, belief_ref[start:stop, :], 1, 1) + contract(
            arrived, sibling_belief_ref[start:stop, :], 1, 1
        )
        put_columns(raw, start // COLS, raw_ref)
    for order, part in enumerate((slice(0, 4), slice(4, 7))):
        for side, blocks in enumerate(kept_and_sent(place_ref[1], order)):
            out_ref = refs[2 * order + side]
            for position, y in enumerate(blocks):
                for x in range(4):
                    out_ref[position, x] = raw_ref[4 * y + x, part].astype(out_ref.dtype)


def halve_kernel(*refs):
    for part in range(4):
        kept_ref, arrived_ref = refs[2 * part : 2 * part + 2]
        kept_out, sent_out = refs[8 + 2 * part : 10 + 2 * part]
        kept_out[...] = kept_ref[0] + wide(arrived_ref[0])
        sent_out[...] = narrow(kept_ref[1] + wide(arrived_ref[1]))


def turn_kernel(place_ref, *refs):
    scratch = refs[16:]
    for part in range(4):
        kept_ref, arrived_ref = refs[2 * part : 2 * part + 2]
        scratch[part][...] = kept_ref[...] + wide(arrived_ref[...])
        for side, blocks in enumerate(kept_and_sent(place_ref[2 if part < 2 else 1], part % 2)):
            out_ref = refs[8 + 2 * part + side]
            for position, block in enumerate(blocks):
                out_ref[position] = scratch[part][block].astype(out_ref.dtype)


def z_cut_kernel(place_ref, *refs):
    sent_ref, own_ref, last_sum, middle_sum = refs[8:12]
    z_hi = place_ref[3]
    low, high, last, middle = (
        refs[2 * part][...] + wide(refs[2 * part + 1][...]) for part in range(4)
    )
    last_sum[...] = last
    middle_sum[...] = middle
    rows = [low[granule] for granule in range(4)] + [high[granule] for granule in range(3)]
    for side, out_ref in ((1 - z_hi, sent_ref), (z_hi, own_ref)):
        kind = out_ref.dtype
        out_ref[0:2] = last_sum[pl.ds(2 * side, 2)].astype(kind)
        out_ref[2:4] = middle_sum[pl.ds(2 * side, 2)].astype(kind)
        halves = [jnp.where(side == 0, row[0:12], row[12:24]) for row in rows]
        halves.append(jnp.zeros_like(halves[0]))
        for pair in range(4):
            out_ref[4 + pair] = jnp.concatenate(halves[2 * pair : 2 * pair + 2], 0).astype(kind)


def square_kernel(own_ref, arrived_ref, total_ref, squares_ref):
    total = own_ref[...] + wide(arrived_ref[...])
    total_ref[...] = total
    squares_ref[...] = jnp.broadcast_to(jnp.sum(total * total), squares_ref.shape)


def scale_kernel(total_ref, squares_ref, first_ref, middle_ref, last_ref):
    square_sum = jnp.sum(squares_ref[...], axis=0)
    norm_scale = lax.rsqrt(square_sum / PARAMS + 1e-06)
    norm_scale = jnp.concatenate([norm_scale] * 3, 1)
    for ref, start in ((last_ref, 0), (middle_ref, 2)):
        for half in range(2):
            columns = slice(half * COLS, min((half + 1) * COLS, ref.shape[1]))
            width = columns.stop - columns.start
            ref[:, columns] = (total_ref[start + half] * norm_scale)[:, :width]
    for granule, (start, stop) in enumerate(column_cuts(first_ref.shape[1])):
        row = granule % 2 * 12
        scaled = total_ref[4 + granule // 2, row : row + 12] * norm_scale
        first_ref[:, start:stop] = scaled[:, : stop - start]


def granules(*lead, kind=BF16):
    return ((*lead, ROWS, COLS), kind)


def per_device(belief, target_value, counts, w_first, w_middle, w_last):
    total_rows, inputs = belief.shape
    width = w_last.shape[1]
    units = w_first.shape[1]
    hidden = w_middle.shape[1]
    belief_t, w_last_t = belief.T, w_last.T

    indices = (CORE, Y, X, ZH, "mp")
    place = jnp.stack([lax.axis_index(axis) for axis in indices])

    (half,) = call(
        half_kernel,
        "half",
        [SMEM, HBM],
        [((SIZE, hidden), BF16)],
        [pltpu.VMEM(w_last_t.shape, BF16), pltpu.SemaphoreType.DMA],
    )(place, w_last_t)
    fetched = lax.ppermute(half, (ZH, "mp"), [(0, 3), (3, 0), (1, 2), (2, 1)])
    belief_first, half = lax.optimization_barrier((belief_t, half))

    pre_first, act_first, hidden_sent = call(
        forward_kernel,
        "forward",
        [HBM] * 3,
        [
            ((total_rows, units), F32),
            ((total_rows, units), BF16),
            ((total_rows, hidden), BF16),
        ],
        [
            pltpu.VMEM((inputs, total_rows), BF16),
            pltpu.VMEM((inputs, units), BF16),
            pltpu.VMEM((units, hidden), BF16),
            pltpu.SemaphoreType.DMA((2 * pl.cdiv(inputs, DEPTH) + 1,)),
        ],
        kind=pltpu.HBM,
    )(belief_first, w_first, w_middle)
    arrived = swap(hidden_sent, "mp")

    order = np.arange(units, dtype=np.int32).reshape(4, 2, 4, 2, -1).transpose(3, 0, 2, 1, 4)
    orders = np.stack([order[::-1], order]).reshape(2, units, 1)
    w_own, target_own, target_other, first_slope, onehot, live = call(
        stage_kernel,
        "stage",
        [SMEM, SMEM, VMEM, VMEM, HBM, HBM],
        [
            ((width, hidden), BF16),
            ((width, total_rows), BF16),
            ((width, total_rows), BF16),
            ((total_rows, units), F32),
            ((units, units), BF16),
            ((1, total_rows), F32),
        ],
        [pltpu.VMEM((2 * width, total_rows), BF16), pltpu.SemaphoreType.DMA((2,))],
    )(place, counts, pre_first, jnp.asarray(orders), target_value.T, w_last_t)
    fetched, live = lax.optimization_barrier((fetched, live))
    relayed = swap(fetched, CORE)
    belief_swapped, act_swapped = lax.optimization_barrier((belief_t, act_first))
    sibling_belief = swap(belief_swapped, CORE)
    sibling_act = swap(act_swapped, CORE)

    act, act_slope, back_own, last_sent, last_own = call(
        hidden_kernel,
        "hidden",
        [SMEM] + [VMEM] * 5,
        [
            ((total_rows, hidden), BF16),
            ((total_rows, hidden), F32),
            ((total_rows, hidden), F32),
            ((hidden // 2 + width, total_rows), BF16),
            ((hidden // 2, total_rows), BF16),
        ],
        [pltpu.VMEM((hidden, total_rows), F32)],
    )(place, hidden_sent, arrived, live, target_own, w_own)
    last_arrived = swap(last_sent, CORE)

    slopes_sent, slopes_own = call(
        slopes_kernel,
        "slopes",
        [SMEM] + [VMEM] * 10,
        [((hidden // 2 + units // 2, total_rows), BF16)] * 2,
        [pltpu.VMEM((hidden, total_rows), F32)],
    )(
        place, act, act_slope, back_own, live, target_other, first_slope, onehot,
        fetched, relayed, w_middle,
    )
    slopes_arrived = swap(slopes_sent, CORE)

    def pairs(*sizes):
        return [out for size in sizes for out in (granules(*size, kind=F32), granules(*size))]

    def exchange(parts, axes, orders):
        return [
            part if side == 0 else to_pair(part, axes[i], orders[i])
            for i in range(len(parts) // 2)
            for side, part in enumerate(parts[2 * i : 2 * i + 2])
        ]

    raw = pltpu.VMEM((hidden // 2, units), F32)
    last_parts = call(
        last_kernel,
        "last",
        [SMEM] + [VMEM] * 3,
        pairs((2, 4, 4)),
        [raw, pltpu.VMEM((2, units, total_rows), BF16)],
    )(place, last_own, last_sent, last_arrived)
    first_parts = call(
        first_kernel,
        "first",
        [SMEM] + [VMEM] * 4,
        pairs((2, 4, 4), (2, 4, 3)),
        [pltpu.VMEM((16, 7, ROWS, COLS), F32)],
    )(place, slopes_own, slopes_arrived, belief_t, sibling_belief)
    middle_parts = call(
        middle_kernel, "middle", [SMEM] + [VMEM] * 4, pairs((2, 4, 4)), [raw]
    )(place, slopes_own, slopes_arrived, act_first, sibling_act)
    parts = exchange([*first_parts, *last_parts, *middle_parts], (Y, Y, X, X), (0, 1, 0, 1))
    sizes = (4, 3, 4, 4)
    parts = exchange(
        call(halve_kernel, "halve", [VMEM] * 8, pairs(*((4, size) for size in sizes)))(*parts),
        (Y, Y, X, X),
        (1, 0, 1, 0),
    )
    parts = exchange(
        call(
            turn_kernel,
            "turn",
            [SMEM] + [VMEM] * 8,
            pairs(*((2, size) for size in sizes)),
            [pltpu.VMEM((4, size, ROWS, COLS), F32) for size in sizes],
        )(place, *parts),
        (X, X, Y, Y),
        (0, 1, 0, 1),
    )
    parts = exchange(
        call(halve_kernel, "halve", [VMEM] * 8, pairs(*((size,) for size in sizes)))(*parts),
        (X, X, Y, Y),
        (1, 0, 1, 0),
    )
    sent, own = call(
        z_cut_kernel,
        "z_cut",
        [SMEM] + [VMEM] * 8,
        [granules(8), granules(8, kind=F32)],
        [pltpu.VMEM((4, ROWS, COLS), F32)] * 2,
    )(place, *parts)

    total, squares = call(
        square_kernel, "square", [VMEM] * 2, [((8, ROWS, COLS), F32), ((128, 1, LANES), F32)]
    )(own, swap(sent, ZH))
    squares = lax.all_to_all(squares, ALL, 0, 0, tiled=True)
    grad_first, grad_middle, grad_last = call(
        scale_kernel,
        "scale",
        [VMEM] * 2,
        [((units // 64, inputs), F32), ((ROWS, units), F32), ((ROWS, width), F32)],
        kind=jax.ShapeDtypeStruct,
    )(total, squares)
    return grad_first.T, grad_middle.T, grad_last


def solution(mesh):
    finer = Mesh(mesh.devices.reshape(4, 2, 4, 2, mesh.shape["mp"]), ALL)
    return jax.shard_map(
        per_device,
        mesh=finer,
        in_specs=(P(DP, None), P(DP, None), P(DP), P(None, "mp"), P("mp", None), P(None, "mp")),
        out_specs=(P(None, MP_DP), P("mp", DP), P(DP, "mp")),
        check_vma=False,
    )
```

```python
import functools

import jax
import jax.numpy as jnp
import numpy as np
from jax import lax
from jax.experimental import pallas as pl
from jax.experimental.pallas import tpu as pltpu
from jax.sharding import Mesh
from jax.sharding import PartitionSpec as P

BLOCK = 128
PARAMS = 8469504
DP = ("dp_0", "dp_1", "dp_2", "dp_3")
MP_DP = ("mp", "dp_0", "dp_1", "dp_2", "dp_3")
ALL = DP + ("mp",)
Y, ZH, X, CORE = DP
LANES = 128
ROWS, COLS = 24, 384
SIZE, SECOND = 344, 320
DEPTH = 512
VMEM = pl.BlockSpec(memory_space=pltpu.VMEM)
SMEM = pl.BlockSpec(memory_space=pltpu.SMEM)
HBM = pl.BlockSpec(memory_space=pl.ANY)
BF16, F32 = jnp.bfloat16, jnp.float32


def wide(shard):
    return shard.astype(F32)


def narrow(shard):
    return shard.astype(BF16)


def swap(shard, axis):
    return lax.ppermute(shard, axis, [(0, 1), (1, 0)])


def to_pair(shard, axis, order):
    pairs = [(i, i ^ 1) for i in range(4)] if order == 0 else [(i, 3 - i) for i in range(4)]
    return lax.ppermute(shard, axis, pairs)


def silu_slope(pre_act):
    sigmoid_of = 1.0 / (1.0 + jnp.exp(-pre_act))
    return sigmoid_of * (1.0 + pre_act * (1.0 - sigmoid_of))


def dot(left, right):
    return jnp.dot(left, right, preferred_element_type=F32)


def contract(left, right, left_dim, right_dim):
    return lax.dot_general(
        left, right, (((left_dim,), (right_dim,)), ((), ())), preferred_element_type=F32
    )


def call(body, name, in_specs, outs, scratch=(), kind=pltpu.VMEM):
    kernel = pl.pallas_call(
        body,
        out_shape=[kind(*out) for out in outs],
        in_specs=in_specs,
        out_specs=[VMEM] * len(outs),
        scratch_shapes=list(scratch),
        compiler_params=pltpu.CompilerParams(vmem_limit_bytes=24 << 20),
        cost_estimate=pl.CostEstimate(flops=1 << 34, bytes_accessed=1 << 26, transcendentals=0),
        name=name,
    )

    def run(*operands):
        return kernel(
            *(
                operand if spec is SMEM else pltpu.with_memory_space_constraint(
                    operand, pltpu.VMEM if spec is VMEM else pltpu.HBM
                )
                for operand, spec in zip(operands, in_specs)
            )
        )

    return run


def rows_of_core(rows_ref, core, out_ref):
    for block in range(32):
        y, x, z_hi = block // 8, block // 2 % 4, block % 2
        first = 2 * ROWS * ((2 * y + z_hi) * 4 + x)
        rows = pl.ds(pl.multiple_of(first + ROWS * core, 8), ROWS)
        out_ref[ROWS * block : ROWS * (block + 1), :] = narrow(rows_ref[rows, :])


def forward_kernel(
    belief_hbm, w_first_hbm, w_middle_hbm, pre_first_ref, act_first_ref, sent_ref,
    belief, w_first, w_middle, sems,
):
    inputs = belief.shape[0]
    cuts = [(start, min(start + DEPTH, inputs)) for start in range(0, inputs, DEPTH)]
    copies = []
    for i, (start, stop) in enumerate(cuts):
        rows = pl.ds(start, stop - start)
        copies.append(
            (
                pltpu.make_async_copy(belief_hbm.at[rows], belief.at[rows], sems.at[2 * i]),
                pltpu.make_async_copy(w_first_hbm.at[rows], w_first.at[rows], sems.at[2 * i + 1]),
            )
        )
    copies.append((pltpu.make_async_copy(w_middle_hbm, w_middle, sems.at[2 * len(cuts)]),))
    for pair in copies:
        for copy in pair:
            copy.start()
    pre_first = jnp.zeros(pre_first_ref.shape, F32)
    for (start, stop), pair in zip(cuts, copies):
        for copy in pair:
            copy.wait()
        pre_first += contract(belief[start:stop, :], w_first[start:stop, :], 0, 0)
    pre_first_ref[...] = pre_first
    act_first = narrow(pre_first / (1.0 + jnp.exp(-pre_first)))
    act_first_ref[...] = act_first
    copies[-1][0].wait()
    sent_ref[...] = narrow(dot(act_first, w_middle[...]))


def half_kernel(place_ref, w_last_hbm, half_ref, w_last, sem):
    copy = pltpu.make_async_copy(w_last_hbm, w_last, sem)
    copy.start()
    copy.wait()
    size, total = half_ref.shape[0], w_last.shape[0]

    @pl.when(place_ref[0] == 0)
    def _():
        half_ref[...] = w_last[0:size, :]

    @pl.when(place_ref[0] != 0)
    def _():
        half_ref[size - 8 :, :] = jnp.zeros((8, half_ref.shape[1]), half_ref.dtype)
        half_ref[0 : total - SECOND, :] = w_last[SECOND:total, :]


def stage_kernel(
    place_ref, counts_ref, pre_first_ref, orders_ref, target_hbm, w_last_hbm,
    w_own_ref, target_own_ref, target_other_ref, first_slope_ref, onehot_ref, live_ref,
    target_ref, sems,
):
    copies = (
        pltpu.make_async_copy(target_hbm, target_ref, sems.at[0]),
        pltpu.make_async_copy(w_last_hbm, w_own_ref, sems.at[1]),
    )
    for copy in copies:
        copy.start()
    first_slope_ref[...] = silu_slope(pre_first_ref[...])
    order = jnp.where(place_ref[0] == 0, orders_ref[0], orders_ref[1])
    units = lax.broadcasted_iota(jnp.int32, onehot_ref.shape, 1)
    onehot_ref[...] = jnp.where(order == units, 1.0, 0.0).astype(BF16)
    row = lax.broadcasted_iota(jnp.int32, live_ref.shape, 1)
    count = jnp.where(row < BLOCK, counts_ref[0], counts_ref[1] + BLOCK)
    live_ref[...] = jnp.where(row < count, 1.0, 0.0)
    copies[0].wait()
    width = target_own_ref.shape[0]
    low, high = target_ref[0:width, :], target_ref[width : 2 * width, :]
    is_low = place_ref[4] == 0
    target_own_ref[...] = jnp.where(is_low, low, high)
    target_other_ref[...] = jnp.where(is_low, high, low)
    copies[1].wait()


def hidden_kernel(
    place_ref, partial_ref, arrived_ref, live_ref, target_ref, w_ref,
    act_ref, act_slope_ref, back_ref, sent_ref, own_ref, rows_ref,
):
    core = place_ref[0]
    pre_middle = wide(partial_ref[...]) + wide(arrived_ref[...])
    sigmoid_of = 1.0 / (1.0 + jnp.exp(-pre_middle))
    act = narrow(pre_middle * sigmoid_of)
    act_ref[...] = act
    act_slope_ref[...] = sigmoid_of * (1.0 + pre_middle * (1.0 - sigmoid_of))
    slope = slope_of(w_ref[...], act, target_ref[...], live_ref[...])
    half = own_ref.shape[0]
    sent_ref[half:, :] = slope
    back_ref[...] = contract(slope, w_ref[...], 0, 0)
    rows_ref[...] = wide(act).T
    rows_of_core(rows_ref, 1 - core, sent_ref)
    rows_of_core(rows_ref, core, own_ref)


def slope_of(weights, act, target, live):
    mismatch = contract(weights, act, 1, 1) - wide(target)
    return narrow(jnp.clip(mismatch, -1.0, 1.0) * live)


def slopes_kernel(
    place_ref, act_ref, act_slope_ref, back_ref, live_ref, target_ref, first_slope_ref,
    onehot_ref, fetched_ref, relayed_ref, w_middle_ref, sent_ref, own_ref, rows_ref,
):
    core = place_ref[0]
    size, total = fetched_ref.shape[0], target_ref.shape[0]
    act, live = act_ref[...], live_ref[...]
    back = back_ref[...]
    for is_own, start, stop in ((core == 0, 0, size), (core != 0, SECOND, total)):
        rows = slice(0, stop - start)
        weights = jnp.where(is_own, fetched_ref[rows, :], relayed_ref[rows, :])
        slope = slope_of(weights, act, target_ref[start:stop, :], live)
        if start:
            column = lax.broadcasted_iota(jnp.int32, slope.shape, 0) + start
            slope = jnp.where(column >= size, slope, jnp.zeros_like(slope))
        back += contract(slope, weights, 0, 0)
    slope_middle = narrow(back * act_slope_ref[...])
    slope_first = narrow(contract(slope_middle, w_middle_ref[...], 1, 1) * first_slope_ref[...])
    slope_first = narrow(contract(onehot_ref[...], slope_first, 1, 1))
    half = slope_first.shape[0] // 2
    sent_ref[2 * half :, :] = slope_first[:half]
    own_ref[2 * half :, :] = slope_first[half:]
    rows_ref[...] = wide(slope_middle).T
    rows_of_core(rows_ref, 1 - core, sent_ref)
    rows_of_core(rows_ref, core, own_ref)


def column_cuts(width):
    return [(start, min(start + COLS, width)) for start in range(0, width, COLS)]


def put_columns(raw, granule, out_ref):
    width = raw.shape[1]
    if width < COLS:
        raw = jnp.concatenate([raw, jnp.zeros((raw.shape[0], COLS - width), raw.dtype)], 1)
    for unit in range(16):
        out_ref[unit, granule] = raw[unit * ROWS : (unit + 1) * ROWS]


def kept_and_sent(me, order):
    near, far, opposite = lax.bitwise_xor(me, 1), 3 - me, lax.bitwise_xor(me, 2)
    return ((me, far), (near, opposite)) if order == 0 else ((me, near), (far, opposite))


def cut_rows(raw_ref, me, order, kept_ref, sent_ref):
    for out_ref, blocks in zip((kept_ref, sent_ref), kept_and_sent(me, order)):
        for position, x in enumerate(blocks):
            for y in range(4):
                for granule in range(4):
                    first = ROWS * (2 * (4 * y + x) + granule // 2)
                    columns = slice(granule % 2 * COLS, (granule % 2 + 1) * COLS)
                    rows = raw_ref[pl.ds(pl.multiple_of(first, 8), ROWS), columns]
                    out_ref[position, y, granule] = rows.astype(out_ref.dtype)


def last_kernel(place_ref, own_ref, sent_ref, arrived_ref, kept_out, sent_out, raw_ref, padded_ref):
    half = own_ref.shape[0]
    width = sent_ref.shape[0] - half
    padded_ref[...] = jnp.zeros_like(padded_ref)
    padded_ref[0, 0:width, :] = sent_ref[half:, :]
    padded_ref[1, 0:width, :] = arrived_ref[half:, :]
    raw_ref[...] = contract(own_ref[...], padded_ref[0], 1, 1) + contract(
        arrived_ref[0:half, :], padded_ref[1], 1, 1
    )
    cut_rows(raw_ref, place_ref[2], 0, kept_out, sent_out)


def middle_kernel(
    place_ref, own_ref, arrived_ref, act_ref, sibling_act_ref, kept_out, sent_out, raw_ref
):
    half = raw_ref.shape[0]
    raw_ref[...] = dot(own_ref[0:half, :], act_ref[...]) + dot(
        arrived_ref[0:half, :], sibling_act_ref[...]
    )
    cut_rows(raw_ref, place_ref[2], 1, kept_out, sent_out)


def first_kernel(place_ref, own_ref, arrived_ref, belief_ref, sibling_belief_ref, *refs):
    raw_ref = refs[-1]
    start_row = own_ref.shape[0] // 3 * 2
    own, arrived = own_ref[start_row:, :], arrived_ref[start_row:, :]
    for start, stop in column_cuts(belief_ref.shape[0]):
        raw = contract(own, belief_ref[start:stop, :], 1, 1) + contract(
            arrived, sibling_belief_ref[start:stop, :], 1, 1
        )
        put_columns(raw, start // COLS, raw_ref)
    for order, part in enumerate((slice(0, 4), slice(4, 7))):
        for side, blocks in enumerate(kept_and_sent(place_ref[1], order)):
            out_ref = refs[2 * order + side]
            for position, y in enumerate(blocks):
                for x in range(4):
                    out_ref[position, x] = raw_ref[4 * y + x, part].astype(out_ref.dtype)


def halve_kernel(kept_ref, arrived_ref, kept_out, sent_out):
    kept_out[...] = kept_ref[0] + wide(arrived_ref[0])
    sent_out[...] = narrow(kept_ref[1] + wide(arrived_ref[1]))


def turn_kernel(axis, order, place_ref, kept_ref, arrived_ref, kept_out, sent_out, sum_ref):
    sum_ref[...] = kept_ref[...] + wide(arrived_ref[...])
    for out_ref, blocks in zip((kept_out, sent_out), kept_and_sent(place_ref[axis], order)):
        for position, block in enumerate(blocks):
            out_ref[position] = sum_ref[block].astype(out_ref.dtype)


def z_cut_kernel(place_ref, *refs):
    sent_ref, own_ref, last_sum, middle_sum = refs[8:12]
    z_hi = place_ref[3]
    low, high, last, middle = (
        refs[2 * part][...] + wide(refs[2 * part + 1][...]) for part in range(4)
    )
    last_sum[...] = last
    middle_sum[...] = middle
    rows = [low[granule] for granule in range(4)] + [high[granule] for granule in range(3)]
    for side, out_ref in ((1 - z_hi, sent_ref), (z_hi, own_ref)):
        kind = out_ref.dtype
        out_ref[0:2] = last_sum[pl.ds(2 * side, 2)].astype(kind)
        out_ref[2:4] = middle_sum[pl.ds(2 * side, 2)].astype(kind)
        halves = [jnp.where(side == 0, row[0:12], row[12:24]) for row in rows]
        halves.append(jnp.zeros_like(halves[0]))
        for pair in range(4):
            out_ref[4 + pair] = jnp.concatenate(halves[2 * pair : 2 * pair + 2], 0).astype(kind)


def square_kernel(own_ref, arrived_ref, total_ref, squares_ref):
    total = own_ref[...] + wide(arrived_ref[...])
    total_ref[...] = total
    squares_ref[...] = jnp.broadcast_to(jnp.sum(total * total), squares_ref.shape)


def scale_kernel(total_ref, squares_ref, first_ref, middle_ref, last_ref):
    square_sum = jnp.sum(squares_ref[...], axis=0)
    norm_scale = lax.rsqrt(square_sum / PARAMS + 1e-06)
    norm_scale = jnp.concatenate([norm_scale] * 3, 1)
    for ref, start in ((last_ref, 0), (middle_ref, 2)):
        for half in range(2):
            columns = slice(half * COLS, min((half + 1) * COLS, ref.shape[1]))
            width = columns.stop - columns.start
            ref[:, columns] = (total_ref[start + half] * norm_scale)[:, :width]
    for granule, (start, stop) in enumerate(column_cuts(first_ref.shape[1])):
        row = granule % 2 * 12
        scaled = total_ref[4 + granule // 2, row : row + 12] * norm_scale
        first_ref[:, start:stop] = scaled[:, : stop - start]


def granules(*lead, kind=BF16):
    return ((*lead, ROWS, COLS), kind)


def per_device(belief, target_value, counts, w_first, w_middle, w_last):
    total_rows, inputs = belief.shape
    width = w_last.shape[1]
    units = w_first.shape[1]
    hidden = w_middle.shape[1]
    belief_t, w_last_t = belief.T, w_last.T

    indices = (CORE, Y, X, ZH, "mp")
    place = jnp.stack([lax.axis_index(axis) for axis in indices])

    (half,) = call(
        half_kernel,
        "half",
        [SMEM, HBM],
        [((SIZE, hidden), BF16)],
        [pltpu.VMEM(w_last_t.shape, BF16), pltpu.SemaphoreType.DMA],
    )(place, w_last_t)
    fetched = lax.ppermute(half, (ZH, "mp"), [(0, 3), (3, 0), (1, 2), (2, 1)])
    belief_first, half = lax.optimization_barrier((belief_t, half))

    pre_first, act_first, hidden_sent = call(
        forward_kernel,
        "forward",
        [HBM] * 3,
        [
            ((total_rows, units), F32),
            ((total_rows, units), BF16),
            ((total_rows, hidden), BF16),
        ],
        [
            pltpu.VMEM((inputs, total_rows), BF16),
            pltpu.VMEM((inputs, units), BF16),
            pltpu.VMEM((units, hidden), BF16),
            pltpu.SemaphoreType.DMA((2 * pl.cdiv(inputs, DEPTH) + 1,)),
        ],
        kind=pltpu.HBM,
    )(belief_first, w_first, w_middle)
    arrived = swap(hidden_sent, "mp")

    order = np.arange(units, dtype=np.int32).reshape(4, 2, 4, 2, -1).transpose(3, 0, 2, 1, 4)
    orders = np.stack([order[::-1], order]).reshape(2, units, 1)
    w_own, target_own, target_other, first_slope, onehot, live = call(
        stage_kernel,
        "stage",
        [SMEM, SMEM, VMEM, VMEM, HBM, HBM],
        [
            ((width, hidden), BF16),
            ((width, total_rows), BF16),
            ((width, total_rows), BF16),
            ((total_rows, units), F32),
            ((units, units), BF16),
            ((1, total_rows), F32),
        ],
        [pltpu.VMEM((2 * width, total_rows), BF16), pltpu.SemaphoreType.DMA((2,))],
    )(place, counts, pre_first, jnp.asarray(orders), target_value.T, w_last_t)
    fetched, live = lax.optimization_barrier((fetched, live))
    relayed = swap(fetched, CORE)
    belief_swapped, act_swapped = lax.optimization_barrier((belief_t, act_first))
    sibling_belief = swap(belief_swapped, CORE)
    sibling_act = swap(act_swapped, CORE)

    act, act_slope, back_own, last_sent, last_own = call(
        hidden_kernel,
        "hidden",
        [SMEM] + [VMEM] * 5,
        [
            ((total_rows, hidden), BF16),
            ((total_rows, hidden), F32),
            ((total_rows, hidden), F32),
            ((hidden // 2 + width, total_rows), BF16),
            ((hidden // 2, total_rows), BF16),
        ],
        [pltpu.VMEM((hidden, total_rows), F32)],
    )(place, hidden_sent, arrived, live, target_own, w_own)
    last_arrived = swap(last_sent, CORE)

    slopes_sent, slopes_own = call(
        slopes_kernel,
        "slopes",
        [SMEM] + [VMEM] * 10,
        [((hidden // 2 + units // 2, total_rows), BF16)] * 2,
        [pltpu.VMEM((hidden, total_rows), F32)],
    )(
        place, act, act_slope, back_own, live, target_other, first_slope, onehot,
        fetched, relayed, w_middle,
    )
    slopes_arrived = swap(slopes_sent, CORE)

    def pairs(*sizes):
        return [out for size in sizes for out in (granules(*size, kind=F32), granules(*size))]

    def exchange(parts, axes, orders):
        sent = [part[1] for part in parts]
        arrived = [to_pair(*sending) for sending in zip(sent, axes, orders)]
        return [
            (part[0], lax.optimization_barrier((coming, *sent))[0])
            for part, coming in zip(parts, arrived)
        ]

    def halve(part, *lead):
        return call(halve_kernel, "halve", [VMEM] * 2, pairs((*lead, part[0].shape[-3])))(*part)

    def turn(part, axis, order):
        size = part[0].shape[-3]
        return call(
            functools.partial(turn_kernel, 1 if axis == Y else 2, order),
            "turn",
            [SMEM] + [VMEM] * 2,
            pairs((2, size)),
            [pltpu.VMEM((4, size, ROWS, COLS), F32)],
        )(place, *part)

    raw = pltpu.VMEM((hidden // 2, units), F32)
    last_own, slopes_own = lax.optimization_barrier((last_own, slopes_own))
    last_parts = call(
        last_kernel,
        "last",
        [SMEM] + [VMEM] * 3,
        pairs((2, 4, 4)),
        [raw, pltpu.VMEM((2, units, total_rows), BF16)],
    )(place, last_own, last_sent, last_arrived)
    first_parts = call(
        first_kernel,
        "first",
        [SMEM] + [VMEM] * 4,
        pairs((2, 4, 4), (2, 4, 3)),
        [pltpu.VMEM((16, 7, ROWS, COLS), F32)],
    )(place, slopes_own, slopes_arrived, belief_t, sibling_belief)
    middle_parts = call(
        middle_kernel, "middle", [SMEM] + [VMEM] * 4, pairs((2, 4, 4)), [raw]
    )(place, slopes_own, slopes_arrived, act_first, sibling_act)
    axes, turned, orders, swapped = (X, X, Y, Y), (Y, Y, X, X), (0, 1, 0, 1), (1, 0, 1, 0)
    parts = (last_parts, middle_parts, first_parts[0:2], first_parts[2:4])
    parts = [halve(part, 4) for part in exchange(parts, axes, orders)]
    parts = [
        turn(part, turned[i], orders[i]) for i, part in enumerate(exchange(parts, axes, swapped))
    ]
    parts = [halve(part) for part in exchange(parts, turned, orders)]
    last_parts, middle_parts, *first_parts = exchange(parts, turned, swapped)
    parts = (*first_parts[0], *first_parts[1], *last_parts, *middle_parts)
    sent, own = call(
        z_cut_kernel,
        "z_cut",
        [SMEM] + [VMEM] * 8,
        [granules(8), granules(8, kind=F32)],
        [pltpu.VMEM((4, ROWS, COLS), F32)] * 2,
    )(place, *parts)

    total, squares = call(
        square_kernel, "square", [VMEM] * 2, [((8, ROWS, COLS), F32), ((128, 1, LANES), F32)]
    )(own, swap(sent, ZH))
    squares = lax.all_to_all(squares, ALL, 0, 0, tiled=True)
    grad_first, grad_middle, grad_last = call(
        scale_kernel,
        "scale",
        [VMEM] * 2,
        [((units // 64, inputs), F32), ((ROWS, units), F32), ((ROWS, width), F32)],
        kind=jax.ShapeDtypeStruct,
    )(total, squares)
    return grad_first.T, grad_middle.T, grad_last


def solution(mesh):
    finer = Mesh(mesh.devices.reshape(4, 2, 4, 2, mesh.shape["mp"]), ALL)
    return jax.shard_map(
        per_device,
        mesh=finer,
        in_specs=(P(DP, None), P(DP, None), P(DP), P(None, "mp"), P("mp", None), P(None, "mp")),
        out_specs=(P(None, MP_DP), P("mp", DP), P(DP, "mp")),
        check_vma=False,
    )
```

```python
import functools

import jax
import jax.numpy as jnp
import numpy as np
from jax import lax
from jax.experimental import pallas as pl
from jax.experimental.pallas import tpu as pltpu
from jax.sharding import Mesh
from jax.sharding import PartitionSpec as P

BLOCK = 128
PARAMS = 8469504
DP = ("dp_0", "dp_1", "dp_2", "dp_3")
MP_DP = ("mp", "dp_0", "dp_1", "dp_2", "dp_3")
ALL = DP + ("mp",)
Y, ZH, X, CORE = DP
LANES = 128
ROWS, COLS = 24, 384
SIZE, SECOND = 344, 320
DEPTH = 512
VMEM = pl.BlockSpec(memory_space=pltpu.VMEM)
SMEM = pl.BlockSpec(memory_space=pltpu.SMEM)
HBM = pl.BlockSpec(memory_space=pl.ANY)
BF16, F32 = jnp.bfloat16, jnp.float32


def wide(shard):
    return shard.astype(F32)


def narrow(shard):
    return shard.astype(BF16)


def swap(shard, axis):
    return lax.ppermute(shard, axis, [(0, 1), (1, 0)])


def to_pair(shard, axis, order):
    pairs = [(i, i ^ 1) for i in range(4)] if order == 0 else [(i, 3 - i) for i in range(4)]
    return lax.ppermute(shard, axis, pairs)


def silu_slope(pre_act):
    sigmoid_of = 1.0 / (1.0 + jnp.exp(-pre_act))
    return sigmoid_of * (1.0 + pre_act * (1.0 - sigmoid_of))


def dot(left, right):
    return jnp.dot(left, right, preferred_element_type=F32)


def contract(left, right, left_dim, right_dim):
    return lax.dot_general(
        left, right, (((left_dim,), (right_dim,)), ((), ())), preferred_element_type=F32
    )


def call(body, name, in_specs, outs, scratch=(), kind=pltpu.VMEM, far=0):
    kernel = pl.pallas_call(
        body,
        out_shape=[(pltpu.HBM if i < far else kind)(*out) for i, out in enumerate(outs)],
        in_specs=in_specs,
        out_specs=[HBM if i < far else VMEM for i in range(len(outs))],
        scratch_shapes=list(scratch),
        compiler_params=pltpu.CompilerParams(vmem_limit_bytes=24 << 20),
        cost_estimate=pl.CostEstimate(flops=1 << 34, bytes_accessed=1 << 26, transcendentals=0),
        name=name,
    )

    def run(*operands):
        return kernel(
            *(
                operand if spec is SMEM else pltpu.with_memory_space_constraint(
                    operand, pltpu.VMEM if spec is VMEM else pltpu.HBM
                )
                for operand, spec in zip(operands, in_specs)
            )
        )

    return run


def rows_of_core(rows_ref, core, out_ref):
    for block in range(32):
        y, x, z_hi = block // 8, block // 2 % 4, block % 2
        first = 2 * ROWS * ((2 * y + z_hi) * 4 + x)
        rows = pl.ds(pl.multiple_of(first + ROWS * core, 8), ROWS)
        out_ref[ROWS * block : ROWS * (block + 1), :] = narrow(rows_ref[rows, :])


def forward_kernel(
    belief_hbm, w_first_hbm, w_middle_hbm, pre_first_hbm, act_first_hbm, sent_ref,
    belief, w_first, w_middle, pre_first_ref, act_first_ref, sems,
):
    inputs = belief.shape[0]
    cuts = [(start, min(start + DEPTH, inputs)) for start in range(0, inputs, DEPTH)]
    copies = []
    for i, (start, stop) in enumerate(cuts):
        rows = pl.ds(start, stop - start)
        copies.append(
            (
                pltpu.make_async_copy(belief_hbm.at[rows], belief.at[rows], sems.at[2 * i]),
                pltpu.make_async_copy(w_first_hbm.at[rows], w_first.at[rows], sems.at[2 * i + 1]),
            )
        )
    copies.append((pltpu.make_async_copy(w_middle_hbm, w_middle, sems.at[2 * len(cuts)]),))
    for pair in copies:
        for copy in pair:
            copy.start()
    results = (
        pltpu.make_async_copy(pre_first_ref, pre_first_hbm, sems.at[2 * len(cuts) + 1]),
        pltpu.make_async_copy(act_first_ref, act_first_hbm, sems.at[2 * len(cuts) + 2]),
    )
    pre_first = jnp.zeros(pre_first_ref.shape, F32)
    for (start, stop), pair in zip(cuts, copies):
        for copy in pair:
            copy.wait()
        pre_first += contract(belief[start:stop, :], w_first[start:stop, :], 0, 0)
    pre_first_ref[...] = pre_first
    results[0].start()
    act_first = narrow(pre_first / (1.0 + jnp.exp(-pre_first)))
    act_first_ref[...] = act_first
    results[1].start()
    copies[-1][0].wait()
    sent_ref[...] = narrow(dot(act_first, w_middle[...]))
    for copy in results:
        copy.wait()


def half_kernel(place_ref, w_last_hbm, half_ref, last_ref, sem):
    size, total = half_ref.shape[0], w_last_hbm.shape[0]

    @pl.when(place_ref[0] == 0)
    def _():
        copy = pltpu.make_async_copy(w_last_hbm.at[pl.ds(0, size)], half_ref, sem)
        copy.start()
        copy.wait()

    @pl.when(place_ref[0] != 0)
    def _():
        copy = pltpu.make_async_copy(w_last_hbm.at[pl.ds(SECOND, total - SECOND)], last_ref, sem)
        copy.start()
        half_ref[size - 8 :, :] = jnp.zeros((8, half_ref.shape[1]), half_ref.dtype)
        copy.wait()
        half_ref[0 : total - SECOND, :] = last_ref[...]


def stage_kernel(
    place_ref, counts_ref, pre_first_ref, orders_ref, target_hbm, w_last_hbm,
    w_own_ref, target_own_ref, target_other_ref, first_slope_ref, onehot_ref, live_ref,
    target_ref, sems,
):
    copies = (
        pltpu.make_async_copy(target_hbm, target_ref, sems.at[0]),
        pltpu.make_async_copy(w_last_hbm, w_own_ref, sems.at[1]),
    )
    for copy in copies:
        copy.start()
    first_slope_ref[...] = silu_slope(pre_first_ref[...])
    order = jnp.where(place_ref[0] == 0, orders_ref[0], orders_ref[1])
    units = lax.broadcasted_iota(jnp.int32, onehot_ref.shape, 1)
    onehot_ref[...] = jnp.where(order == units, 1.0, 0.0).astype(BF16)
    row = lax.broadcasted_iota(jnp.int32, live_ref.shape, 1)
    count = jnp.where(row < BLOCK, counts_ref[0], counts_ref[1] + BLOCK)
    live_ref[...] = jnp.where(row < count, 1.0, 0.0)
    copies[0].wait()
    width = target_own_ref.shape[0]
    low, high = target_ref[0:width, :], target_ref[width : 2 * width, :]
    is_low = place_ref[4] == 0
    target_own_ref[...] = jnp.where(is_low, low, high)
    other = jnp.where(is_low, high, low)
    size = target_other_ref.shape[1]
    for side in range(2):

        @pl.when(place_ref[0] == side)
        def _():
            target_other_ref[side] = other[0:size]
            target_other_ref[1 - side, size - 8 :, :] = jnp.zeros((8, other.shape[1]), other.dtype)
            target_other_ref[1 - side, 0 : width - SECOND, :] = other[SECOND:]

    copies[1].wait()


def hidden_kernel(
    place_ref, partial_ref, arrived_ref, live_ref, target_ref, w_ref,
    act_ref, act_slope_ref, back_ref, sent_ref, own_ref, rows_ref,
):
    core = place_ref[0]
    pre_middle = wide(partial_ref[...]) + wide(arrived_ref[...])
    sigmoid_of = 1.0 / (1.0 + jnp.exp(-pre_middle))
    act = narrow(pre_middle * sigmoid_of)
    act_ref[...] = act
    act_slope_ref[...] = sigmoid_of * (1.0 + pre_middle * (1.0 - sigmoid_of))
    slope = slope_of(w_ref[...], act, target_ref[...], live_ref[...])
    half = own_ref.shape[0]
    sent_ref[half:, :] = slope
    back_ref[...] = contract(slope, w_ref[...], 0, 0)
    rows_ref[...] = wide(act).T
    rows_of_core(rows_ref, 1 - core, sent_ref)
    rows_of_core(rows_ref, core, own_ref)


def slope_of(weights, act, target, live):
    mismatch = contract(weights, act, 1, 1) - wide(target)
    return narrow(jnp.clip(mismatch, -1.0, 1.0) * live)


def slopes_kernel(
    place_ref, act_ref, act_slope_ref, back_ref, live_ref, target_ref, first_slope_ref,
    onehot_ref, fetched_ref, relayed_ref, w_middle_ref, sent_ref, own_ref, rows_ref,
):
    core = place_ref[0]
    act, live = act_ref[...], live_ref[...]
    back = back_ref[...]
    for side, w_ref in enumerate((fetched_ref, relayed_ref)):
        weights = w_ref[...]
        slope = slope_of(weights, act, target_ref[side], live)
        repeated = jnp.where(core == side, 0, SIZE - SECOND)
        column = lax.broadcasted_iota(jnp.int32, slope.shape, 0)
        slope = jnp.where(column >= repeated, slope, jnp.zeros_like(slope))
        back += contract(slope, weights, 0, 0)
    slope_middle = narrow(back * act_slope_ref[...])
    slope_first = narrow(contract(slope_middle, w_middle_ref[...], 1, 1) * first_slope_ref[...])
    slope_first = narrow(contract(onehot_ref[...], slope_first, 1, 1))
    half = slope_first.shape[0] // 2
    sent_ref[2 * half :, :] = slope_first[:half]
    own_ref[2 * half :, :] = slope_first[half:]
    rows_ref[...] = wide(slope_middle).T
    rows_of_core(rows_ref, 1 - core, sent_ref)
    rows_of_core(rows_ref, core, own_ref)


def column_cuts(width):
    return [(start, min(start + COLS, width)) for start in range(0, width, COLS)]


def put_columns(raw, granule, out_ref):
    width = raw.shape[1]
    if width < COLS:
        raw = jnp.concatenate([raw, jnp.zeros((raw.shape[0], COLS - width), raw.dtype)], 1)
    for unit in range(16):
        out_ref[unit, granule] = raw[unit * ROWS : (unit + 1) * ROWS]


def kept_and_sent(me, order):
    near, far, opposite = lax.bitwise_xor(me, 1), 3 - me, lax.bitwise_xor(me, 2)
    return ((me, far), (near, opposite)) if order == 0 else ((me, near), (far, opposite))


def cut_rows(raw_ref, me, order, kept_ref, sent_ref):
    for out_ref, blocks in zip((kept_ref, sent_ref), kept_and_sent(me, order)):
        for position, x in enumerate(blocks):
            for y in range(4):
                for granule in range(4):
                    first = ROWS * (2 * (4 * y + x) + granule // 2)
                    columns = slice(granule % 2 * COLS, (granule % 2 + 1) * COLS)
                    rows = raw_ref[pl.ds(pl.multiple_of(first, 8), ROWS), columns]
                    out_ref[position, y, granule] = rows.astype(out_ref.dtype)


def last_kernel(place_ref, own_ref, sent_ref, arrived_ref, kept_out, sent_out, raw_ref, padded_ref):
    half = own_ref.shape[0]
    width = sent_ref.shape[0] - half
    padded_ref[...] = jnp.zeros_like(padded_ref)
    padded_ref[0, 0:width, :] = sent_ref[half:, :]
    padded_ref[1, 0:width, :] = arrived_ref[half:, :]
    raw_ref[...] = contract(own_ref[...], padded_ref[0], 1, 1) + contract(
        arrived_ref[0:half, :], padded_ref[1], 1, 1
    )
    cut_rows(raw_ref, place_ref[2], 0, kept_out, sent_out)


def middle_kernel(
    place_ref, own_ref, arrived_ref, act_ref, sibling_act_ref, kept_out, sent_out, raw_ref
):
    half = raw_ref.shape[0]
    raw_ref[...] = dot(own_ref[0:half, :], act_ref[...]) + dot(
        arrived_ref[0:half, :], sibling_act_ref[...]
    )
    cut_rows(raw_ref, place_ref[2], 1, kept_out, sent_out)


def first_kernel(place_ref, own_ref, arrived_ref, belief_ref, sibling_belief_ref, *refs):
    raw_ref = refs[-1]
    start_row = own_ref.shape[0] // 3 * 2
    own, arrived = own_ref[start_row:, :], arrived_ref[start_row:, :]
    for start, stop in column_cuts(belief_ref.shape[0]):
        raw = contract(own, belief_ref[start:stop, :], 1, 1) + contract(
            arrived, sibling_belief_ref[start:stop, :], 1, 1
        )
        put_columns(raw, start // COLS, raw_ref)
    for order, part in enumerate((slice(0, 4), slice(4, 7))):
        for side, blocks in enumerate(kept_and_sent(place_ref[1], order)):
            out_ref = refs[2 * order + side]
            for position, y in enumerate(blocks):
                for x in range(4):
                    out_ref[position, x] = raw_ref[4 * y + x, part].astype(out_ref.dtype)


def halve_kernel(kept_ref, arrived_ref, kept_out, sent_out):
    kept_out[...] = kept_ref[0] + wide(arrived_ref[0])
    sent_out[...] = narrow(kept_ref[1] + wide(arrived_ref[1]))


def turn_kernel(axis, order, place_ref, kept_ref, arrived_ref, kept_out, sent_out):
    for out_ref, blocks in zip((kept_out, sent_out), kept_and_sent(place_ref[axis], order)):
        for position, block in enumerate(blocks):
            total = kept_ref[block] + wide(arrived_ref[block])
            out_ref[position] = total.astype(out_ref.dtype)


def z_cut_kernel(place_ref, *refs):
    sent_ref, own_ref, last_sum, middle_sum = refs[8:12]
    z_hi = place_ref[3]
    low, high, last, middle = (
        refs[2 * part][...] + wide(refs[2 * part + 1][...]) for part in range(4)
    )
    last_sum[...] = last
    middle_sum[...] = middle
    rows = [low[granule] for granule in range(4)] + [high[granule] for granule in range(3)]
    for side, out_ref in ((1 - z_hi, sent_ref), (z_hi, own_ref)):
        kind = out_ref.dtype
        out_ref[0:2] = last_sum[pl.ds(2 * side, 2)].astype(kind)
        out_ref[2:4] = middle_sum[pl.ds(2 * side, 2)].astype(kind)
        halves = [jnp.where(side == 0, row[0:12], row[12:24]) for row in rows]
        halves.append(jnp.zeros_like(halves[0]))
        for pair in range(4):
            out_ref[4 + pair] = jnp.concatenate(halves[2 * pair : 2 * pair + 2], 0).astype(kind)


def square_kernel(own_ref, arrived_ref, total_ref, squares_ref):
    total = own_ref[...] + wide(arrived_ref[...])
    total_ref[...] = total
    squares_ref[...] = jnp.broadcast_to(jnp.sum(total * total), squares_ref.shape)


def scale_kernel(total_ref, squares_ref, first_ref, middle_ref, last_ref):
    square_sum = jnp.sum(squares_ref[...], axis=0)
    norm_scale = lax.rsqrt(square_sum / PARAMS + 1e-06)
    norm_scale = jnp.concatenate([norm_scale] * 3, 1)
    for ref, start in ((last_ref, 0), (middle_ref, 2)):
        for half in range(2):
            columns = slice(half * COLS, min((half + 1) * COLS, ref.shape[1]))
            width = columns.stop - columns.start
            ref[:, columns] = (total_ref[start + half] * norm_scale)[:, :width]
    for granule, (start, stop) in enumerate(column_cuts(first_ref.shape[1])):
        row = granule % 2 * 12
        scaled = total_ref[4 + granule // 2, row : row + 12] * norm_scale
        first_ref[:, start:stop] = scaled[:, : stop - start]


def granules(*lead, kind=BF16):
    return ((*lead, ROWS, COLS), kind)


def per_device(belief, target_value, counts, w_first, w_middle, w_last):
    total_rows, inputs = belief.shape
    width = w_last.shape[1]
    units = w_first.shape[1]
    hidden = w_middle.shape[1]
    belief_t, w_last_t = belief.T, w_last.T

    indices = (CORE, Y, X, ZH, "mp")
    place = jnp.stack([lax.axis_index(axis) for axis in indices])

    (half,) = call(
        half_kernel,
        "half",
        [SMEM, HBM],
        [((SIZE, hidden), BF16)],
        [pltpu.VMEM((width - SECOND, hidden), BF16), pltpu.SemaphoreType.DMA],
    )(place, w_last_t)
    fetched = lax.ppermute(half, (ZH, "mp"), [(0, 3), (3, 0), (1, 2), (2, 1)])
    belief_first, half = lax.optimization_barrier((belief_t, half))

    pre_first, act_first, hidden_sent = call(
        forward_kernel,
        "forward",
        [HBM] * 3,
        [
            ((total_rows, units), F32),
            ((total_rows, units), BF16),
            ((total_rows, hidden), BF16),
        ],
        [
            pltpu.VMEM((inputs, total_rows), BF16),
            pltpu.VMEM((inputs, units), BF16),
            pltpu.VMEM((units, hidden), BF16),
            pltpu.VMEM((total_rows, units), F32),
            pltpu.VMEM((total_rows, units), BF16),
            pltpu.SemaphoreType.DMA((2 * pl.cdiv(inputs, DEPTH) + 3,)),
        ],
        far=2,
    )(belief_first, w_first, w_middle)
    arrived = swap(hidden_sent, "mp")

    order = np.arange(units, dtype=np.int32).reshape(4, 2, 4, 2, -1).transpose(3, 0, 2, 1, 4)
    orders = np.stack([order[::-1], order]).reshape(2, units, 1)
    w_own, target_own, target_other, first_slope, onehot, live = call(
        stage_kernel,
        "stage",
        [SMEM, SMEM, VMEM, VMEM, HBM, HBM],
        [
            ((width, hidden), BF16),
            ((width, total_rows), BF16),
            ((2, SIZE, total_rows), BF16),
            ((total_rows, units), F32),
            ((units, units), BF16),
            ((1, total_rows), F32),
        ],
        [pltpu.VMEM((2 * width, total_rows), BF16), pltpu.SemaphoreType.DMA((2,))],
    )(place, counts, pre_first, jnp.asarray(orders), target_value.T, w_last_t)
    fetched, live = lax.optimization_barrier((fetched, live))
    relayed = swap(fetched, CORE)
    belief_swapped, act_swapped = lax.optimization_barrier((belief_t, act_first))
    sibling_belief = swap(belief_swapped, CORE)
    sibling_act = swap(act_swapped, CORE)

    act, act_slope, back_own, last_sent, last_own = call(
        hidden_kernel,
        "hidden",
        [SMEM] + [VMEM] * 5,
        [
            ((total_rows, hidden), BF16),
            ((total_rows, hidden), F32),
            ((total_rows, hidden), F32),
            ((hidden // 2 + width, total_rows), BF16),
            ((hidden // 2, total_rows), BF16),
        ],
        [pltpu.VMEM((hidden, total_rows), F32)],
    )(place, hidden_sent, arrived, live, target_own, w_own)
    last_arrived = swap(last_sent, CORE)

    slopes_sent, slopes_own = call(
        slopes_kernel,
        "slopes",
        [SMEM] + [VMEM] * 10,
        [((hidden // 2 + units // 2, total_rows), BF16)] * 2,
        [pltpu.VMEM((hidden, total_rows), F32)],
    )(
        place, act, act_slope, back_own, live, target_other, first_slope, onehot,
        fetched, relayed, w_middle,
    )
    slopes_arrived = swap(slopes_sent, CORE)

    def pairs(*sizes):
        return [out for size in sizes for out in (granules(*size, kind=F32), granules(*size))]

    def exchange(parts, axes, orders):
        sent = [part[1] for part in parts]
        arrived = [to_pair(*sending) for sending in zip(sent, axes, orders)]
        return [
            (part[0], lax.optimization_barrier((coming, *sent))[0])
            for part, coming in zip(parts, arrived)
        ]

    def halve(part, *lead):
        return call(halve_kernel, "halve", [VMEM] * 2, pairs((*lead, part[0].shape[-3])))(*part)

    def turn(part, axis, order):
        size = part[0].shape[-3]
        return call(
            functools.partial(turn_kernel, 1 if axis == Y else 2, order),
            "turn",
            [SMEM] + [VMEM] * 2,
            pairs((2, size)),
        )(place, *part)

    raw = pltpu.VMEM((hidden // 2, units), F32)
    last_own, slopes_own = lax.optimization_barrier((last_own, slopes_own))
    last_parts = call(
        last_kernel,
        "last",
        [SMEM] + [VMEM] * 3,
        pairs((2, 4, 4)),
        [raw, pltpu.VMEM((2, units, total_rows), BF16)],
    )(place, last_own, last_sent, last_arrived)
    first_parts = call(
        first_kernel,
        "first",
        [SMEM] + [VMEM] * 4,
        pairs((2, 4, 4), (2, 4, 3)),
        [pltpu.VMEM((16, 7, ROWS, COLS), F32)],
    )(place, slopes_own, slopes_arrived, belief_t, sibling_belief)
    middle_parts = call(
        middle_kernel, "middle", [SMEM] + [VMEM] * 4, pairs((2, 4, 4)), [raw]
    )(place, slopes_own, slopes_arrived, act_first, sibling_act)
    axes, turned, orders, swapped = (X, X, Y, Y), (Y, Y, X, X), (0, 1, 0, 1), (1, 0, 1, 0)
    parts = (last_parts, middle_parts, first_parts[0:2], first_parts[2:4])
    parts = [halve(part, 4) for part in exchange(parts, axes, orders)]
    parts = [
        turn(part, turned[i], orders[i]) for i, part in enumerate(exchange(parts, axes, swapped))
    ]
    parts = [halve(part) for part in exchange(parts, turned, orders)]
    last_parts, middle_parts, *first_parts = exchange(parts, turned, swapped)
    parts = (*first_parts[0], *first_parts[1], *last_parts, *middle_parts)
    sent, own = call(
        z_cut_kernel,
        "z_cut",
        [SMEM] + [VMEM] * 8,
        [granules(8), granules(8, kind=F32)],
        [pltpu.VMEM((4, ROWS, COLS), F32)] * 2,
    )(place, *parts)

    total, squares = call(
        square_kernel, "square", [VMEM] * 2, [((8, ROWS, COLS), F32), ((128, 1, LANES), F32)]
    )(own, swap(sent, ZH))
    squares = lax.all_to_all(squares, ALL, 0, 0, tiled=True)
    grad_first, grad_middle, grad_last = call(
        scale_kernel,
        "scale",
        [VMEM] * 2,
        [((units // 64, inputs), F32), ((ROWS, units), F32), ((ROWS, width), F32)],
        kind=jax.ShapeDtypeStruct,
    )(total, squares)
    return grad_first.T, grad_middle.T, grad_last


def solution(mesh):
    finer = Mesh(mesh.devices.reshape(4, 2, 4, 2, mesh.shape["mp"]), ALL)
    return jax.shard_map(
        per_device,
        mesh=finer,
        in_specs=(P(DP, None), P(DP, None), P(DP), P(None, "mp"), P("mp", None), P(None, "mp")),
        out_specs=(P(None, MP_DP), P("mp", DP), P(DP, "mp")),
        check_vma=False,
    )
```

```python
import functools

import jax
import jax.numpy as jnp
import numpy as np
from jax import lax
from jax.experimental import pallas as pl
from jax.experimental.pallas import tpu as pltpu
from jax.sharding import Mesh
from jax.sharding import PartitionSpec as P

BLOCK = 128
PARAMS = 8469504
DP = ("dp_0", "dp_1", "dp_2", "dp_3")
MP_DP = ("mp", "dp_0", "dp_1", "dp_2", "dp_3")
ALL = DP + ("mp",)
Y, ZH, X, CORE = DP
LANES = 128
ROWS, COLS = 24, 384
SIZE, SECOND = 344, 320
DEPTH = 512
VMEM = pl.BlockSpec(memory_space=pltpu.VMEM)
SMEM = pl.BlockSpec(memory_space=pltpu.SMEM)
HBM = pl.BlockSpec(memory_space=pl.ANY)
BF16, F32 = jnp.bfloat16, jnp.float32


def wide(shard):
    return shard.astype(F32)


def narrow(shard):
    return shard.astype(BF16)


def swap(shard, axis):
    return lax.ppermute(shard, axis, [(0, 1), (1, 0)])


def to_pair(shard, axis, order):
    pairs = [(i, i ^ 1) for i in range(4)] if order == 0 else [(i, 3 - i) for i in range(4)]
    return lax.ppermute(shard, axis, pairs)


def silu_slope(pre_act):
    sigmoid_of = 1.0 / (1.0 + jnp.exp(-pre_act))
    return sigmoid_of * (1.0 + pre_act * (1.0 - sigmoid_of))


def dot(left, right):
    return jnp.dot(left, right, preferred_element_type=F32)


def contract(left, right, left_dim, right_dim):
    return lax.dot_general(
        left, right, (((left_dim,), (right_dim,)), ((), ())), preferred_element_type=F32
    )


def call(body, name, in_specs, outs, scratch=(), kind=pltpu.VMEM, far=0):
    kernel = pl.pallas_call(
        body,
        out_shape=[(pltpu.HBM if i < far else kind)(*out) for i, out in enumerate(outs)],
        in_specs=in_specs,
        out_specs=[HBM if i < far else VMEM for i in range(len(outs))],
        scratch_shapes=list(scratch),
        compiler_params=pltpu.CompilerParams(vmem_limit_bytes=24 << 20),
        cost_estimate=pl.CostEstimate(flops=1 << 34, bytes_accessed=1 << 26, transcendentals=0),
        name=name,
    )

    def run(*operands):
        return kernel(
            *(
                operand if spec is SMEM else pltpu.with_memory_space_constraint(
                    operand, pltpu.VMEM if spec is VMEM else pltpu.HBM
                )
                for operand, spec in zip(operands, in_specs)
            )
        )

    return run


def rows_of_core(rows_ref, core, out_ref):
    for block in range(32):
        y, x, z_hi = block // 8, block // 2 % 4, block % 2
        first = 2 * ROWS * ((2 * y + z_hi) * 4 + x)
        rows = pl.ds(pl.multiple_of(first + ROWS * core, 8), ROWS)
        out_ref[ROWS * block : ROWS * (block + 1), :] = narrow(rows_ref[rows, :])


def forward_kernel(
    belief_hbm, w_first_hbm, w_middle_hbm, pre_first_hbm, act_first_hbm, sent_ref,
    belief, w_first, w_middle, pre_first_ref, act_first_ref, sems,
):
    inputs = belief.shape[0]
    cuts = [(start, min(start + DEPTH, inputs)) for start in range(0, inputs, DEPTH)]
    copies = []
    for i, (start, stop) in enumerate(cuts):
        rows = pl.ds(start, stop - start)
        copies.append(
            (
                pltpu.make_async_copy(belief_hbm.at[rows], belief.at[rows], sems.at[2 * i]),
                pltpu.make_async_copy(w_first_hbm.at[rows], w_first.at[rows], sems.at[2 * i + 1]),
            )
        )
    copies.append((pltpu.make_async_copy(w_middle_hbm, w_middle, sems.at[2 * len(cuts)]),))
    for pair in copies:
        for copy in pair:
            copy.start()
    results = (
        pltpu.make_async_copy(pre_first_ref, pre_first_hbm, sems.at[2 * len(cuts) + 1]),
        pltpu.make_async_copy(act_first_ref, act_first_hbm, sems.at[2 * len(cuts) + 2]),
    )
    pre_first = jnp.zeros(pre_first_ref.shape, F32)
    for (start, stop), pair in zip(cuts, copies):
        for copy in pair:
            copy.wait()
        pre_first += contract(belief[start:stop, :], w_first[start:stop, :], 0, 0)
    pre_first_ref[...] = pre_first
    results[0].start()
    act_first = narrow(pre_first / (1.0 + jnp.exp(-pre_first)))
    act_first_ref[...] = act_first
    results[1].start()
    copies[-1][0].wait()
    sent_ref[...] = narrow(dot(act_first, w_middle[...]))
    for copy in results:
        copy.wait()


def half_kernel(place_ref, w_last_hbm, half_ref, last_ref, sem):
    size, total = half_ref.shape[0], w_last_hbm.shape[0]

    @pl.when(place_ref[0] == 0)
    def _():
        copy = pltpu.make_async_copy(w_last_hbm.at[pl.ds(0, size)], half_ref, sem)
        copy.start()
        copy.wait()

    @pl.when(place_ref[0] != 0)
    def _():
        copy = pltpu.make_async_copy(w_last_hbm.at[pl.ds(SECOND, total - SECOND)], last_ref, sem)
        copy.start()
        half_ref[size - 8 :, :] = jnp.zeros((8, half_ref.shape[1]), half_ref.dtype)
        copy.wait()
        half_ref[0 : total - SECOND, :] = last_ref[...]


def stage_kernel(
    place_ref, counts_ref, pre_first_ref, orders_ref, target_hbm, w_last_hbm,
    w_own_ref, target_own_ref, target_other_ref, first_slope_ref, onehot_ref, live_ref,
    target_ref, sems,
):
    copies = (
        pltpu.make_async_copy(target_hbm, target_ref, sems.at[0]),
        pltpu.make_async_copy(w_last_hbm, w_own_ref, sems.at[1]),
    )
    for copy in copies:
        copy.start()
    first_slope_ref[...] = silu_slope(pre_first_ref[...])
    order = jnp.where(place_ref[0] == 0, orders_ref[0], orders_ref[1])
    units = lax.broadcasted_iota(jnp.int32, onehot_ref.shape, 1)
    onehot_ref[...] = jnp.where(order == units, 1.0, 0.0).astype(BF16)
    row = lax.broadcasted_iota(jnp.int32, live_ref.shape, 1)
    count = jnp.where(row < BLOCK, counts_ref[0], counts_ref[1] + BLOCK)
    live_ref[...] = jnp.where(row < count, 1.0, 0.0)
    copies[0].wait()
    width = target_own_ref.shape[0]
    low, high = target_ref[0:width, :], target_ref[width : 2 * width, :]
    is_low = place_ref[4] == 0
    target_own_ref[...] = jnp.where(is_low, low, high)
    other = jnp.where(is_low, high, low)
    size = target_other_ref.shape[1]
    for side in range(2):

        @pl.when(place_ref[0] == side)
        def _():
            target_other_ref[side] = other[0:size]
            target_other_ref[1 - side, size - 8 :, :] = jnp.zeros((8, other.shape[1]), other.dtype)
            target_other_ref[1 - side, 0 : width - SECOND, :] = other[SECOND:]

    copies[1].wait()


def hidden_kernel(
    place_ref, partial_ref, arrived_ref, live_ref, target_ref, w_ref,
    act_ref, act_slope_ref, back_ref, sent_ref, own_ref, rows_ref,
):
    core = place_ref[0]
    pre_middle = wide(partial_ref[...]) + wide(arrived_ref[...])
    sigmoid_of = 1.0 / (1.0 + jnp.exp(-pre_middle))
    act = narrow(pre_middle * sigmoid_of)
    act_ref[...] = act
    act_slope_ref[...] = sigmoid_of * (1.0 + pre_middle * (1.0 - sigmoid_of))
    slope = slope_of(w_ref[...], act, target_ref[...], live_ref[...])
    half = own_ref.shape[0]
    sent_ref[half:, :] = slope
    back_ref[...] = contract(slope, w_ref[...], 0, 0)
    rows_ref[...] = wide(act).T
    rows_of_core(rows_ref, 1 - core, sent_ref)
    rows_of_core(rows_ref, core, own_ref)


def slope_of(weights, act, target, live):
    mismatch = contract(weights, act, 1, 1) - wide(target)
    return narrow(jnp.clip(mismatch, -1.0, 1.0) * live)


def slopes_kernel(
    place_ref, act_ref, act_slope_ref, back_ref, live_ref, target_ref, first_slope_ref,
    onehot_ref, fetched_ref, relayed_ref, w_middle_ref, sent_ref, own_ref, rows_ref,
):
    core = place_ref[0]
    act, live = act_ref[...], live_ref[...]
    back = back_ref[...]
    for side, w_ref in enumerate((fetched_ref, relayed_ref)):
        weights = w_ref[...]
        slope = slope_of(weights, act, target_ref[side], live)
        repeated = jnp.where(core == side, 0, SIZE - SECOND)
        column = lax.broadcasted_iota(jnp.int32, slope.shape, 0)
        slope = jnp.where(column >= repeated, slope, jnp.zeros_like(slope))
        back += contract(slope, weights, 0, 0)
    slope_middle = narrow(back * act_slope_ref[...])
    slope_first = narrow(contract(slope_middle, w_middle_ref[...], 1, 1) * first_slope_ref[...])
    slope_first = narrow(contract(onehot_ref[...], slope_first, 1, 1))
    half = slope_first.shape[0] // 2
    sent_ref[2 * half :, :] = slope_first[:half]
    own_ref[2 * half :, :] = slope_first[half:]
    rows_ref[...] = wide(slope_middle).T
    rows_of_core(rows_ref, 1 - core, sent_ref)
    rows_of_core(rows_ref, core, own_ref)


def column_cuts(width):
    return [(start, min(start + COLS, width)) for start in range(0, width, COLS)]


def put_columns(raw, granule, out_ref):
    width = raw.shape[1]
    if width < COLS:
        raw = jnp.concatenate([raw, jnp.zeros((raw.shape[0], COLS - width), raw.dtype)], 1)
    for unit in range(16):
        out_ref[unit, granule] = raw[unit * ROWS : (unit + 1) * ROWS]


def kept_and_sent(me, order):
    near, far, opposite = lax.bitwise_xor(me, 1), 3 - me, lax.bitwise_xor(me, 2)
    return ((me, far), (near, opposite)) if order == 0 else ((me, near), (far, opposite))


def cut_rows(raw_ref, me, order, kept_ref, sent_ref):
    for out_ref, blocks in zip((kept_ref, sent_ref), kept_and_sent(me, order)):
        for position, x in enumerate(blocks):
            for y in range(4):
                for granule in range(4):
                    first = ROWS * (2 * (4 * y + x) + granule // 2)
                    columns = slice(granule % 2 * COLS, (granule % 2 + 1) * COLS)
                    rows = raw_ref[pl.ds(pl.multiple_of(first, 8), ROWS), columns]
                    out_ref[position, y, granule] = rows.astype(out_ref.dtype)


def last_kernel(place_ref, own_ref, sent_ref, arrived_ref, kept_out, sent_out, raw_ref, padded_ref):
    half = own_ref.shape[0]
    width = sent_ref.shape[0] - half
    padded_ref[...] = jnp.zeros_like(padded_ref)
    padded_ref[0, 0:width, :] = sent_ref[half:, :]
    padded_ref[1, 0:width, :] = arrived_ref[half:, :]
    raw_ref[...] = contract(own_ref[...], padded_ref[0], 1, 1) + contract(
        arrived_ref[0:half, :], padded_ref[1], 1, 1
    )
    cut_rows(raw_ref, place_ref[2], 0, kept_out, sent_out)


def middle_kernel(
    place_ref, own_ref, arrived_ref, act_ref, sibling_act_ref, kept_out, sent_out, raw_ref
):
    half = raw_ref.shape[0]
    raw_ref[...] = dot(own_ref[0:half, :], act_ref[...]) + dot(
        arrived_ref[0:half, :], sibling_act_ref[...]
    )
    cut_rows(raw_ref, place_ref[2], 1, kept_out, sent_out)


def first_kernel(place_ref, own_ref, arrived_ref, belief_ref, sibling_belief_ref, *refs):
    raw_ref = refs[-1]
    start_row = own_ref.shape[0] // 3 * 2
    own, arrived = own_ref[start_row:, :], arrived_ref[start_row:, :]
    for start, stop in column_cuts(belief_ref.shape[0]):
        raw = contract(own, belief_ref[start:stop, :], 1, 1) + contract(
            arrived, sibling_belief_ref[start:stop, :], 1, 1
        )
        put_columns(raw, start // COLS, raw_ref)
    for order, part in enumerate((slice(0, 3), slice(3, 7))):
        for side, blocks in enumerate(kept_and_sent(place_ref[1], order)):
            out_ref = refs[2 * order + side]
            for position, y in enumerate(blocks):
                for x in range(4):
                    out_ref[position, x] = raw_ref[4 * y + x, part].astype(out_ref.dtype)


def halve_kernel(kept_ref, arrived_ref, kept_out, sent_out):
    kept_out[...] = kept_ref[0] + wide(arrived_ref[0])
    sent_out[...] = narrow(kept_ref[1] + wide(arrived_ref[1]))


def turn_kernel(axis, order, place_ref, kept_ref, arrived_ref, kept_out, sent_out):
    for out_ref, blocks in zip((kept_out, sent_out), kept_and_sent(place_ref[axis], order)):
        for position, block in enumerate(blocks):
            total = kept_ref[block] + wide(arrived_ref[block])
            out_ref[position] = total.astype(out_ref.dtype)


def z_cut_kernel(place_ref, *refs):
    sent_ref, own_ref, last_sum, middle_sum = refs[8:12]
    z_hi = place_ref[3]
    low, high, last, middle = (
        refs[2 * part][...] + wide(refs[2 * part + 1][...]) for part in range(4)
    )
    last_sum[...] = last
    middle_sum[...] = middle
    rows = [low[granule] for granule in range(3)] + [high[granule] for granule in range(4)]
    for side, out_ref in ((1 - z_hi, sent_ref), (z_hi, own_ref)):
        kind = out_ref.dtype
        out_ref[0:2] = last_sum[pl.ds(2 * side, 2)].astype(kind)
        out_ref[2:4] = middle_sum[pl.ds(2 * side, 2)].astype(kind)
        halves = [jnp.where(side == 0, row[0:12], row[12:24]) for row in rows]
        halves.append(jnp.zeros_like(halves[0]))
        for pair in range(4):
            out_ref[4 + pair] = jnp.concatenate(halves[2 * pair : 2 * pair + 2], 0).astype(kind)


def square_kernel(own_ref, arrived_ref, total_ref, squares_ref):
    total = own_ref[...] + wide(arrived_ref[...])
    total_ref[...] = total
    squares_ref[...] = jnp.broadcast_to(jnp.sum(total * total), squares_ref.shape)


def scale_kernel(total_ref, squares_ref, first_ref, middle_ref, last_ref):
    square_sum = jnp.sum(squares_ref[...], axis=0)
    norm_scale = lax.rsqrt(square_sum / PARAMS + 1e-06)
    norm_scale = jnp.concatenate([norm_scale] * 3, 1)
    for ref, start in ((last_ref, 0), (middle_ref, 2)):
        for half in range(2):
            columns = slice(half * COLS, min((half + 1) * COLS, ref.shape[1]))
            width = columns.stop - columns.start
            ref[:, columns] = (total_ref[start + half] * norm_scale)[:, :width]
    for granule, (start, stop) in enumerate(column_cuts(first_ref.shape[1])):
        row = granule % 2 * 12
        scaled = total_ref[4 + granule // 2, row : row + 12] * norm_scale
        first_ref[:, start:stop] = scaled[:, : stop - start]


def granules(*lead, kind=BF16):
    return ((*lead, ROWS, COLS), kind)


def per_device(belief, target_value, counts, w_first, w_middle, w_last):
    total_rows, inputs = belief.shape
    width = w_last.shape[1]
    units = w_first.shape[1]
    hidden = w_middle.shape[1]
    belief_t, w_last_t = belief.T, w_last.T

    indices = (CORE, Y, X, ZH, "mp")
    place = jnp.stack([lax.axis_index(axis) for axis in indices])

    (half,) = call(
        half_kernel,
        "half",
        [SMEM, HBM],
        [((SIZE, hidden), BF16)],
        [pltpu.VMEM((width - SECOND, hidden), BF16), pltpu.SemaphoreType.DMA],
    )(place, w_last_t)
    fetched = lax.ppermute(half, (ZH, "mp"), [(0, 3), (3, 0), (1, 2), (2, 1)])
    belief_first, half = lax.optimization_barrier((belief_t, half))

    pre_first, act_first, hidden_sent = call(
        forward_kernel,
        "forward",
        [HBM] * 3,
        [
            ((total_rows, units), F32),
            ((total_rows, units), BF16),
            ((total_rows, hidden), BF16),
        ],
        [
            pltpu.VMEM((inputs, total_rows), BF16),
            pltpu.VMEM((inputs, units), BF16),
            pltpu.VMEM((units, hidden), BF16),
            pltpu.VMEM((total_rows, units), F32),
            pltpu.VMEM((total_rows, units), BF16),
            pltpu.SemaphoreType.DMA((2 * pl.cdiv(inputs, DEPTH) + 3,)),
        ],
        far=2,
    )(belief_first, w_first, w_middle)
    arrived = swap(hidden_sent, "mp")

    order = np.arange(units, dtype=np.int32).reshape(4, 2, 4, 2, -1).transpose(3, 0, 2, 1, 4)
    orders = np.stack([order[::-1], order]).reshape(2, units, 1)
    w_own, target_own, target_other, first_slope, onehot, live = call(
        stage_kernel,
        "stage",
        [SMEM, SMEM, VMEM, VMEM, HBM, HBM],
        [
            ((width, hidden), BF16),
            ((width, total_rows), BF16),
            ((2, SIZE, total_rows), BF16),
            ((total_rows, units), F32),
            ((units, units), BF16),
            ((1, total_rows), F32),
        ],
        [pltpu.VMEM((2 * width, total_rows), BF16), pltpu.SemaphoreType.DMA((2,))],
    )(place, counts, pre_first, jnp.asarray(orders), target_value.T, w_last_t)
    fetched, live = lax.optimization_barrier((fetched, live))
    relayed = swap(fetched, CORE)
    belief_swapped, act_swapped = lax.optimization_barrier((belief_t, act_first))
    sibling_belief = swap(belief_swapped, CORE)
    sibling_act = swap(act_swapped, CORE)

    act, act_slope, back_own, last_sent, last_own = call(
        hidden_kernel,
        "hidden",
        [SMEM] + [VMEM] * 5,
        [
            ((total_rows, hidden), BF16),
            ((total_rows, hidden), F32),
            ((total_rows, hidden), F32),
            ((hidden // 2 + width, total_rows), BF16),
            ((hidden // 2, total_rows), BF16),
        ],
        [pltpu.VMEM((hidden, total_rows), F32)],
    )(place, hidden_sent, arrived, live, target_own, w_own)
    last_arrived = swap(last_sent, CORE)

    slopes_sent, slopes_own = call(
        slopes_kernel,
        "slopes",
        [SMEM] + [VMEM] * 10,
        [((hidden // 2 + units // 2, total_rows), BF16)] * 2,
        [pltpu.VMEM((hidden, total_rows), F32)],
    )(
        place, act, act_slope, back_own, live, target_other, first_slope, onehot,
        fetched, relayed, w_middle,
    )
    slopes_arrived = swap(slopes_sent, CORE)

    def pairs(*sizes):
        return [out for size in sizes for out in (granules(*size, kind=F32), granules(*size))]

    def exchange(parts, axes, orders):
        sent = [part[1] for part in parts]
        arrived = [to_pair(*sending) for sending in zip(sent, axes, orders)]
        return [
            (part[0], lax.optimization_barrier((coming, *sent))[0])
            for part, coming in zip(parts, arrived)
        ]

    def halve(part, *lead):
        return call(halve_kernel, "halve", [VMEM] * 2, pairs((*lead, part[0].shape[-3])))(*part)

    def turn(part, axis, order):
        size = part[0].shape[-3]
        return call(
            functools.partial(turn_kernel, 1 if axis == Y else 2, order),
            "turn",
            [SMEM] + [VMEM] * 2,
            pairs((2, size)),
        )(place, *part)

    raw = pltpu.VMEM((hidden // 2, units), F32)
    last_own, slopes_own = lax.optimization_barrier((last_own, slopes_own))
    last_parts = call(
        last_kernel,
        "last",
        [SMEM] + [VMEM] * 3,
        pairs((2, 4, 4)),
        [raw, pltpu.VMEM((2, units, total_rows), BF16)],
    )(place, last_own, last_sent, last_arrived)
    middle_parts = call(
        middle_kernel, "middle", [SMEM] + [VMEM] * 4, pairs((2, 4, 4)), [raw]
    )(place, slopes_own, slopes_arrived, act_first, sibling_act)
    slopes_own, _ = lax.optimization_barrier((slopes_own, middle_parts[1]))
    first_parts = call(
        first_kernel,
        "first",
        [SMEM] + [VMEM] * 4,
        pairs((2, 4, 3), (2, 4, 4)),
        [pltpu.VMEM((16, 7, ROWS, COLS), F32)],
    )(place, slopes_own, slopes_arrived, belief_t, sibling_belief)
    axes, turned, orders, swapped = (X, X, Y, Y), (Y, Y, X, X), (0, 1, 0, 1), (1, 0, 1, 0)
    parts = (last_parts, middle_parts, first_parts[0:2], first_parts[2:4])
    parts = [halve(part, 4) for part in exchange(parts, axes, orders)]
    parts = [
        turn(part, turned[i], orders[i]) for i, part in enumerate(exchange(parts, axes, swapped))
    ]
    parts = [halve(part) for part in exchange(parts, turned, orders)]
    last_parts, middle_parts, *first_parts = exchange(parts, turned, swapped)
    parts = (*first_parts[0], *first_parts[1], *last_parts, *middle_parts)
    sent, own = call(
        z_cut_kernel,
        "z_cut",
        [SMEM] + [VMEM] * 8,
        [granules(8), granules(8, kind=F32)],
        [pltpu.VMEM((4, ROWS, COLS), F32)] * 2,
    )(place, *parts)

    total, squares = call(
        square_kernel, "square", [VMEM] * 2, [((8, ROWS, COLS), F32), ((128, 1, LANES), F32)]
    )(own, swap(sent, ZH))
    squares = lax.all_to_all(squares, ALL, 0, 0, tiled=True)
    grad_first, grad_middle, grad_last = call(
        scale_kernel,
        "scale",
        [VMEM] * 2,
        [((units // 64, inputs), F32), ((ROWS, units), F32), ((ROWS, width), F32)],
        kind=jax.ShapeDtypeStruct,
    )(total, squares)
    return grad_first.T, grad_middle.T, grad_last


def solution(mesh):
    finer = Mesh(mesh.devices.reshape(4, 2, 4, 2, mesh.shape["mp"]), ALL)
    return jax.shard_map(
        per_device,
        mesh=finer,
        in_specs=(P(DP, None), P(DP, None), P(DP), P(None, "mp"), P("mp", None), P(None, "mp")),
        out_specs=(P(None, MP_DP), P("mp", DP), P(DP, "mp")),
        check_vma=False,
    )
```

```python
import functools

import jax
import jax.numpy as jnp
import numpy as np
from jax import lax
from jax.experimental import pallas as pl
from jax.experimental.pallas import tpu as pltpu
from jax.sharding import Mesh
from jax.sharding import PartitionSpec as P

BLOCK = 128
PARAMS = 8469504
DP = ("dp_0", "dp_1", "dp_2", "dp_3")
MP_DP = ("mp", "dp_0", "dp_1", "dp_2", "dp_3")
ALL = DP + ("mp",)
Y, ZH, X, CORE = DP
LANES = 128
ROWS, COLS = 24, 384
SIZE, SECOND = 344, 320
DEPTH = 512
VMEM = pl.BlockSpec(memory_space=pltpu.VMEM)
SMEM = pl.BlockSpec(memory_space=pltpu.SMEM)
HBM = pl.BlockSpec(memory_space=pl.ANY)
BF16, F32 = jnp.bfloat16, jnp.float32


def wide(shard):
    return shard.astype(F32)


def narrow(shard):
    return shard.astype(BF16)


def swap(shard, axis):
    return lax.ppermute(shard, axis, [(0, 1), (1, 0)])


def to_pair(shard, axis, order):
    pairs = [(i, i ^ 1) for i in range(4)] if order == 0 else [(i, 3 - i) for i in range(4)]
    return lax.ppermute(shard, axis, pairs)


def silu_slope(pre_act):
    sigmoid_of = 1.0 / (1.0 + jnp.exp(-pre_act))
    return sigmoid_of * (1.0 + pre_act * (1.0 - sigmoid_of))


def dot(left, right):
    return jnp.dot(left, right, preferred_element_type=F32)


def contract(left, right, left_dim, right_dim):
    return lax.dot_general(
        left, right, (((left_dim,), (right_dim,)), ((), ())), preferred_element_type=F32
    )


def call(body, name, in_specs, outs, scratch=(), kind=pltpu.VMEM, far=0):
    kernel = pl.pallas_call(
        body,
        out_shape=[(pltpu.HBM if i < far else kind)(*out) for i, out in enumerate(outs)],
        in_specs=in_specs,
        out_specs=[HBM if i < far else VMEM for i in range(len(outs))],
        scratch_shapes=list(scratch),
        compiler_params=pltpu.CompilerParams(vmem_limit_bytes=24 << 20),
        cost_estimate=pl.CostEstimate(flops=1 << 34, bytes_accessed=1 << 26, transcendentals=0),
        name=name,
    )

    def run(*operands):
        return kernel(
            *(
                operand if spec is SMEM else pltpu.with_memory_space_constraint(
                    operand, pltpu.VMEM if spec is VMEM else pltpu.HBM
                )
                for operand, spec in zip(operands, in_specs)
            )
        )

    return run


def rows_of_core(rows_ref, core, out_ref):
    for block in range(32):
        y, x, z_hi = block // 8, block // 2 % 4, block % 2
        first = 2 * ROWS * ((2 * y + z_hi) * 4 + x)
        rows = pl.ds(pl.multiple_of(first + ROWS * core, 8), ROWS)
        out_ref[ROWS * block : ROWS * (block + 1), :] = narrow(rows_ref[rows, :])


def forward_kernel(
    belief_hbm, w_first_hbm, w_middle_hbm, pre_first_hbm, act_first_hbm, sent_ref,
    belief, w_first, w_middle, pre_first_ref, act_first_ref, sems,
):
    inputs = belief.shape[0]
    cuts = [(start, min(start + DEPTH, inputs)) for start in range(0, inputs, DEPTH)]
    copies = []
    for i, (start, stop) in enumerate(cuts):
        rows = pl.ds(start, stop - start)
        copies.append(
            (
                pltpu.make_async_copy(belief_hbm.at[rows], belief.at[rows], sems.at[2 * i]),
                pltpu.make_async_copy(w_first_hbm.at[rows], w_first.at[rows], sems.at[2 * i + 1]),
            )
        )
    copies.append((pltpu.make_async_copy(w_middle_hbm, w_middle, sems.at[2 * len(cuts)]),))
    for pair in copies:
        for copy in pair:
            copy.start()
    results = (
        pltpu.make_async_copy(pre_first_ref, pre_first_hbm, sems.at[2 * len(cuts) + 1]),
        pltpu.make_async_copy(act_first_ref, act_first_hbm, sems.at[2 * len(cuts) + 2]),
    )
    pre_first = jnp.zeros(pre_first_ref.shape, F32)
    for (start, stop), pair in zip(cuts, copies):
        for copy in pair:
            copy.wait()
        pre_first += contract(belief[start:stop, :], w_first[start:stop, :], 0, 0)
    pre_first_ref[...] = pre_first
    results[0].start()
    act_first = narrow(pre_first / (1.0 + jnp.exp(-pre_first)))
    act_first_ref[...] = act_first
    results[1].start()
    copies[-1][0].wait()
    sent_ref[...] = narrow(dot(act_first, w_middle[...]))
    for copy in results:
        copy.wait()


def half_kernel(place_ref, w_last_hbm, half_ref, last_ref, sem):
    size, total = half_ref.shape[0], w_last_hbm.shape[0]

    @pl.when(place_ref[0] == 0)
    def _():
        copy = pltpu.make_async_copy(w_last_hbm.at[pl.ds(0, size)], half_ref, sem)
        copy.start()
        copy.wait()

    @pl.when(place_ref[0] != 0)
    def _():
        copy = pltpu.make_async_copy(w_last_hbm.at[pl.ds(SECOND, total - SECOND)], last_ref, sem)
        copy.start()
        half_ref[size - 8 :, :] = jnp.zeros((8, half_ref.shape[1]), half_ref.dtype)
        copy.wait()
        half_ref[0 : total - SECOND, :] = last_ref[...]


def stage_kernel(
    place_ref, counts_ref, pre_first_ref, orders_ref, target_hbm, w_last_hbm,
    w_own_ref, target_own_ref, target_other_ref, first_slope_ref, onehot_ref, live_ref,
    target_ref, sems,
):
    copies = (
        pltpu.make_async_copy(target_hbm, target_ref, sems.at[0]),
        pltpu.make_async_copy(w_last_hbm, w_own_ref, sems.at[1]),
    )
    for copy in copies:
        copy.start()
    first_slope_ref[...] = silu_slope(pre_first_ref[...])
    order = jnp.where(place_ref[0] == 0, orders_ref[0], orders_ref[1])
    units = lax.broadcasted_iota(jnp.int32, onehot_ref.shape, 1)
    onehot_ref[...] = jnp.where(order == units, 1.0, 0.0).astype(BF16)
    row = lax.broadcasted_iota(jnp.int32, live_ref.shape, 1)
    count = jnp.where(row < BLOCK, counts_ref[0], counts_ref[1] + BLOCK)
    live_ref[...] = jnp.where(row < count, 1.0, 0.0)
    copies[0].wait()
    width = target_own_ref.shape[0]
    low, high = target_ref[0:width, :], target_ref[width : 2 * width, :]
    is_low = place_ref[4] == 0
    target_own_ref[...] = jnp.where(is_low, low, high)
    other = jnp.where(is_low, high, low)
    size = target_other_ref.shape[1]
    for side in range(2):

        @pl.when(place_ref[0] == side)
        def _():
            target_other_ref[side] = other[0:size]
            target_other_ref[1 - side, size - 8 :, :] = jnp.zeros((8, other.shape[1]), other.dtype)
            target_other_ref[1 - side, 0 : width - SECOND, :] = other[SECOND:]

    copies[1].wait()


def hidden_kernel(
    place_ref, partial_ref, arrived_ref, live_ref, target_ref, w_ref,
    act_ref, act_slope_ref, back_ref, sent_ref, own_ref, rows_ref,
):
    core = place_ref[0]
    pre_middle = wide(partial_ref[...]) + wide(arrived_ref[...])
    sigmoid_of = 1.0 / (1.0 + jnp.exp(-pre_middle))
    act = narrow(pre_middle * sigmoid_of)
    act_ref[...] = act
    act_slope_ref[...] = sigmoid_of * (1.0 + pre_middle * (1.0 - sigmoid_of))
    slope = slope_of(w_ref[...], act, target_ref[...], live_ref[...])
    half = own_ref.shape[0]
    sent_ref[half:, :] = slope
    back_ref[...] = contract(slope, w_ref[...], 0, 0)
    rows_ref[...] = wide(act).T
    rows_of_core(rows_ref, 1 - core, sent_ref)
    rows_of_core(rows_ref, core, own_ref)


def slope_of(weights, act, target, live):
    mismatch = contract(weights, act, 1, 1) - wide(target)
    return narrow(jnp.clip(mismatch, -1.0, 1.0) * live)


def slopes_kernel(
    place_ref, act_ref, act_slope_ref, back_ref, live_ref, target_ref, first_slope_ref,
    onehot_ref, fetched_ref, relayed_ref, w_middle_ref, sent_ref, own_ref, rows_ref,
):
    core = place_ref[0]
    act, live = act_ref[...], live_ref[...]
    back = back_ref[...]
    for side, w_ref in enumerate((fetched_ref, relayed_ref)):
        weights = w_ref[...]
        slope = slope_of(weights, act, target_ref[side], live)
        repeated = jnp.where(core == side, 0, SIZE - SECOND)
        column = lax.broadcasted_iota(jnp.int32, slope.shape, 0)
        slope = jnp.where(column >= repeated, slope, jnp.zeros_like(slope))
        back += contract(slope, weights, 0, 0)
    slope_middle = narrow(back * act_slope_ref[...])
    slope_first = narrow(contract(slope_middle, w_middle_ref[...], 1, 1) * first_slope_ref[...])
    slope_first = narrow(contract(onehot_ref[...], slope_first, 1, 1))
    half = slope_first.shape[0] // 2
    sent_ref[2 * half :, :] = slope_first[:half]
    own_ref[2 * half :, :] = slope_first[half:]
    rows_ref[...] = wide(slope_middle).T
    rows_of_core(rows_ref, 1 - core, sent_ref)
    rows_of_core(rows_ref, core, own_ref)


def column_cuts(width):
    return [(start, min(start + COLS, width)) for start in range(0, width, COLS)]


def put_columns(raw, granule, out_ref):
    width = raw.shape[1]
    if width < COLS:
        raw = jnp.concatenate([raw, jnp.zeros((raw.shape[0], COLS - width), raw.dtype)], 1)
    for unit in range(16):
        out_ref[unit, granule] = raw[unit * ROWS : (unit + 1) * ROWS]


def kept_and_sent(me, order):
    near, far, opposite = lax.bitwise_xor(me, 1), 3 - me, lax.bitwise_xor(me, 2)
    return ((me, far), (near, opposite)) if order == 0 else ((me, near), (far, opposite))


def cut_rows(raw_ref, me, order, kept_ref, sent_ref):
    for out_ref, blocks in zip((kept_ref, sent_ref), kept_and_sent(me, order)):
        for position, x in enumerate(blocks):
            for y in range(4):
                for granule in range(4):
                    first = ROWS * (2 * (4 * y + x) + granule // 2)
                    columns = slice(granule % 2 * COLS, (granule % 2 + 1) * COLS)
                    rows = raw_ref[pl.ds(pl.multiple_of(first, 8), ROWS), columns]
                    out_ref[position, y, granule] = rows.astype(out_ref.dtype)


def last_kernel(place_ref, own_ref, sent_ref, arrived_ref, kept_out, sent_out, raw_ref, padded_ref):
    half = own_ref.shape[0]
    width = sent_ref.shape[0] - half
    padded_ref[...] = jnp.zeros_like(padded_ref)
    padded_ref[0, 0:width, :] = sent_ref[half:, :]
    padded_ref[1, 0:width, :] = arrived_ref[half:, :]
    raw_ref[...] = contract(own_ref[...], padded_ref[0], 1, 1) + contract(
        arrived_ref[0:half, :], padded_ref[1], 1, 1
    )
    cut_rows(raw_ref, place_ref[2], 0, kept_out, sent_out)


def middle_kernel(
    place_ref, own_ref, arrived_ref, act_ref, sibling_act_ref, kept_out, sent_out, raw_ref
):
    half = raw_ref.shape[0]
    raw_ref[...] = dot(own_ref[0:half, :], act_ref[...]) + dot(
        arrived_ref[0:half, :], sibling_act_ref[...]
    )
    cut_rows(raw_ref, place_ref[2], 1, kept_out, sent_out)


def first_kernel(place_ref, own_ref, arrived_ref, belief_ref, sibling_belief_ref, *refs):
    raw_ref = refs[-1]
    start_row = own_ref.shape[0] // 3 * 2
    own, arrived = own_ref[start_row:, :], arrived_ref[start_row:, :]
    for start, stop in column_cuts(belief_ref.shape[0]):
        raw = contract(own, belief_ref[start:stop, :], 1, 1) + contract(
            arrived, sibling_belief_ref[start:stop, :], 1, 1
        )
        put_columns(raw, start // COLS, raw_ref)
    for order, part in enumerate((slice(0, 3), slice(3, 7))):
        for side, blocks in enumerate(kept_and_sent(place_ref[1], order)):
            out_ref = refs[2 * order + side]
            for position, y in enumerate(blocks):
                for x in range(4):
                    out_ref[position, x] = raw_ref[4 * y + x, part].astype(out_ref.dtype)


def halve_kernel(kept_ref, arrived_ref, kept_out, sent_out):
    kept_out[...] = kept_ref[0] + wide(arrived_ref[0])
    sent_out[...] = narrow(kept_ref[1] + wide(arrived_ref[1]))


def turn_kernel(axis, order, place_ref, kept_ref, arrived_ref, kept_out, sent_out):
    for out_ref, blocks in zip((kept_out, sent_out), kept_and_sent(place_ref[axis], order)):
        for position, block in enumerate(blocks):
            total = kept_ref[block] + wide(arrived_ref[block])
            out_ref[position] = total.astype(out_ref.dtype)


def z_cut_kernel(place_ref, *refs):
    sent_ref, own_ref, last_sum, middle_sum = refs[8:12]
    z_hi = place_ref[3]
    low, high, last, middle = (
        refs[2 * part][...] + wide(refs[2 * part + 1][...]) for part in range(4)
    )
    last_sum[...] = last
    middle_sum[...] = middle
    rows = [low[granule] for granule in range(3)] + [high[granule] for granule in range(4)]
    for side, out_ref in ((1 - z_hi, sent_ref), (z_hi, own_ref)):
        kind = out_ref.dtype
        out_ref[0:2] = last_sum[pl.ds(2 * side, 2)].astype(kind)
        out_ref[2:4] = middle_sum[pl.ds(2 * side, 2)].astype(kind)
        halves = [jnp.where(side == 0, row[0:12], row[12:24]) for row in rows]
        halves.append(jnp.zeros_like(halves[0]))
        for pair in range(4):
            out_ref[4 + pair] = jnp.concatenate(halves[2 * pair : 2 * pair + 2], 0).astype(kind)


def square_kernel(own_ref, arrived_ref, total_ref, squares_ref):
    total = own_ref[...] + wide(arrived_ref[...])
    total_ref[...] = total
    squares_ref[...] = jnp.broadcast_to(jnp.sum(total * total), squares_ref.shape)


def scale_kernel(total_ref, squares_ref, first_ref, middle_ref, last_ref):
    square_sum = jnp.sum(squares_ref[...], axis=0)
    norm_scale = lax.rsqrt(square_sum / PARAMS + 1e-06)
    norm_scale = jnp.concatenate([norm_scale] * 3, 1)
    for ref, start in ((last_ref, 0), (middle_ref, 2)):
        for half in range(2):
            columns = slice(half * COLS, min((half + 1) * COLS, ref.shape[1]))
            width = columns.stop - columns.start
            ref[:, columns] = (total_ref[start + half] * norm_scale)[:, :width]
    for granule, (start, stop) in enumerate(column_cuts(first_ref.shape[1])):
        row = granule % 2 * 12
        scaled = total_ref[4 + granule // 2, row : row + 12] * norm_scale
        first_ref[:, start:stop] = scaled[:, : stop - start]


def granules(*lead, kind=BF16):
    return ((*lead, ROWS, COLS), kind)


def per_device(belief, target_value, counts, w_first, w_middle, w_last):
    total_rows, inputs = belief.shape
    width = w_last.shape[1]
    units = w_first.shape[1]
    hidden = w_middle.shape[1]
    belief_t, w_last_t = belief.T, w_last.T

    indices = (CORE, Y, X, ZH, "mp")
    place = jnp.stack([lax.axis_index(axis) for axis in indices])

    (half,) = call(
        half_kernel,
        "half",
        [SMEM, HBM],
        [((SIZE, hidden), BF16)],
        [pltpu.VMEM((width - SECOND, hidden), BF16), pltpu.SemaphoreType.DMA],
    )(place, w_last_t)
    fetched = lax.ppermute(half, (ZH, "mp"), [(0, 3), (3, 0), (1, 2), (2, 1)])
    belief_first, half = lax.optimization_barrier((belief_t, half))

    pre_first, act_first, hidden_sent = call(
        forward_kernel,
        "forward",
        [HBM] * 3,
        [
            ((total_rows, units), F32),
            ((total_rows, units), BF16),
            ((total_rows, hidden), BF16),
        ],
        [
            pltpu.VMEM((inputs, total_rows), BF16),
            pltpu.VMEM((inputs, units), BF16),
            pltpu.VMEM((units, hidden), BF16),
            pltpu.VMEM((total_rows, units), F32),
            pltpu.VMEM((total_rows, units), BF16),
            pltpu.SemaphoreType.DMA((2 * pl.cdiv(inputs, DEPTH) + 3,)),
        ],
        far=2,
    )(belief_first, w_first, w_middle)
    arrived = swap(hidden_sent, "mp")

    order = np.arange(units, dtype=np.int32).reshape(4, 2, 4, 2, -1).transpose(3, 0, 2, 1, 4)
    orders = np.stack([order[::-1], order]).reshape(2, units, 1)
    w_own, target_own, target_other, first_slope, onehot, live = call(
        stage_kernel,
        "stage",
        [SMEM, SMEM, VMEM, VMEM, HBM, HBM],
        [
            ((width, hidden), BF16),
            ((width, total_rows), BF16),
            ((2, SIZE, total_rows), BF16),
            ((total_rows, units), F32),
            ((units, units), BF16),
            ((1, total_rows), F32),
        ],
        [pltpu.VMEM((2 * width, total_rows), BF16), pltpu.SemaphoreType.DMA((2,))],
    )(place, counts, pre_first, jnp.asarray(orders), target_value.T, w_last_t)
    fetched, live = lax.optimization_barrier((fetched, live))
    relayed = swap(fetched, CORE)
    belief_swapped, act_swapped = lax.optimization_barrier((belief_t, act_first))
    sibling_belief = swap(belief_swapped, CORE)
    sibling_act = swap(act_swapped, CORE)

    act, act_slope, back_own, last_sent, last_own = call(
        hidden_kernel,
        "hidden",
        [SMEM] + [VMEM] * 5,
        [
            ((total_rows, hidden), BF16),
            ((total_rows, hidden), F32),
            ((total_rows, hidden), F32),
            ((hidden // 2 + width, total_rows), BF16),
            ((hidden // 2, total_rows), BF16),
        ],
        [pltpu.VMEM((hidden, total_rows), F32)],
    )(place, hidden_sent, arrived, live, target_own, w_own)
    last_arrived = swap(last_sent, CORE)

    slopes_sent, slopes_own = call(
        slopes_kernel,
        "slopes",
        [SMEM] + [VMEM] * 10,
        [((hidden // 2 + units // 2, total_rows), BF16)] * 2,
        [pltpu.VMEM((hidden, total_rows), F32)],
    )(
        place, act, act_slope, back_own, live, target_other, first_slope, onehot,
        fetched, relayed, w_middle,
    )
    slopes_arrived = swap(slopes_sent, CORE)

    def pairs(*sizes):
        return [out for size in sizes for out in (granules(*size, kind=F32), granules(*size))]

    def exchange(parts, axes, orders):
        sent = [part[1] for part in parts]
        arrived = [to_pair(*sending) for sending in zip(sent, axes, orders)]
        return [
            (part[0], lax.optimization_barrier((coming, *sent))[0])
            for part, coming in zip(parts, arrived)
        ]

    def halve(part, *lead):
        return call(halve_kernel, "halve", [VMEM] * 2, pairs((*lead, part[0].shape[-3])))(*part)

    def turn(part, axis, order):
        size = part[0].shape[-3]
        return call(
            functools.partial(turn_kernel, 1 if axis == Y else 2, order),
            "turn",
            [SMEM] + [VMEM] * 2,
            pairs((2, size)),
        )(place, *part)

    raw = pltpu.VMEM((hidden // 2, units), F32)
    last_own, slopes_own = lax.optimization_barrier((last_own, slopes_own))
    last_parts = call(
        last_kernel,
        "last",
        [SMEM] + [VMEM] * 3,
        pairs((2, 4, 4)),
        [raw, pltpu.VMEM((2, units, total_rows), BF16)],
    )(place, last_own, last_sent, last_arrived)
    middle_parts = call(
        middle_kernel, "middle", [SMEM] + [VMEM] * 4, pairs((2, 4, 4)), [raw]
    )(place, slopes_own, slopes_arrived, act_first, sibling_act)
    slopes_own, _ = lax.optimization_barrier((slopes_own, middle_parts[1]))
    first_parts = call(
        first_kernel,
        "first",
        [SMEM] + [VMEM] * 4,
        pairs((2, 4, 3), (2, 4, 4)),
        [pltpu.VMEM((16, 7, ROWS, COLS), F32)],
    )(place, slopes_own, slopes_arrived, belief_t, sibling_belief)
    def in_turn(step, parts):
        done = []
        for i, (kept, arrived) in enumerate(parts):
            if done:
                arrived, _ = lax.optimization_barrier((arrived, done[-1][1]))
            done.append(step(i, (kept, arrived)))
        return done

    axes, turned, orders, swapped = (X, X, Y, Y), (Y, Y, X, X), (0, 1, 1, 0), (1, 0, 0, 1)
    parts = (last_parts, middle_parts, first_parts[2:4], first_parts[0:2])
    parts = in_turn(lambda i, part: halve(part, 4), exchange(parts, axes, orders))
    parts = in_turn(
        lambda i, part: turn(part, turned[i], orders[i]), exchange(parts, axes, swapped)
    )
    parts = in_turn(lambda i, part: halve(part), exchange(parts, turned, orders))
    last_parts, middle_parts, high_parts, low_parts = exchange(parts, turned, swapped)
    parts = (*low_parts, *high_parts, *last_parts, *middle_parts)
    sent, own = call(
        z_cut_kernel,
        "z_cut",
        [SMEM] + [VMEM] * 8,
        [granules(8), granules(8, kind=F32)],
        [pltpu.VMEM((4, ROWS, COLS), F32)] * 2,
    )(place, *parts)

    total, squares = call(
        square_kernel, "square", [VMEM] * 2, [((8, ROWS, COLS), F32), ((128, 1, LANES), F32)]
    )(own, swap(sent, ZH))
    squares = lax.all_to_all(squares, ALL, 0, 0, tiled=True)
    grad_first, grad_middle, grad_last = call(
        scale_kernel,
        "scale",
        [VMEM] * 2,
        [((units // 64, inputs), F32), ((ROWS, units), F32), ((ROWS, width), F32)],
        kind=jax.ShapeDtypeStruct,
    )(total, squares)
    return grad_first.T, grad_middle.T, grad_last


def solution(mesh):
    finer = Mesh(mesh.devices.reshape(4, 2, 4, 2, mesh.shape["mp"]), ALL)
    return jax.shard_map(
        per_device,
        mesh=finer,
        in_specs=(P(DP, None), P(DP, None), P(DP), P(None, "mp"), P("mp", None), P(None, "mp")),
        out_specs=(P(None, MP_DP), P("mp", DP), P(DP, "mp")),
        check_vma=False,
    )
```

```python
import functools

import jax
import jax.numpy as jnp
import numpy as np
from jax import lax
from jax.experimental import pallas as pl
from jax.experimental.pallas import tpu as pltpu
from jax.sharding import Mesh
from jax.sharding import PartitionSpec as P

BLOCK = 128
PARAMS = 8469504
DP = ("dp_0", "dp_1", "dp_2", "dp_3")
MP_DP = ("mp", "dp_0", "dp_1", "dp_2", "dp_3")
ALL = DP + ("mp",)
Y, ZH, X, CORE = DP
LANES = 128
ROWS, COLS = 24, 384
SIZE, SECOND = 336, 328
DEPTH = 512
VMEM = pl.BlockSpec(memory_space=pltpu.VMEM)
SMEM = pl.BlockSpec(memory_space=pltpu.SMEM)
HBM = pl.BlockSpec(memory_space=pl.ANY)
BF16, F32 = jnp.bfloat16, jnp.float32


def wide(shard):
    return shard.astype(F32)


def narrow(shard):
    return shard.astype(BF16)


def swap(shard, axis):
    return lax.ppermute(shard, axis, [(0, 1), (1, 0)])


def to_pair(shard, axis, order):
    pairs = [(i, i ^ 1) for i in range(4)] if order == 0 else [(i, 3 - i) for i in range(4)]
    return lax.ppermute(shard, axis, pairs)


def silu_slope(pre_act):
    sigmoid_of = 1.0 / (1.0 + jnp.exp(-pre_act))
    return sigmoid_of * (1.0 + pre_act * (1.0 - sigmoid_of))


def dot(left, right):
    return jnp.dot(left, right, preferred_element_type=F32)


def contract(left, right, left_dim, right_dim):
    return lax.dot_general(
        left, right, (((left_dim,), (right_dim,)), ((), ())), preferred_element_type=F32
    )


def call(body, name, in_specs, outs, scratch=(), kind=pltpu.VMEM, far=0):
    kernel = pl.pallas_call(
        body,
        out_shape=[(pltpu.HBM if i < far else kind)(*out) for i, out in enumerate(outs)],
        in_specs=in_specs,
        out_specs=[HBM if i < far else VMEM for i in range(len(outs))],
        scratch_shapes=list(scratch),
        compiler_params=pltpu.CompilerParams(vmem_limit_bytes=24 << 20),
        cost_estimate=pl.CostEstimate(flops=1 << 34, bytes_accessed=1 << 26, transcendentals=0),
        name=name,
    )

    def run(*operands):
        return kernel(
            *(
                operand if spec is SMEM else pltpu.with_memory_space_constraint(
                    operand, pltpu.VMEM if spec is VMEM else pltpu.HBM
                )
                for operand, spec in zip(operands, in_specs)
            )
        )

    return run


def rows_of_core(rows_ref, core, out_ref):
    for block in range(32):
        y, x, z_hi = block // 8, block // 2 % 4, block % 2
        first = 2 * ROWS * ((2 * y + z_hi) * 4 + x)
        rows = pl.ds(pl.multiple_of(first + ROWS * core, 8), ROWS)
        out_ref[ROWS * block : ROWS * (block + 1), :] = narrow(rows_ref[rows, :])


def forward_kernel(
    belief_hbm, w_first_hbm, w_middle_hbm, pre_first_hbm, act_first_hbm, sent_ref,
    belief, w_first, w_middle, pre_first_ref, act_first_ref, sems,
):
    inputs = belief.shape[0]
    cuts = [(start, min(start + DEPTH, inputs)) for start in range(0, inputs, DEPTH)]
    copies = []
    for i, (start, stop) in enumerate(cuts):
        rows = pl.ds(start, stop - start)
        copies.append(
            (
                pltpu.make_async_copy(belief_hbm.at[rows], belief.at[rows], sems.at[2 * i]),
                pltpu.make_async_copy(w_first_hbm.at[rows], w_first.at[rows], sems.at[2 * i + 1]),
            )
        )
    copies.append((pltpu.make_async_copy(w_middle_hbm, w_middle, sems.at[2 * len(cuts)]),))
    for pair in copies:
        for copy in pair:
            copy.start()
    results = (
        pltpu.make_async_copy(pre_first_ref, pre_first_hbm, sems.at[2 * len(cuts) + 1]),
        pltpu.make_async_copy(act_first_ref, act_first_hbm, sems.at[2 * len(cuts) + 2]),
    )
    pre_first = jnp.zeros(pre_first_ref.shape, F32)
    for (start, stop), pair in zip(cuts, copies):
        for copy in pair:
            copy.wait()
        pre_first += contract(belief[start:stop, :], w_first[start:stop, :], 0, 0)
    pre_first_ref[...] = pre_first
    results[0].start()
    act_first = narrow(pre_first / (1.0 + jnp.exp(-pre_first)))
    act_first_ref[...] = act_first
    results[1].start()
    copies[-1][0].wait()
    sent_ref[...] = narrow(dot(act_first, w_middle[...]))
    for copy in results:
        copy.wait()


def half_kernel(place_ref, w_last_hbm, half_ref, last_ref, sem):
    size, total = half_ref.shape[0], w_last_hbm.shape[0]

    @pl.when(place_ref[0] == 0)
    def _():
        copy = pltpu.make_async_copy(w_last_hbm.at[pl.ds(0, size)], half_ref, sem)
        copy.start()
        copy.wait()

    @pl.when(place_ref[0] != 0)
    def _():
        copy = pltpu.make_async_copy(w_last_hbm.at[pl.ds(SECOND, total - SECOND)], last_ref, sem)
        copy.start()
        half_ref[size - 8 :, :] = jnp.zeros((8, half_ref.shape[1]), half_ref.dtype)
        copy.wait()
        half_ref[0 : total - SECOND, :] = last_ref[...]


def stage_kernel(
    place_ref, counts_ref, pre_first_ref, orders_ref, w_middle_ref, target_hbm, w_last_hbm,
    w_own_ref, target_own_ref, target_other_ref, first_slope_ref, w_sorted_ref, live_ref,
    target_ref, sems,
):
    copies = (
        pltpu.make_async_copy(target_hbm, target_ref, sems.at[0]),
        pltpu.make_async_copy(w_last_hbm, w_own_ref, sems.at[1]),
    )
    for copy in copies:
        copy.start()
    order = jnp.where(place_ref[0] == 0, orders_ref[0], orders_ref[1])
    units = lax.broadcasted_iota(jnp.int32, (order.shape[0], order.shape[0]), 1)
    onehot = jnp.where(order == units, 1.0, 0.0)
    w_sorted_ref[...] = narrow(dot(narrow(onehot), w_middle_ref[...]))
    first_slope_ref[...] = lax.dot_general(
        onehot,
        silu_slope(pre_first_ref[...]),
        (((1,), (1,)), ((), ())),
        precision=lax.Precision.HIGHEST,
        preferred_element_type=F32,
    )
    row = lax.broadcasted_iota(jnp.int32, live_ref.shape, 1)
    count = jnp.where(row < BLOCK, counts_ref[0], counts_ref[1] + BLOCK)
    live_ref[...] = jnp.where(row < count, 1.0, 0.0)
    copies[0].wait()
    width = target_own_ref.shape[0]
    low, high = target_ref[0:width, :], target_ref[width : 2 * width, :]
    is_low = place_ref[4] == 0
    target_own_ref[...] = jnp.where(is_low, low, high)
    other = jnp.where(is_low, high, low)
    size = target_other_ref.shape[1]
    for side in range(2):

        @pl.when(place_ref[0] == side)
        def _():
            target_other_ref[side] = other[0:size]
            target_other_ref[1 - side, size - 8 :, :] = jnp.zeros((8, other.shape[1]), other.dtype)
            target_other_ref[1 - side, 0 : width - SECOND, :] = other[SECOND:]

    copies[1].wait()


def hidden_kernel(
    place_ref, partial_ref, arrived_ref, live_ref, target_ref, w_ref,
    act_ref, act_slope_ref, back_ref, sent_ref, own_ref, rows_ref,
):
    core = place_ref[0]
    pre_middle = wide(partial_ref[...]) + wide(arrived_ref[...])
    sigmoid_of = 1.0 / (1.0 + jnp.exp(-pre_middle))
    act = narrow(pre_middle * sigmoid_of)
    act_ref[...] = act
    act_slope_ref[...] = sigmoid_of * (1.0 + pre_middle * (1.0 - sigmoid_of))
    slope = slope_of(w_ref[...], act, target_ref[...], live_ref[...])
    half = own_ref.shape[0]
    sent_ref[half:, :] = slope
    back_ref[...] = contract(slope, w_ref[...], 0, 0)
    rows_ref[...] = wide(act).T
    rows_of_core(rows_ref, 1 - core, sent_ref)
    rows_of_core(rows_ref, core, own_ref)


def slope_of(weights, act, target, live):
    mismatch = contract(weights, act, 1, 1) - wide(target)
    return narrow(jnp.clip(mismatch, -1.0, 1.0) * live)


def slopes_kernel(
    place_ref, act_ref, act_slope_ref, back_ref, live_ref, target_ref, first_slope_ref,
    fetched_ref, relayed_ref, w_sorted_ref, sent_ref, own_ref, rows_ref,
):
    core = place_ref[0]
    act, live = act_ref[...], live_ref[...]
    back = back_ref[...]
    for side, w_ref in enumerate((fetched_ref, relayed_ref)):
        weights = w_ref[...]
        slope = slope_of(weights, act, target_ref[side], live)
        repeated = jnp.where(core == side, 0, SIZE - SECOND)
        column = lax.broadcasted_iota(jnp.int32, slope.shape, 0)
        slope = jnp.where(column >= repeated, slope, jnp.zeros_like(slope))
        back += contract(slope, weights, 0, 0)
    slope_middle = narrow(back * act_slope_ref[...])
    slope_first = narrow(contract(w_sorted_ref[...], slope_middle, 1, 1) * first_slope_ref[...])
    half = slope_first.shape[0] // 2
    sent_ref[2 * half :, :] = slope_first[:half]
    own_ref[2 * half :, :] = slope_first[half:]
    rows_ref[...] = wide(slope_middle).T
    rows_of_core(rows_ref, 1 - core, sent_ref)
    rows_of_core(rows_ref, core, own_ref)


def column_cuts(width):
    return [(start, min(start + COLS, width)) for start in range(0, width, COLS)]


def put_columns(raw, granule, out_ref):
    width = raw.shape[1]
    if width < COLS:
        raw = jnp.concatenate([raw, jnp.zeros((raw.shape[0], COLS - width), raw.dtype)], 1)
    for unit in range(16):
        out_ref[unit, granule] = raw[unit * ROWS : (unit + 1) * ROWS]


def kept_and_sent(me, order):
    near, far, opposite = lax.bitwise_xor(me, 1), 3 - me, lax.bitwise_xor(me, 2)
    return ((me, far), (near, opposite)) if order == 0 else ((me, near), (far, opposite))


def cut_rows(raw_ref, me, order, kept_ref, sent_ref):
    for out_ref, blocks in zip((kept_ref, sent_ref), kept_and_sent(me, order)):
        for position, x in enumerate(blocks):
            for y in range(4):
                for granule in range(4):
                    first = ROWS * (2 * (4 * y + x) + granule // 2)
                    columns = slice(granule % 2 * COLS, (granule % 2 + 1) * COLS)
                    rows = raw_ref[pl.ds(pl.multiple_of(first, 8), ROWS), columns]
                    out_ref[position, y, granule] = rows.astype(out_ref.dtype)


def last_kernel(place_ref, own_ref, sent_ref, arrived_ref, kept_out, sent_out, raw_ref, padded_ref):
    half = own_ref.shape[0]
    width = sent_ref.shape[0] - half
    padded_ref[...] = jnp.zeros_like(padded_ref)
    padded_ref[0, 0:width, :] = sent_ref[half:, :]
    padded_ref[1, 0:width, :] = arrived_ref[half:, :]
    raw_ref[...] = contract(own_ref[...], padded_ref[0], 1, 1) + contract(
        arrived_ref[0:half, :], padded_ref[1], 1, 1
    )
    cut_rows(raw_ref, place_ref[2], 0, kept_out, sent_out)


def middle_kernel(
    place_ref, own_ref, arrived_ref, act_ref, sibling_act_ref, kept_out, sent_out, raw_ref
):
    half = raw_ref.shape[0]
    raw_ref[...] = dot(own_ref[0:half, :], act_ref[...]) + dot(
        arrived_ref[0:half, :], sibling_act_ref[...]
    )
    cut_rows(raw_ref, place_ref[2], 1, kept_out, sent_out)


def first_kernel(place_ref, own_ref, arrived_ref, belief_ref, sibling_belief_ref, *refs):
    raw_ref = refs[-1]
    start_row = own_ref.shape[0] // 3 * 2
    own, arrived = own_ref[start_row:, :], arrived_ref[start_row:, :]
    for start, stop in column_cuts(belief_ref.shape[0]):
        raw = contract(own, belief_ref[start:stop, :], 1, 1) + contract(
            arrived, sibling_belief_ref[start:stop, :], 1, 1
        )
        put_columns(raw, start // COLS, raw_ref)
    for order, part in enumerate((slice(0, 4), slice(4, 7))):
        for side, blocks in enumerate(kept_and_sent(place_ref[1], order)):
            out_ref = refs[2 * order + side]
            for position, y in enumerate(blocks):
                for x in range(4):
                    out_ref[position, x] = raw_ref[4 * y + x, part].astype(out_ref.dtype)


def halve_kernel(kept_ref, arrived_ref, kept_out, sent_out):
    kept_out[...] = kept_ref[0] + wide(arrived_ref[0])
    sent_out[...] = narrow(kept_ref[1] + wide(arrived_ref[1]))


def turn_kernel(axis, order, place_ref, kept_ref, arrived_ref, kept_out, sent_out):
    for out_ref, blocks in zip((kept_out, sent_out), kept_and_sent(place_ref[axis], order)):
        for position, block in enumerate(blocks):
            total = kept_ref[block] + wide(arrived_ref[block])
            out_ref[position] = total.astype(out_ref.dtype)


def z_cut_kernel(place_ref, *refs):
    sent_ref, own_ref, last_sum, middle_sum = refs[8:12]
    z_hi = place_ref[3]
    low, high, last, middle = (
        refs[2 * part][...] + wide(refs[2 * part + 1][...]) for part in range(4)
    )
    last_sum[...] = last
    middle_sum[...] = middle
    rows = [low[granule] for granule in range(4)] + [high[granule] for granule in range(3)]
    for side, out_ref in ((1 - z_hi, sent_ref), (z_hi, own_ref)):
        kind = out_ref.dtype
        out_ref[0:2] = last_sum[pl.ds(2 * side, 2)].astype(kind)
        out_ref[2:4] = middle_sum[pl.ds(2 * side, 2)].astype(kind)
        halves = [jnp.where(side == 0, row[0:12], row[12:24]) for row in rows]
        halves.append(jnp.zeros_like(halves[0]))
        for pair in range(4):
            out_ref[4 + pair] = jnp.concatenate(halves[2 * pair : 2 * pair + 2], 0).astype(kind)


def square_kernel(own_ref, arrived_ref, total_ref, squares_ref):
    total = own_ref[...] + wide(arrived_ref[...])
    total_ref[...] = total
    squares_ref[...] = jnp.broadcast_to(jnp.sum(total * total), squares_ref.shape)


def scale_kernel(total_ref, squares_ref, first_ref, middle_ref, last_ref):
    square_sum = jnp.sum(squares_ref[...], axis=0)
    norm_scale = lax.rsqrt(square_sum / PARAMS + 1e-06)
    norm_scale = jnp.concatenate([norm_scale] * 3, 1)
    for ref, start in ((last_ref, 0), (middle_ref, 2)):
        for half in range(2):
            columns = slice(half * COLS, min((half + 1) * COLS, ref.shape[1]))
            width = columns.stop - columns.start
            ref[:, columns] = (total_ref[start + half] * norm_scale)[:, :width]
    for granule, (start, stop) in enumerate(column_cuts(first_ref.shape[1])):
        row = granule % 2 * 12
        scaled = total_ref[4 + granule // 2, row : row + 12] * norm_scale
        first_ref[:, start:stop] = scaled[:, : stop - start]


def granules(*lead, kind=BF16):
    return ((*lead, ROWS, COLS), kind)


def per_device(belief, target_value, counts, w_first, w_middle, w_last):
    total_rows, inputs = belief.shape
    width = w_last.shape[1]
    units = w_first.shape[1]
    hidden = w_middle.shape[1]
    belief_t, w_last_t = belief.T, w_last.T

    indices = (CORE, Y, X, ZH, "mp")
    place = jnp.stack([lax.axis_index(axis) for axis in indices])

    (half,) = call(
        half_kernel,
        "half",
        [SMEM, HBM],
        [((SIZE, hidden), BF16)],
        [pltpu.VMEM((width - SECOND, hidden), BF16), pltpu.SemaphoreType.DMA],
    )(place, w_last_t)
    fetched = lax.ppermute(half, (ZH, "mp"), [(0, 3), (3, 0), (1, 2), (2, 1)])
    belief_first, half = lax.optimization_barrier((belief_t, half))

    pre_first, act_first, hidden_sent = call(
        forward_kernel,
        "forward",
        [HBM] * 3,
        [
            ((total_rows, units), F32),
            ((total_rows, units), BF16),
            ((total_rows, hidden), BF16),
        ],
        [
            pltpu.VMEM((inputs, total_rows), BF16),
            pltpu.VMEM((inputs, units), BF16),
            pltpu.VMEM((units, hidden), BF16),
            pltpu.VMEM((total_rows, units), F32),
            pltpu.VMEM((total_rows, units), BF16),
            pltpu.SemaphoreType.DMA((2 * pl.cdiv(inputs, DEPTH) + 3,)),
        ],
        far=2,
    )(belief_first, w_first, w_middle)
    arrived = swap(hidden_sent, "mp")

    order = np.arange(units, dtype=np.int32).reshape(4, 2, 4, 2, -1).transpose(3, 0, 2, 1, 4)
    orders = np.stack([order[::-1], order]).reshape(2, units, 1)
    w_own, target_own, target_other, first_slope, w_sorted, live = call(
        stage_kernel,
        "stage",
        [SMEM, SMEM, VMEM, VMEM, VMEM, HBM, HBM],
        [
            ((width, hidden), BF16),
            ((width, total_rows), BF16),
            ((2, SIZE, total_rows), BF16),
            ((units, total_rows), F32),
            ((units, hidden), BF16),
            ((1, total_rows), F32),
        ],
        [pltpu.VMEM((2 * width, total_rows), BF16), pltpu.SemaphoreType.DMA((2,))],
    )(place, counts, pre_first, jnp.asarray(orders), w_middle, target_value.T, w_last_t)
    fetched, live = lax.optimization_barrier((fetched, live))
    relayed = swap(fetched, CORE)
    belief_swapped, act_swapped = lax.optimization_barrier((belief_t, act_first))
    sibling_belief = swap(belief_swapped, CORE)
    sibling_act = swap(act_swapped, CORE)

    act, act_slope, back_own, last_sent, last_own = call(
        hidden_kernel,
        "hidden",
        [SMEM] + [VMEM] * 5,
        [
            ((total_rows, hidden), BF16),
            ((total_rows, hidden), F32),
            ((total_rows, hidden), F32),
            ((hidden // 2 + width, total_rows), BF16),
            ((hidden // 2, total_rows), BF16),
        ],
        [pltpu.VMEM((hidden, total_rows), F32)],
    )(place, hidden_sent, arrived, live, target_own, w_own)
    last_arrived = swap(last_sent, CORE)

    slopes_sent, slopes_own = call(
        slopes_kernel,
        "slopes",
        [SMEM] + [VMEM] * 9,
        [((hidden // 2 + units // 2, total_rows), BF16)] * 2,
        [pltpu.VMEM((hidden, total_rows), F32)],
    )(
        place, act, act_slope, back_own, live, target_other, first_slope,
        fetched, relayed, w_sorted,
    )
    slopes_arrived = swap(slopes_sent, CORE)

    def pairs(*sizes):
        return [out for size in sizes for out in (granules(*size, kind=F32), granules(*size))]

    def exchange(parts, axes, orders):
        sent = [part[1] for part in parts]
        arrived = [to_pair(*sending) for sending in zip(sent, axes, orders)]
        return [
            (part[0], lax.optimization_barrier((coming, *sent))[0])
            for part, coming in zip(parts, arrived)
        ]

    def halve(part, *lead):
        return call(halve_kernel, "halve", [VMEM] * 2, pairs((*lead, part[0].shape[-3])))(*part)

    def turn(part, axis, order):
        size = part[0].shape[-3]
        return call(
            functools.partial(turn_kernel, 1 if axis == Y else 2, order),
            "turn",
            [SMEM] + [VMEM] * 2,
            pairs((2, size)),
        )(place, *part)

    raw = pltpu.VMEM((hidden // 2, units), F32)
    last_own, slopes_own = lax.optimization_barrier((last_own, slopes_own))
    last_parts = call(
        last_kernel,
        "last",
        [SMEM] + [VMEM] * 3,
        pairs((2, 4, 4)),
        [raw, pltpu.VMEM((2, units, total_rows), BF16)],
    )(place, last_own, last_sent, last_arrived)
    first_parts = call(
        first_kernel,
        "first",
        [SMEM] + [VMEM] * 4,
        pairs((2, 4, 4), (2, 4, 3)),
        [pltpu.VMEM((16, 7, ROWS, COLS), F32)],
    )(place, slopes_own, slopes_arrived, belief_t, sibling_belief)
    middle_parts = call(
        middle_kernel, "middle", [SMEM] + [VMEM] * 4, pairs((2, 4, 4)), [raw]
    )(place, slopes_own, slopes_arrived, act_first, sibling_act)
    axes, turned, orders, swapped = (X, X, Y, Y), (Y, Y, X, X), (0, 1, 0, 1), (1, 0, 1, 0)
    parts = (last_parts, middle_parts, first_parts[0:2], first_parts[2:4])
    parts = [halve(part, 4) for part in exchange(parts, axes, orders)]
    parts = [
        turn(part, turned[i], orders[i]) for i, part in enumerate(exchange(parts, axes, swapped))
    ]
    parts = [halve(part) for part in exchange(parts, turned, orders)]
    last_parts, middle_parts, *first_parts = exchange(parts, turned, swapped)
    parts = (*first_parts[0], *first_parts[1], *last_parts, *middle_parts)
    sent, own = call(
        z_cut_kernel,
        "z_cut",
        [SMEM] + [VMEM] * 8,
        [granules(8), granules(8, kind=F32)],
        [pltpu.VMEM((4, ROWS, COLS), F32)] * 2,
    )(place, *parts)

    total, squares = call(
        square_kernel, "square", [VMEM] * 2, [((8, ROWS, COLS), F32), ((128, 1, LANES), F32)]
    )(own, swap(sent, ZH))
    squares = lax.all_to_all(squares, ALL, 0, 0, tiled=True)
    grad_first, grad_middle, grad_last = call(
        scale_kernel,
        "scale",
        [VMEM] * 2,
        [((units // 64, inputs), F32), ((ROWS, units), F32), ((ROWS, width), F32)],
        kind=jax.ShapeDtypeStruct,
    )(total, squares)
    return grad_first.T, grad_middle.T, grad_last


def solution(mesh):
    finer = Mesh(mesh.devices.reshape(4, 2, 4, 2, mesh.shape["mp"]), ALL)
    return jax.shard_map(
        per_device,
        mesh=finer,
        in_specs=(P(DP, None), P(DP, None), P(DP), P(None, "mp"), P("mp", None), P(None, "mp")),
        out_specs=(P(None, MP_DP), P("mp", DP), P(DP, "mp")),
        check_vma=False,
    )
```

```python
import functools

import jax
import jax.numpy as jnp
import numpy as np
from jax import lax
from jax.experimental import pallas as pl
from jax.experimental.pallas import tpu as pltpu
from jax.sharding import Mesh
from jax.sharding import PartitionSpec as P

BLOCK = 128
PARAMS = 8469504
DP = ("dp_0", "dp_1", "dp_2", "dp_3")
MP_DP = ("mp", "dp_0", "dp_1", "dp_2", "dp_3")
ALL = DP + ("mp",)
Y, ZH, X, CORE = DP
LANES = 128
ROWS, COLS = 24, 384
SIZE, SECOND = 336, 328
DEPTH = 512
VMEM = pl.BlockSpec(memory_space=pltpu.VMEM)
SMEM = pl.BlockSpec(memory_space=pltpu.SMEM)
HBM = pl.BlockSpec(memory_space=pl.ANY)
BF16, F32 = jnp.bfloat16, jnp.float32


def wide(shard):
    return shard.astype(F32)


def narrow(shard):
    return shard.astype(BF16)


def swap(shard, axis):
    return lax.ppermute(shard, axis, [(0, 1), (1, 0)])


def to_pair(shard, axis, order):
    pairs = [(i, i ^ 1) for i in range(4)] if order == 0 else [(i, 3 - i) for i in range(4)]
    return lax.ppermute(shard, axis, pairs)


def silu_slope(pre_act):
    sigmoid_of = 1.0 / (1.0 + jnp.exp(-pre_act))
    return sigmoid_of * (1.0 + pre_act * (1.0 - sigmoid_of))


def dot(left, right):
    return jnp.dot(left, right, preferred_element_type=F32)


def contract(left, right, left_dim, right_dim):
    return lax.dot_general(
        left, right, (((left_dim,), (right_dim,)), ((), ())), preferred_element_type=F32
    )


def call(body, name, in_specs, outs, scratch=(), kind=pltpu.VMEM, far=0):
    kernel = pl.pallas_call(
        body,
        out_shape=[(pltpu.HBM if i < far else kind)(*out) for i, out in enumerate(outs)],
        in_specs=in_specs,
        out_specs=[HBM if i < far else VMEM for i in range(len(outs))],
        scratch_shapes=list(scratch),
        compiler_params=pltpu.CompilerParams(vmem_limit_bytes=24 << 20),
        cost_estimate=pl.CostEstimate(flops=1 << 34, bytes_accessed=1 << 26, transcendentals=0),
        name=name,
    )

    def run(*operands):
        return kernel(
            *(
                operand if spec is SMEM else pltpu.with_memory_space_constraint(
                    operand, pltpu.VMEM if spec is VMEM else pltpu.HBM
                )
                for operand, spec in zip(operands, in_specs)
            )
        )

    return run


def rows_of_core(rows_ref, core, out_ref):
    for block in range(32):
        y, x, z_hi = block // 8, block // 2 % 4, block % 2
        first = 2 * ROWS * ((2 * y + z_hi) * 4 + x)
        rows = pl.ds(pl.multiple_of(first + ROWS * core, 8), ROWS)
        out_ref[ROWS * block : ROWS * (block + 1), :] = narrow(rows_ref[rows, :])


def forward_kernel(
    belief_hbm, w_first_hbm, w_middle_hbm, pre_first_hbm, act_first_hbm, sent_ref,
    belief, w_first, w_middle, pre_first_ref, act_first_ref, sems,
):
    inputs = belief.shape[0]
    cuts = [(start, min(start + DEPTH, inputs)) for start in range(0, inputs, DEPTH)]
    copies = []
    for i, (start, stop) in enumerate(cuts):
        rows = pl.ds(start, stop - start)
        copies.append(
            (
                pltpu.make_async_copy(belief_hbm.at[rows], belief.at[rows], sems.at[2 * i]),
                pltpu.make_async_copy(w_first_hbm.at[rows], w_first.at[rows], sems.at[2 * i + 1]),
            )
        )
    copies.append((pltpu.make_async_copy(w_middle_hbm, w_middle, sems.at[2 * len(cuts)]),))
    for pair in copies:
        for copy in pair:
            copy.start()
    results = (
        pltpu.make_async_copy(pre_first_ref, pre_first_hbm, sems.at[2 * len(cuts) + 1]),
        pltpu.make_async_copy(act_first_ref, act_first_hbm, sems.at[2 * len(cuts) + 2]),
    )
    pre_first = jnp.zeros(pre_first_ref.shape, F32)
    for (start, stop), pair in zip(cuts, copies):
        for copy in pair:
            copy.wait()
        pre_first += contract(belief[start:stop, :], w_first[start:stop, :], 0, 0)
    pre_first_ref[...] = pre_first
    results[0].start()
    act_first = narrow(pre_first / (1.0 + jnp.exp(-pre_first)))
    act_first_ref[...] = act_first
    results[1].start()
    copies[-1][0].wait()
    sent_ref[...] = narrow(dot(act_first, w_middle[...]))
    for copy in results:
        copy.wait()


def half_kernel(place_ref, w_last_hbm, half_ref, last_ref, sem):
    size, total = half_ref.shape[0], w_last_hbm.shape[0]

    @pl.when(place_ref[0] == 0)
    def _():
        copy = pltpu.make_async_copy(w_last_hbm.at[pl.ds(0, size)], half_ref, sem)
        copy.start()
        copy.wait()

    @pl.when(place_ref[0] != 0)
    def _():
        copy = pltpu.make_async_copy(w_last_hbm.at[pl.ds(SECOND, total - SECOND)], last_ref, sem)
        copy.start()
        half_ref[size - 8 :, :] = jnp.zeros((8, half_ref.shape[1]), half_ref.dtype)
        copy.wait()
        half_ref[0 : total - SECOND, :] = last_ref[...]


def stage_kernel(
    place_ref, counts_ref, pre_first_ref, orders_ref, w_middle_ref, target_hbm, w_last_hbm,
    w_own_ref, target_own_ref, target_other_ref, first_slope_ref, w_sorted_ref, live_ref,
    target_ref, sems,
):
    copies = (
        pltpu.make_async_copy(target_hbm, target_ref, sems.at[0]),
        pltpu.make_async_copy(w_last_hbm, w_own_ref, sems.at[1]),
    )
    for copy in copies:
        copy.start()
    order = jnp.where(place_ref[0] == 0, orders_ref[0], orders_ref[1])
    units = lax.broadcasted_iota(jnp.int32, (order.shape[0], order.shape[0]), 1)
    onehot = jnp.where(order == units, 1.0, 0.0)
    w_sorted_ref[...] = narrow(dot(narrow(onehot), w_middle_ref[...]))
    first_slope_ref[...] = lax.dot_general(
        onehot,
        silu_slope(pre_first_ref[...]),
        (((1,), (1,)), ((), ())),
        precision=lax.Precision.HIGHEST,
        preferred_element_type=F32,
    )
    row = lax.broadcasted_iota(jnp.int32, live_ref.shape, 1)
    count = jnp.where(row < BLOCK, counts_ref[0], counts_ref[1] + BLOCK)
    live_ref[...] = jnp.where(row < count, 1.0, 0.0)
    copies[0].wait()
    width = target_own_ref.shape[0]
    low, high = target_ref[0:width, :], target_ref[width : 2 * width, :]
    is_low = place_ref[4] == 0
    target_own_ref[...] = jnp.where(is_low, low, high)
    other = jnp.where(is_low, high, low)
    size = target_other_ref.shape[1]
    for side in range(2):

        @pl.when(place_ref[0] == side)
        def _():
            target_other_ref[side] = other[0:size]
            target_other_ref[1 - side, size - 8 :, :] = jnp.zeros((8, other.shape[1]), other.dtype)
            target_other_ref[1 - side, 0 : width - SECOND, :] = other[SECOND:]

    copies[1].wait()


def hidden_kernel(
    place_ref, partial_ref, arrived_ref, live_ref, target_ref, w_ref,
    act_ref, act_slope_ref, back_ref, sent_ref, own_ref, rows_ref,
):
    core = place_ref[0]
    pre_middle = wide(partial_ref[...]) + wide(arrived_ref[...])
    sigmoid_of = 1.0 / (1.0 + jnp.exp(-pre_middle))
    act = narrow(pre_middle * sigmoid_of)
    act_ref[...] = act
    act_slope_ref[...] = sigmoid_of * (1.0 + pre_middle * (1.0 - sigmoid_of))
    slope = slope_of(w_ref[...], act, target_ref[...], live_ref[...])
    half = own_ref.shape[0]
    sent_ref[half:, :] = slope
    back_ref[...] = contract(slope, w_ref[...], 0, 0)
    rows_ref[...] = wide(act).T
    rows_of_core(rows_ref, 1 - core, sent_ref)
    rows_of_core(rows_ref, core, own_ref)


def slope_of(weights, act, target, live):
    mismatch = contract(weights, act, 1, 1) - wide(target)
    return narrow(jnp.clip(mismatch, -1.0, 1.0) * live)


def slopes_kernel(
    place_ref, act_ref, act_slope_ref, back_ref, live_ref, target_ref, first_slope_ref,
    fetched_ref, relayed_ref, w_sorted_ref, sent_ref, own_ref, rows_ref,
):
    core = place_ref[0]
    act, live = act_ref[...], live_ref[...]
    back = back_ref[...]
    for side, w_ref in enumerate((fetched_ref, relayed_ref)):
        weights = w_ref[...]
        slope = slope_of(weights, act, target_ref[side], live)
        repeated = jnp.where(core == side, 0, SIZE - SECOND)
        column = lax.broadcasted_iota(jnp.int32, slope.shape, 0)
        slope = jnp.where(column >= repeated, slope, jnp.zeros_like(slope))
        back += contract(slope, weights, 0, 0)
    slope_middle = narrow(back * act_slope_ref[...])
    slope_first = narrow(contract(w_sorted_ref[...], slope_middle, 1, 1) * first_slope_ref[...])
    half = slope_first.shape[0] // 2
    sent_ref[2 * half :, :] = slope_first[:half]
    own_ref[2 * half :, :] = slope_first[half:]
    rows_ref[...] = wide(slope_middle).T
    rows_of_core(rows_ref, 1 - core, sent_ref)
    rows_of_core(rows_ref, core, own_ref)


def column_cuts(width):
    return [(start, min(start + COLS, width)) for start in range(0, width, COLS)]


def kept_and_sent(me, order):
    near, far, opposite = lax.bitwise_xor(me, 1), 3 - me, lax.bitwise_xor(me, 2)
    return ((me, far), (near, opposite)) if order == 0 else ((me, near), (far, opposite))


def rows_along_x(ref, me, order):
    kept, sent = kept_and_sent(me, order)
    firsts = [2 * ROWS * (4 * y + x) for x in (*kept, *sent) for y in range(4)]
    return jnp.concatenate(
        [ref[pl.ds(pl.multiple_of(first, 16), 2 * ROWS), :] for first in firsts], 0
    )


def put_rows(raw, kept_ref, sent_ref):
    for block in range(16):
        out_ref = (kept_ref, sent_ref)[block // 8]
        for granule in range(4):
            first = ROWS * (2 * block + granule // 2)
            columns = slice(granule % 2 * COLS, (granule % 2 + 1) * COLS)
            rows = raw[first : first + ROWS, columns]
            out_ref[block // 4 % 2, block % 4, granule] = rows.astype(out_ref.dtype)


def last_kernel(place_ref, own_ref, sent_ref, arrived_ref, kept_out, sent_out, padded_ref):
    half = own_ref.shape[0]
    width = sent_ref.shape[0] - half
    padded_ref[...] = jnp.zeros_like(padded_ref)
    padded_ref[0, 0:width, :] = sent_ref[half:, :]
    padded_ref[1, 0:width, :] = arrived_ref[half:, :]
    own, arrived = (rows_along_x(ref, place_ref[2], 0) for ref in (own_ref, arrived_ref))
    raw = contract(own, padded_ref[0], 1, 1) + contract(arrived, padded_ref[1], 1, 1)
    put_rows(raw, kept_out, sent_out)


def middle_kernel(place_ref, own_ref, arrived_ref, act_ref, sibling_act_ref, kept_out, sent_out):
    own, arrived = (rows_along_x(ref, place_ref[2], 1) for ref in (own_ref, arrived_ref))
    raw = dot(own, act_ref[...]) + dot(arrived, sibling_act_ref[...])
    put_rows(raw, kept_out, sent_out)


def first_kernel(place_ref, own_ref, arrived_ref, belief_ref, sibling_belief_ref, *out_refs):
    start_row = own_ref.shape[0] // 3 * 2
    cuts = column_cuts(belief_ref.shape[0])
    for order, part in enumerate((cuts[0:4], cuts[4:7])):
        kept, sent = kept_and_sent(place_ref[1], order)
        own, arrived = (
            jnp.concatenate(
                [
                    ref[pl.ds(pl.multiple_of(start_row + 4 * ROWS * y, 32), 4 * ROWS), :]
                    for y in (*kept, *sent)
                ],
                0,
            )
            for ref in (own_ref, arrived_ref)
        )
        for granule, (start, stop) in enumerate(part):
            raw = contract(own, belief_ref[start:stop, :], 1, 1) + contract(
                arrived, sibling_belief_ref[start:stop, :], 1, 1
            )
            if stop - start < COLS:
                pad = jnp.zeros((raw.shape[0], COLS - raw.shape[1]), raw.dtype)
                raw = jnp.concatenate([raw, pad], 1)
            for unit in range(16):
                out_ref = out_refs[2 * order + unit // 8]
                rows = raw[unit * ROWS : (unit + 1) * ROWS]
                out_ref[unit // 4 % 2, unit % 4, granule] = rows.astype(out_ref.dtype)


def halve_kernel(kept_ref, arrived_ref, kept_out, sent_out):
    kept_out[...] = kept_ref[0] + wide(arrived_ref[0])
    sent_out[...] = narrow(kept_ref[1] + wide(arrived_ref[1]))


def turn_kernel(axis, order, place_ref, kept_ref, arrived_ref, kept_out, sent_out):
    for out_ref, blocks in zip((kept_out, sent_out), kept_and_sent(place_ref[axis], order)):
        for position, block in enumerate(blocks):
            total = kept_ref[block] + wide(arrived_ref[block])
            out_ref[position] = total.astype(out_ref.dtype)


def z_cut_kernel(place_ref, *refs):
    sent_ref, own_ref, last_sum, middle_sum = refs[8:12]
    z_hi = place_ref[3]
    low, high, last, middle = (
        refs[2 * part][...] + wide(refs[2 * part + 1][...]) for part in range(4)
    )
    last_sum[...] = last
    middle_sum[...] = middle
    rows = [low[granule] for granule in range(4)] + [high[granule] for granule in range(3)]
    for side, out_ref in ((1 - z_hi, sent_ref), (z_hi, own_ref)):
        kind = out_ref.dtype
        out_ref[0:2] = last_sum[pl.ds(2 * side, 2)].astype(kind)
        out_ref[2:4] = middle_sum[pl.ds(2 * side, 2)].astype(kind)
        halves = [jnp.where(side == 0, row[0:12], row[12:24]) for row in rows]
        halves.append(jnp.zeros_like(halves[0]))
        for pair in range(4):
            out_ref[4 + pair] = jnp.concatenate(halves[2 * pair : 2 * pair + 2], 0).astype(kind)


def square_kernel(own_ref, arrived_ref, total_ref, squares_ref):
    total = own_ref[...] + wide(arrived_ref[...])
    total_ref[...] = total
    squares_ref[...] = jnp.broadcast_to(jnp.sum(total * total), squares_ref.shape)


def scale_kernel(total_ref, squares_ref, first_ref, middle_ref, last_ref):
    square_sum = jnp.sum(squares_ref[...], axis=0)
    norm_scale = lax.rsqrt(square_sum / PARAMS + 1e-06)
    norm_scale = jnp.concatenate([norm_scale] * 3, 1)
    for ref, start in ((last_ref, 0), (middle_ref, 2)):
        for half in range(2):
            columns = slice(half * COLS, min((half + 1) * COLS, ref.shape[1]))
            width = columns.stop - columns.start
            ref[:, columns] = (total_ref[start + half] * norm_scale)[:, :width]
    for granule, (start, stop) in enumerate(column_cuts(first_ref.shape[1])):
        row = granule % 2 * 12
        scaled = total_ref[4 + granule // 2, row : row + 12] * norm_scale
        first_ref[:, start:stop] = scaled[:, : stop - start]


def granules(*lead, kind=BF16):
    return ((*lead, ROWS, COLS), kind)


def per_device(belief, target_value, counts, w_first, w_middle, w_last):
    total_rows, inputs = belief.shape
    width = w_last.shape[1]
    units = w_first.shape[1]
    hidden = w_middle.shape[1]
    belief_t, w_last_t = belief.T, w_last.T

    indices = (CORE, Y, X, ZH, "mp")
    place = jnp.stack([lax.axis_index(axis) for axis in indices])

    (half,) = call(
        half_kernel,
        "half",
        [SMEM, HBM],
        [((SIZE, hidden), BF16)],
        [pltpu.VMEM((width - SECOND, hidden), BF16), pltpu.SemaphoreType.DMA],
    )(place, w_last_t)
    fetched = lax.ppermute(half, (ZH, "mp"), [(0, 3), (3, 0), (1, 2), (2, 1)])
    belief_first, half = lax.optimization_barrier((belief_t, half))

    pre_first, act_first, hidden_sent = call(
        forward_kernel,
        "forward",
        [HBM] * 3,
        [
            ((total_rows, units), F32),
            ((total_rows, units), BF16),
            ((total_rows, hidden), BF16),
        ],
        [
            pltpu.VMEM((inputs, total_rows), BF16),
            pltpu.VMEM((inputs, units), BF16),
            pltpu.VMEM((units, hidden), BF16),
            pltpu.VMEM((total_rows, units), F32),
            pltpu.VMEM((total_rows, units), BF16),
            pltpu.SemaphoreType.DMA((2 * pl.cdiv(inputs, DEPTH) + 3,)),
        ],
        far=2,
    )(belief_first, w_first, w_middle)
    arrived = swap(hidden_sent, "mp")

    order = np.arange(units, dtype=np.int32).reshape(4, 2, 4, 2, -1).transpose(3, 0, 2, 1, 4)
    orders = np.stack([order[::-1], order]).reshape(2, units, 1)
    w_own, target_own, target_other, first_slope, w_sorted, live = call(
        stage_kernel,
        "stage",
        [SMEM, SMEM, VMEM, VMEM, VMEM, HBM, HBM],
        [
            ((width, hidden), BF16),
            ((width, total_rows), BF16),
            ((2, SIZE, total_rows), BF16),
            ((units, total_rows), F32),
            ((units, hidden), BF16),
            ((1, total_rows), F32),
        ],
        [pltpu.VMEM((2 * width, total_rows), BF16), pltpu.SemaphoreType.DMA((2,))],
    )(place, counts, pre_first, jnp.asarray(orders), w_middle, target_value.T, w_last_t)
    fetched, live = lax.optimization_barrier((fetched, live))
    relayed = swap(fetched, CORE)
    belief_swapped, act_swapped = lax.optimization_barrier((belief_t, act_first))
    sibling_belief = swap(belief_swapped, CORE)
    sibling_act = swap(act_swapped, CORE)

    act, act_slope, back_own, last_sent, last_own = call(
        hidden_kernel,
        "hidden",
        [SMEM] + [VMEM] * 5,
        [
            ((total_rows, hidden), BF16),
            ((total_rows, hidden), F32),
            ((total_rows, hidden), F32),
            ((hidden // 2 + width, total_rows), BF16),
            ((hidden // 2, total_rows), BF16),
        ],
        [pltpu.VMEM((hidden, total_rows), F32)],
    )(place, hidden_sent, arrived, live, target_own, w_own)
    last_arrived = swap(last_sent, CORE)

    slopes_sent, slopes_own = call(
        slopes_kernel,
        "slopes",
        [SMEM] + [VMEM] * 9,
        [((hidden // 2 + units // 2, total_rows), BF16)] * 2,
        [pltpu.VMEM((hidden, total_rows), F32)],
    )(
        place, act, act_slope, back_own, live, target_other, first_slope,
        fetched, relayed, w_sorted,
    )
    slopes_arrived = swap(slopes_sent, CORE)

    def pairs(*sizes):
        return [out for size in sizes for out in (granules(*size, kind=F32), granules(*size))]

    def exchange(parts, axes, orders):
        sent = [part[1] for part in parts]
        arrived = [to_pair(*sending) for sending in zip(sent, axes, orders)]
        return [
            (part[0], lax.optimization_barrier((coming, *sent))[0])
            for part, coming in zip(parts, arrived)
        ]

    def halve(part, *lead):
        return call(halve_kernel, "halve", [VMEM] * 2, pairs((*lead, part[0].shape[-3])))(*part)

    def turn(part, axis, order):
        size = part[0].shape[-3]
        return call(
            functools.partial(turn_kernel, 1 if axis == Y else 2, order),
            "turn",
            [SMEM] + [VMEM] * 2,
            pairs((2, size)),
        )(place, *part)

    last_own, slopes_own = lax.optimization_barrier((last_own, slopes_own))
    last_parts = call(
        last_kernel,
        "last",
        [SMEM] + [VMEM] * 3,
        pairs((2, 4, 4)),
        [pltpu.VMEM((2, units, total_rows), BF16)],
    )(place, last_own, last_sent, last_arrived)
    first_parts = call(
        first_kernel,
        "first",
        [SMEM] + [VMEM] * 4,
        pairs((2, 4, 4), (2, 4, 3)),
    )(place, slopes_own, slopes_arrived, belief_t, sibling_belief)
    middle_parts = call(
        middle_kernel, "middle", [SMEM] + [VMEM] * 4, pairs((2, 4, 4))
    )(place, slopes_own, slopes_arrived, act_first, sibling_act)
    axes, turned, orders, swapped = (X, X, Y, Y), (Y, Y, X, X), (0, 1, 0, 1), (1, 0, 1, 0)
    parts = (last_parts, middle_parts, first_parts[0:2], first_parts[2:4])
    parts = [halve(part, 4) for part in exchange(parts, axes, orders)]
    parts = [
        turn(part, turned[i], orders[i]) for i, part in enumerate(exchange(parts, axes, swapped))
    ]
    parts = [halve(part) for part in exchange(parts, turned, orders)]
    last_parts, middle_parts, *first_parts = exchange(parts, turned, swapped)
    parts = (*first_parts[0], *first_parts[1], *last_parts, *middle_parts)
    sent, own = call(
        z_cut_kernel,
        "z_cut",
        [SMEM] + [VMEM] * 8,
        [granules(8), granules(8, kind=F32)],
        [pltpu.VMEM((4, ROWS, COLS), F32)] * 2,
    )(place, *parts)

    total, squares = call(
        square_kernel, "square", [VMEM] * 2, [((8, ROWS, COLS), F32), ((128, 1, LANES), F32)]
    )(own, swap(sent, ZH))
    squares = lax.all_to_all(squares, ALL, 0, 0, tiled=True)
    grad_first, grad_middle, grad_last = call(
        scale_kernel,
        "scale",
        [VMEM] * 2,
        [((units // 64, inputs), F32), ((ROWS, units), F32), ((ROWS, width), F32)],
        kind=jax.ShapeDtypeStruct,
    )(total, squares)
    return grad_first.T, grad_middle.T, grad_last


def solution(mesh):
    finer = Mesh(mesh.devices.reshape(4, 2, 4, 2, mesh.shape["mp"]), ALL)
    return jax.shard_map(
        per_device,
        mesh=finer,
        in_specs=(P(DP, None), P(DP, None), P(DP), P(None, "mp"), P("mp", None), P(None, "mp")),
        out_specs=(P(None, MP_DP), P("mp", DP), P(DP, "mp")),
        check_vma=False,
    )
```

```python
import functools

import jax
import jax.numpy as jnp
import numpy as np
from jax import lax
from jax.experimental import pallas as pl
from jax.experimental.pallas import tpu as pltpu
from jax.sharding import Mesh
from jax.sharding import PartitionSpec as P

BLOCK = 128
PARAMS = 8469504
DP = ("dp_0", "dp_1", "dp_2", "dp_3")
MP_DP = ("mp", "dp_0", "dp_1", "dp_2", "dp_3")
ALL = DP + ("mp",)
Y, ZH, X, CORE = DP
LANES = 128
ROWS, COLS = 24, 384
SIZE, SECOND = 336, 328
DEPTH = 512
VMEM = pl.BlockSpec(memory_space=pltpu.VMEM)
SMEM = pl.BlockSpec(memory_space=pltpu.SMEM)
HBM = pl.BlockSpec(memory_space=pl.ANY)
BF16, F32 = jnp.bfloat16, jnp.float32


def wide(shard):
    return shard.astype(F32)


def narrow(shard):
    return shard.astype(BF16)


def swap(shard, axis):
    return lax.ppermute(shard, axis, [(0, 1), (1, 0)])


def to_pair(shard, axis, order):
    pairs = [(i, i ^ 1) for i in range(4)] if order == 0 else [(i, 3 - i) for i in range(4)]
    return lax.ppermute(shard, axis, pairs)


def silu_slope(pre_act):
    sigmoid_of = 1.0 / (1.0 + jnp.exp(-pre_act))
    return sigmoid_of * (1.0 + pre_act * (1.0 - sigmoid_of))


def dot(left, right):
    return jnp.dot(left, right, preferred_element_type=F32)


def contract(left, right, left_dim, right_dim):
    return lax.dot_general(
        left, right, (((left_dim,), (right_dim,)), ((), ())), preferred_element_type=F32
    )


def call(body, name, in_specs, outs, scratch=(), kind=pltpu.VMEM, far=0):
    kernel = pl.pallas_call(
        body,
        out_shape=[(pltpu.HBM if i < far else kind)(*out) for i, out in enumerate(outs)],
        in_specs=in_specs,
        out_specs=[HBM if i < far else VMEM for i in range(len(outs))],
        scratch_shapes=list(scratch),
        compiler_params=pltpu.CompilerParams(vmem_limit_bytes=24 << 20),
        cost_estimate=pl.CostEstimate(flops=1 << 34, bytes_accessed=1 << 26, transcendentals=0),
        name=name,
    )

    def run(*operands):
        return kernel(
            *(
                operand if spec is SMEM else pltpu.with_memory_space_constraint(
                    operand, pltpu.VMEM if spec is VMEM else pltpu.HBM
                )
                for operand, spec in zip(operands, in_specs)
            )
        )

    return run


def rows_of_core(rows_ref, core, out_ref):
    for block in range(32):
        y, x, z_hi = block // 8, block // 2 % 4, block % 2
        first = 2 * ROWS * ((2 * y + z_hi) * 4 + x)
        rows = pl.ds(pl.multiple_of(first + ROWS * core, 8), ROWS)
        out_ref[ROWS * block : ROWS * (block + 1), :] = narrow(rows_ref[rows, :])


def forward_kernel(
    belief_hbm, w_first_hbm, w_middle_hbm, pre_first_hbm, act_first_hbm, sent_ref,
    belief, w_first, w_middle, pre_first_ref, act_first_ref, sems,
):
    inputs = belief.shape[0]
    cuts = [(start, min(start + DEPTH, inputs)) for start in range(0, inputs, DEPTH)]
    copies = []
    for i, (start, stop) in enumerate(cuts):
        rows = pl.ds(start, stop - start)
        copies.append(
            (
                pltpu.make_async_copy(belief_hbm.at[rows], belief.at[rows], sems.at[2 * i]),
                pltpu.make_async_copy(w_first_hbm.at[rows], w_first.at[rows], sems.at[2 * i + 1]),
            )
        )
    copies.append((pltpu.make_async_copy(w_middle_hbm, w_middle, sems.at[2 * len(cuts)]),))
    for pair in copies:
        for copy in pair:
            copy.start()
    results = (
        pltpu.make_async_copy(pre_first_ref, pre_first_hbm, sems.at[2 * len(cuts) + 1]),
        pltpu.make_async_copy(act_first_ref, act_first_hbm, sems.at[2 * len(cuts) + 2]),
    )
    pre_first = jnp.zeros(pre_first_ref.shape, F32)
    for (start, stop), pair in zip(cuts, copies):
        for copy in pair:
            copy.wait()
        pre_first += contract(belief[start:stop, :], w_first[start:stop, :], 0, 0)
    pre_first_ref[...] = pre_first
    results[0].start()
    act_first = narrow(pre_first / (1.0 + jnp.exp(-pre_first)))
    act_first_ref[...] = act_first
    results[1].start()
    copies[-1][0].wait()
    sent_ref[...] = narrow(dot(act_first, w_middle[...]))
    for copy in results:
        copy.wait()


def half_kernel(place_ref, w_last_hbm, half_ref, last_ref, sem):
    size, total = half_ref.shape[0], w_last_hbm.shape[0]

    @pl.when(place_ref[0] == 0)
    def _():
        copy = pltpu.make_async_copy(w_last_hbm.at[pl.ds(0, size)], half_ref, sem)
        copy.start()
        copy.wait()

    @pl.when(place_ref[0] != 0)
    def _():
        copy = pltpu.make_async_copy(w_last_hbm.at[pl.ds(SECOND, total - SECOND)], last_ref, sem)
        copy.start()
        half_ref[size - 8 :, :] = jnp.zeros((8, half_ref.shape[1]), half_ref.dtype)
        copy.wait()
        half_ref[0 : total - SECOND, :] = last_ref[...]


def stage_kernel(
    place_ref, counts_ref, pre_first_ref, orders_ref, w_middle_ref, target_hbm, w_last_hbm,
    w_own_ref, target_own_ref, target_other_ref, first_slope_ref, w_sorted_ref, live_ref,
    target_ref, sems,
):
    copies = (
        pltpu.make_async_copy(target_hbm, target_ref, sems.at[0]),
        pltpu.make_async_copy(w_last_hbm, w_own_ref, sems.at[1]),
    )
    for copy in copies:
        copy.start()
    order = jnp.where(place_ref[0] == 0, orders_ref[0], orders_ref[1])
    units = lax.broadcasted_iota(jnp.int32, (order.shape[0], order.shape[0]), 1)
    onehot = jnp.where(order == units, 1.0, 0.0)
    w_sorted_ref[...] = narrow(dot(narrow(onehot), w_middle_ref[...]))
    first_slope_ref[...] = lax.dot_general(
        onehot,
        silu_slope(pre_first_ref[...]),
        (((1,), (1,)), ((), ())),
        precision=lax.Precision.HIGHEST,
        preferred_element_type=F32,
    )
    row = lax.broadcasted_iota(jnp.int32, live_ref.shape, 1)
    count = jnp.where(row < BLOCK, counts_ref[0], counts_ref[1] + BLOCK)
    live_ref[...] = jnp.where(row < count, 1.0, 0.0)
    copies[0].wait()
    width = target_own_ref.shape[0]
    low, high = target_ref[0:width, :], target_ref[width : 2 * width, :]
    is_low = place_ref[4] == 0
    target_own_ref[...] = jnp.where(is_low, low, high)
    other = jnp.where(is_low, high, low)
    size = target_other_ref.shape[1]
    for side in range(2):

        @pl.when(place_ref[0] == side)
        def _():
            target_other_ref[side] = other[0:size]
            target_other_ref[1 - side, size - 8 :, :] = jnp.zeros((8, other.shape[1]), other.dtype)
            target_other_ref[1 - side, 0 : width - SECOND, :] = other[SECOND:]

    copies[1].wait()


def hidden_kernel(
    place_ref, partial_ref, arrived_ref, live_ref, target_ref, w_ref,
    act_ref, act_slope_ref, back_ref, sent_ref, own_ref, rows_ref,
):
    core = place_ref[0]
    pre_middle = wide(partial_ref[...]) + wide(arrived_ref[...])
    sigmoid_of = 1.0 / (1.0 + jnp.exp(-pre_middle))
    act = narrow(pre_middle * sigmoid_of)
    act_ref[...] = act
    act_slope_ref[...] = sigmoid_of * (1.0 + pre_middle * (1.0 - sigmoid_of))
    slope = slope_of(w_ref[...], act, target_ref[...], live_ref[...])
    half = own_ref.shape[0]
    sent_ref[half:, :] = slope
    back_ref[...] = contract(slope, w_ref[...], 0, 0)
    rows_ref[...] = wide(act).T
    rows_of_core(rows_ref, 1 - core, sent_ref)
    rows_of_core(rows_ref, core, own_ref)


def slope_of(weights, act, target, live):
    mismatch = contract(weights, act, 1, 1) - wide(target)
    return narrow(jnp.clip(mismatch, -1.0, 1.0) * live)


def slopes_kernel(
    place_ref, act_ref, act_slope_ref, back_ref, live_ref, target_ref, first_slope_ref,
    fetched_ref, relayed_ref, w_sorted_ref, sent_ref, own_ref, rows_ref,
):
    core = place_ref[0]
    act, live = act_ref[...], live_ref[...]
    back = back_ref[...]
    for side, w_ref in enumerate((fetched_ref, relayed_ref)):
        weights = w_ref[...]
        slope = slope_of(weights, act, target_ref[side], live)
        repeated = jnp.where(core == side, 0, SIZE - SECOND)
        column = lax.broadcasted_iota(jnp.int32, slope.shape, 0)
        slope = jnp.where(column >= repeated, slope, jnp.zeros_like(slope))
        back += contract(slope, weights, 0, 0)
    slope_middle = narrow(back * act_slope_ref[...])
    slope_first = narrow(contract(w_sorted_ref[...], slope_middle, 1, 1) * first_slope_ref[...])
    half = slope_first.shape[0] // 2
    sent_ref[2 * half :, :] = slope_first[:half]
    own_ref[2 * half :, :] = slope_first[half:]
    rows_ref[...] = wide(slope_middle).T
    rows_of_core(rows_ref, 1 - core, sent_ref)
    rows_of_core(rows_ref, core, own_ref)


def column_cuts(width):
    return [(start, min(start + COLS, width)) for start in range(0, width, COLS)]


def kept_and_sent(me, order):
    near, far, opposite = lax.bitwise_xor(me, 1), 3 - me, lax.bitwise_xor(me, 2)
    return ((me, far), (near, opposite)) if order == 0 else ((me, near), (far, opposite))


def rows_along_x(ref, me, order):
    kept, sent = kept_and_sent(me, order)
    firsts = [2 * ROWS * (4 * y + x) for x in (*kept, *sent) for y in range(4)]
    return jnp.concatenate(
        [ref[pl.ds(pl.multiple_of(first, 16), 2 * ROWS), :] for first in firsts], 0
    )


def put_rows(raw, kept_ref, sent_ref):
    for block in range(16):
        out_ref = (kept_ref, sent_ref)[block // 8]
        for granule in range(4):
            first = ROWS * (2 * block + granule // 2)
            columns = slice(granule % 2 * COLS, (granule % 2 + 1) * COLS)
            rows = raw[first : first + ROWS, columns]
            out_ref[block // 4 % 2, block % 4, granule] = rows.astype(out_ref.dtype)


def last_kernel(place_ref, own_ref, sent_ref, arrived_ref, kept_out, sent_out, padded_ref):
    half = own_ref.shape[0]
    width = sent_ref.shape[0] - half
    padded_ref[...] = jnp.zeros_like(padded_ref)
    padded_ref[0, 0:width, :] = sent_ref[half:, :]
    padded_ref[1, 0:width, :] = arrived_ref[half:, :]
    own, arrived = (rows_along_x(ref, place_ref[2], 0) for ref in (own_ref, arrived_ref))
    raw = contract(own, padded_ref[0], 1, 1) + contract(arrived, padded_ref[1], 1, 1)
    put_rows(raw, kept_out, sent_out)


def middle_kernel(place_ref, own_ref, arrived_ref, act_ref, sibling_act_ref, kept_out, sent_out):
    own, arrived = (rows_along_x(ref, place_ref[2], 1) for ref in (own_ref, arrived_ref))
    raw = dot(own, act_ref[...]) + dot(arrived, sibling_act_ref[...])
    put_rows(raw, kept_out, sent_out)


def first_kernel(place_ref, own_ref, arrived_ref, belief_ref, sibling_belief_ref, *out_refs):
    start_row = own_ref.shape[0] // 3 * 2
    cuts = column_cuts(belief_ref.shape[0])
    for order, part in enumerate((cuts[0:3], cuts[3:7])):
        kept, sent = kept_and_sent(place_ref[1], order)
        own, arrived = (
            jnp.concatenate(
                [
                    ref[pl.ds(pl.multiple_of(start_row + 4 * ROWS * y, 32), 4 * ROWS), :]
                    for y in (*kept, *sent)
                ],
                0,
            )
            for ref in (own_ref, arrived_ref)
        )
        for granule, (start, stop) in enumerate(part):
            raw = contract(own, belief_ref[start:stop, :], 1, 1) + contract(
                arrived, sibling_belief_ref[start:stop, :], 1, 1
            )
            if stop - start < COLS:
                pad = jnp.zeros((raw.shape[0], COLS - raw.shape[1]), raw.dtype)
                raw = jnp.concatenate([raw, pad], 1)
            for unit in range(16):
                out_ref = out_refs[2 * order + unit // 8]
                rows = raw[unit * ROWS : (unit + 1) * ROWS]
                out_ref[unit // 4 % 2, unit % 4, granule] = rows.astype(out_ref.dtype)


def halve_kernel(kept_ref, arrived_ref, kept_out, sent_out):
    kept_out[...] = kept_ref[0] + wide(arrived_ref[0])
    sent_out[...] = narrow(kept_ref[1] + wide(arrived_ref[1]))


def turn_kernel(axis, order, place_ref, kept_ref, arrived_ref, kept_out, sent_out):
    for out_ref, blocks in zip((kept_out, sent_out), kept_and_sent(place_ref[axis], order)):
        for position, block in enumerate(blocks):
            total = kept_ref[block] + wide(arrived_ref[block])
            out_ref[position] = total.astype(out_ref.dtype)


def z_cut_kernel(place_ref, *refs):
    sent_ref, own_ref, last_sum, middle_sum = refs[8:12]
    z_hi = place_ref[3]
    low, high, last, middle = (
        refs[2 * part][...] + wide(refs[2 * part + 1][...]) for part in range(4)
    )
    last_sum[...] = last
    middle_sum[...] = middle
    rows = [low[granule] for granule in range(3)] + [high[granule] for granule in range(4)]
    for side, out_ref in ((1 - z_hi, sent_ref), (z_hi, own_ref)):
        kind = out_ref.dtype
        out_ref[0:2] = last_sum[pl.ds(2 * side, 2)].astype(kind)
        out_ref[2:4] = middle_sum[pl.ds(2 * side, 2)].astype(kind)
        halves = [jnp.where(side == 0, row[0:12], row[12:24]) for row in rows]
        halves.append(jnp.zeros_like(halves[0]))
        for pair in range(4):
            out_ref[4 + pair] = jnp.concatenate(halves[2 * pair : 2 * pair + 2], 0).astype(kind)


def square_kernel(own_ref, arrived_ref, total_ref, squares_ref):
    total = own_ref[...] + wide(arrived_ref[...])
    total_ref[...] = total
    squares_ref[...] = jnp.broadcast_to(jnp.sum(total * total), squares_ref.shape)


def scale_kernel(total_ref, squares_ref, first_ref, middle_ref, last_ref):
    square_sum = jnp.sum(squares_ref[...], axis=0)
    norm_scale = lax.rsqrt(square_sum / PARAMS + 1e-06)
    norm_scale = jnp.concatenate([norm_scale] * 3, 1)
    for ref, start in ((last_ref, 0), (middle_ref, 2)):
        for half in range(2):
            columns = slice(half * COLS, min((half + 1) * COLS, ref.shape[1]))
            width = columns.stop - columns.start
            ref[:, columns] = (total_ref[start + half] * norm_scale)[:, :width]
    for granule, (start, stop) in enumerate(column_cuts(first_ref.shape[1])):
        row = granule % 2 * 12
        scaled = total_ref[4 + granule // 2, row : row + 12] * norm_scale
        first_ref[:, start:stop] = scaled[:, : stop - start]


def granules(*lead, kind=BF16):
    return ((*lead, ROWS, COLS), kind)


def per_device(belief, target_value, counts, w_first, w_middle, w_last):
    total_rows, inputs = belief.shape
    width = w_last.shape[1]
    units = w_first.shape[1]
    hidden = w_middle.shape[1]
    belief_t, w_last_t = belief.T, w_last.T

    indices = (CORE, Y, X, ZH, "mp")
    place = jnp.stack([lax.axis_index(axis) for axis in indices])

    (half,) = call(
        half_kernel,
        "half",
        [SMEM, HBM],
        [((SIZE, hidden), BF16)],
        [pltpu.VMEM((width - SECOND, hidden), BF16), pltpu.SemaphoreType.DMA],
    )(place, w_last_t)
    fetched = lax.ppermute(half, (ZH, "mp"), [(0, 3), (3, 0), (1, 2), (2, 1)])
    belief_first, half = lax.optimization_barrier((belief_t, half))

    pre_first, act_first, hidden_sent = call(
        forward_kernel,
        "forward",
        [HBM] * 3,
        [
            ((total_rows, units), F32),
            ((total_rows, units), BF16),
            ((total_rows, hidden), BF16),
        ],
        [
            pltpu.VMEM((inputs, total_rows), BF16),
            pltpu.VMEM((inputs, units), BF16),
            pltpu.VMEM((units, hidden), BF16),
            pltpu.VMEM((total_rows, units), F32),
            pltpu.VMEM((total_rows, units), BF16),
            pltpu.SemaphoreType.DMA((2 * pl.cdiv(inputs, DEPTH) + 3,)),
        ],
        far=2,
    )(belief_first, w_first, w_middle)
    arrived = swap(hidden_sent, "mp")

    order = np.arange(units, dtype=np.int32).reshape(4, 2, 4, 2, -1).transpose(3, 0, 2, 1, 4)
    orders = np.stack([order[::-1], order]).reshape(2, units, 1)
    w_own, target_own, target_other, first_slope, w_sorted, live = call(
        stage_kernel,
        "stage",
        [SMEM, SMEM, VMEM, VMEM, VMEM, HBM, HBM],
        [
            ((width, hidden), BF16),
            ((width, total_rows), BF16),
            ((2, SIZE, total_rows), BF16),
            ((units, total_rows), F32),
            ((units, hidden), BF16),
            ((1, total_rows), F32),
        ],
        [pltpu.VMEM((2 * width, total_rows), BF16), pltpu.SemaphoreType.DMA((2,))],
    )(place, counts, pre_first, jnp.asarray(orders), w_middle, target_value.T, w_last_t)
    fetched, live = lax.optimization_barrier((fetched, live))
    relayed = swap(fetched, CORE)
    belief_swapped, act_swapped = lax.optimization_barrier((belief_t, act_first))
    sibling_belief = swap(belief_swapped, CORE)
    sibling_act = swap(act_swapped, CORE)

    act, act_slope, back_own, last_sent, last_own = call(
        hidden_kernel,
        "hidden",
        [SMEM] + [VMEM] * 5,
        [
            ((total_rows, hidden), BF16),
            ((total_rows, hidden), F32),
            ((total_rows, hidden), F32),
            ((hidden // 2 + width, total_rows), BF16),
            ((hidden // 2, total_rows), BF16),
        ],
        [pltpu.VMEM((hidden, total_rows), F32)],
    )(place, hidden_sent, arrived, live, target_own, w_own)
    last_arrived = swap(last_sent, CORE)

    slopes_sent, slopes_own = call(
        slopes_kernel,
        "slopes",
        [SMEM] + [VMEM] * 9,
        [((hidden // 2 + units // 2, total_rows), BF16)] * 2,
        [pltpu.VMEM((hidden, total_rows), F32)],
    )(
        place, act, act_slope, back_own, live, target_other, first_slope,
        fetched, relayed, w_sorted,
    )
    slopes_arrived = swap(slopes_sent, CORE)

    def pairs(*sizes):
        return [out for size in sizes for out in (granules(*size, kind=F32), granules(*size))]

    def exchange(parts, axes, orders):
        sent = [part[1] for part in parts]
        arrived = [to_pair(*sending) for sending in zip(sent, axes, orders)]
        return [
            (part[0], lax.optimization_barrier((coming, *sent))[0])
            for part, coming in zip(parts, arrived)
        ]

    def halve(part, *lead):
        return call(halve_kernel, "halve", [VMEM] * 2, pairs((*lead, part[0].shape[-3])))(*part)

    def turn(part, axis, order):
        size = part[0].shape[-3]
        return call(
            functools.partial(turn_kernel, 1 if axis == Y else 2, order),
            "turn",
            [SMEM] + [VMEM] * 2,
            pairs((2, size)),
        )(place, *part)

    last_own, slopes_own = lax.optimization_barrier((last_own, slopes_own))
    last_parts = call(
        last_kernel,
        "last",
        [SMEM] + [VMEM] * 3,
        pairs((2, 4, 4)),
        [pltpu.VMEM((2, units, total_rows), BF16)],
    )(place, last_own, last_sent, last_arrived)
    first_parts = call(
        first_kernel,
        "first",
        [SMEM] + [VMEM] * 4,
        pairs((2, 4, 3), (2, 4, 4)),
    )(place, slopes_own, slopes_arrived, belief_t, sibling_belief)
    middle_parts = call(
        middle_kernel, "middle", [SMEM] + [VMEM] * 4, pairs((2, 4, 4))
    )(place, slopes_own, slopes_arrived, act_first, sibling_act)
    axes, turned, orders, swapped = (X, X, Y, Y), (Y, Y, X, X), (0, 1, 0, 1), (1, 0, 1, 0)
    parts = (last_parts, middle_parts, first_parts[0:2], first_parts[2:4])
    parts = [halve(part, 4) for part in exchange(parts, axes, orders)]
    parts = [
        turn(part, turned[i], orders[i]) for i, part in enumerate(exchange(parts, axes, swapped))
    ]
    parts = [halve(part) for part in exchange(parts, turned, orders)]
    last_parts, middle_parts, *first_parts = exchange(parts, turned, swapped)
    parts = (*first_parts[0], *first_parts[1], *last_parts, *middle_parts)
    sent, own = call(
        z_cut_kernel,
        "z_cut",
        [SMEM] + [VMEM] * 8,
        [granules(8), granules(8, kind=F32)],
        [pltpu.VMEM((4, ROWS, COLS), F32)] * 2,
    )(place, *parts)

    total, squares = call(
        square_kernel, "square", [VMEM] * 2, [((8, ROWS, COLS), F32), ((128, 1, LANES), F32)]
    )(own, swap(sent, ZH))
    squares = lax.all_to_all(squares, ALL, 0, 0, tiled=True)
    grad_first, grad_middle, grad_last = call(
        scale_kernel,
        "scale",
        [VMEM] * 2,
        [((units // 64, inputs), F32), ((ROWS, units), F32), ((ROWS, width), F32)],
        kind=jax.ShapeDtypeStruct,
    )(total, squares)
    return grad_first.T, grad_middle.T, grad_last


def solution(mesh):
    finer = Mesh(mesh.devices.reshape(4, 2, 4, 2, mesh.shape["mp"]), ALL)
    return jax.shard_map(
        per_device,
        mesh=finer,
        in_specs=(P(DP, None), P(DP, None), P(DP), P(None, "mp"), P("mp", None), P(None, "mp")),
        out_specs=(P(None, MP_DP), P("mp", DP), P(DP, "mp")),
        check_vma=False,
    )
```
